32 devices in a mesh: cols: 4 (over y, x), rows: 8 (over z, core).
Axes of the slice: x: 2, y: 2, z: 4, core: 2. Of those that a mesh axis runs over, the one named last changes fastest.
Arguments:
- gradient: float32 [128, 8192], P('cols', 'rows'), may hold values from -100 to 100
- width_factor: float32 [128, 128], P(None, 'cols'), may hold values from -3 to 4, as said below
- diag_blocks: float32 [64, 128, 128], P('rows'), may hold values from -2 to 24, as said below
- jacobi_inverse: float32 [64, 128, 128], P('rows'), may hold values from -2 to 2, as said below
- coupling_tiles: bfloat16 [32, 128, 128], P('rows'), may hold values from -4 to 4, as said below
- tile_local: int32 [32], P('rows'), may hold values from 0 to 7
- tile_remote: int32 [32], P('rows'), may hold values from 0 to 63, as said below
- tile_count: int32 [8], P('rows'), may hold values from 0 to 3, as said below
Outputs:
- solution: float32 [128, 8192], P('cols', 'rows')
- residual: float32 [128, 8192], P('cols', 'rows')
The draws below stay inside these ranges and needn't reach their ends.
Inputs may be any that keep to these rules, and one draw needn't show every extreme that they name: `tile_remote`: the live entries are the first tile_count entries of each device's list; they name distinct devices other than the owner, each at most once. For a live entry of device d naming block J of device e, device e has a live entry naming d's block with its tile the transpose. Pad entries hold valid indices. `tile_count`: at most 3 on one device, reached on some device. `coupling_tiles`: with diag_blocks and the live entries, M is symmetric positive definite. `diag_blocks`: symmetric positive definite tiles. `jacobi_inverse`: the inverses of diag_blocks, symmetric. `width_factor`: symmetric positive definite.
All inputs are finite; a program needn't handle non-finite values.
Results may differ from the reference program's by a relative error of at most 0.0085.
Values may be sent and summed in bfloat16 or wider, within the bound.
No kernel may reach another device: no remote copies, remote signals or barrier semaphores. Data moves between devices by JAX's collectives and lax.ppermute only.
A program may use at most 64 MiB of HBM per device.

```python
import math
import jax
import jax.numpy as jnp
from jax import lax

WIDTH = 128
BLOCK = 128
BLOCKS_DEV = 8
ITERS = 6
OFFSETS = 2
SLOTS_DEV = 4
ALL_BLOCKS = 64
ALL_ROWS = 8192
N_ROWS = 8


def layout(key):
    subkeys = jax.random.split(jax.random.fold_in(key, 7), 7)
    node_count = N_ROWS
    half_way = node_count // 2
    others = jax.random.permutation(subkeys[0], half_way - 2)[:OFFSETS - 2].astype(jnp.int32) + 2
    offsets = jnp.concatenate([jnp.array([1, half_way], dtype=jnp.int32), others])
    weights = jax.random.randint(subkeys[1], (node_count,), 0, 4)
    center = jax.random.randint(subkeys[2], (), 0, node_count)
    device = jnp.arange(node_count, dtype=jnp.int32)[:, None]
    slot_index = jnp.arange(OFFSETS, dtype=jnp.int32)[None, :]
    partner_up = (device + offsets[None, :]) % node_count
    partner_down = (device - offsets[None, :]) % node_count
    rolled = jax.random.randint(subkeys[3], (node_count, OFFSETS), 0, 8)
    random_live = (rolled < 2 + weights[:, None] + weights[partner_up]) | (device == center) | (partner_up == center)
    active = jnp.where(slot_index == 1, device < half_way, random_live)
    planted = slot_index < 2
    block_low = jax.random.randint(subkeys[4], (node_count, OFFSETS), 0, BLOCKS_DEV).astype(jnp.int32)
    block_high = jax.random.randint(subkeys[5], (node_count, OFFSETS), 0, BLOCKS_DEV).astype(jnp.int32)
    boost = jnp.where(planted, 8.0, 1.0)
    strength = boost * jnp.exp(jax.random.uniform(subkeys[6], (node_count, OFFSETS), minval=math.log(0.5), maxval=math.log(2.0))) / SLOTS_DEV
    is_live = jnp.concatenate([active, active[partner_down, slot_index]], axis=1)
    local_block = jnp.concatenate([block_low, block_high[partner_down, slot_index]], axis=1)
    remote = jnp.concatenate([partner_up * BLOCKS_DEV + block_high, partner_down * BLOCKS_DEV + block_low[partner_down, slot_index]], axis=1)
    edge_owner = jnp.concatenate([jnp.broadcast_to(device, (node_count, OFFSETS)), partner_down], axis=1)
    edge_slot = jnp.concatenate([jnp.broadcast_to(slot_index, (node_count, OFFSETS)), jnp.broadcast_to(slot_index, (node_count, OFFSETS))], axis=1)
    flipped = jnp.concatenate([jnp.zeros((node_count, OFFSETS), jnp.int32), jnp.ones((node_count, OFFSETS), jnp.int32)], axis=1)
    slot_strength = strength[edge_owner, edge_slot]
    matches = local_block[:, :, None] == jnp.arange(BLOCKS_DEV, dtype=jnp.int32)[None, None, :]
    shift_rows = jnp.sum((is_live.astype(jnp.float32) * 1.25 * slot_strength)[:, :, None] * matches.astype(jnp.float32), axis=1)
    compact_order = jnp.argsort(jnp.where(is_live, 0, 1), axis=1, stable=True)
    local_block = jnp.take_along_axis(local_block, compact_order, axis=1)
    remote = jnp.take_along_axis(remote, compact_order, axis=1)
    edge_owner = jnp.take_along_axis(edge_owner, compact_order, axis=1)
    edge_slot = jnp.take_along_axis(edge_slot, compact_order, axis=1)
    flipped = jnp.take_along_axis(flipped, compact_order, axis=1)
    live_count = jnp.sum(is_live.astype(jnp.int32), axis=1).astype(jnp.int32)
    return (local_block, remote, edge_owner, edge_slot, flipped, live_count, strength, shift_rows.reshape(ALL_BLOCKS))


def diagonal_matrix(key):
    shift_rows = layout(key)[7]
    entries = jax.random.uniform(jax.random.fold_in(key, 31), (ALL_BLOCKS, BLOCK, BLOCK), minval=-math.sqrt(3.0), maxval=math.sqrt(3.0))
    gram_matrix = jnp.einsum('nij,nkj->nik', entries, entries) / BLOCK
    identity = jnp.eye(BLOCK, dtype=jnp.float32)[None, :, :]
    matrix = 0.5 * identity + 0.5 * gram_matrix + shift_rows[:, None, None] * identity
    return 0.5 * (matrix + jnp.swapaxes(matrix, 1, 2))


def draw_diag_blocks(key, part):
    return diagonal_matrix(key).astype(jnp.float32)


def draw_jacobi_inverse(key, part):
    inverse = jnp.linalg.inv(diagonal_matrix(key))
    return (0.5 * (inverse + jnp.swapaxes(inverse, 1, 2))).astype(jnp.float32)


def draw_coupling_tiles(key, part):
    local_block, remote, edge_owner, edge_slot, flipped, live_count, strength, shift_rows = layout(key)
    raw_basis = jax.random.normal(jax.random.fold_in(key, 21), (N_ROWS, OFFSETS, BLOCK, BLOCK))
    orthogonal, upper_part = jnp.linalg.qr(raw_basis)
    scaled = (orthogonal * strength[:, :, None, None]).astype(jnp.bfloat16)
    picked = scaled[edge_owner, edge_slot]
    picked = jnp.where(flipped[:, :, None, None] == 1, jnp.swapaxes(picked, 2, 3), picked)
    return picked.reshape(N_ROWS * SLOTS_DEV, BLOCK, BLOCK)


def draw_tile_local(key, part):
    return layout(key)[0].reshape(N_ROWS * SLOTS_DEV).astype(jnp.int32)


def draw_tile_remote(key, part):
    return layout(key)[1].reshape(N_ROWS * SLOTS_DEV).astype(jnp.int32)


def draw_tile_count(key, part):
    return layout(key)[5].astype(jnp.int32)


def draw_width_factor(key, part):
    entries = jax.random.uniform(jax.random.fold_in(key, 41), (WIDTH, WIDTH), minval=-math.sqrt(3.0), maxval=math.sqrt(3.0))
    matrix = jnp.dot(entries, entries.T) / WIDTH + 0.05 * jnp.eye(WIDTH, dtype=jnp.float32)
    return (0.5 * (matrix + matrix.T)).astype(jnp.float32)


def draw_gradient(key, part):
    subkeys = jax.random.split(jax.random.fold_in(key, 51), 3)
    spread = math.log(math.sqrt(10.0))
    width_scale = jnp.exp(jax.random.uniform(subkeys[0], (WIDTH,), minval=-spread, maxval=spread))
    width_scale = width_scale * (1.0 + 2.0 * jnp.arange(WIDTH, dtype=jnp.float32) / WIDTH) / 2.0
    row_scale = jnp.exp(jax.random.uniform(subkeys[1], (ALL_ROWS,), minval=-spread, maxval=spread))
    row_scale = row_scale * (1.0 + 2.0 * jnp.arange(ALL_ROWS, dtype=jnp.float32) / ALL_ROWS) / 2.0
    core = jnp.clip(jax.random.normal(subkeys[2], (WIDTH, ALL_ROWS)), -4.0, 4.0)
    return (core * width_scale[:, None] * row_scale[None, :]).astype(jnp.float32)


def setup_inputs(seed: int = 0) -> dict:
    keys = jax.random.split(jax.random.key(seed), 9)
    return {
        "gradient": draw_gradient(jax.random.fold_in(keys[8], 71), 0),
        "width_factor": draw_width_factor(jax.random.fold_in(keys[8], 71), 0),
        "diag_blocks": draw_diag_blocks(jax.random.fold_in(keys[8], 71), 0),
        "jacobi_inverse": draw_jacobi_inverse(jax.random.fold_in(keys[8], 71), 0),
        "coupling_tiles": draw_coupling_tiles(jax.random.fold_in(keys[8], 71), 0),
        "tile_local": draw_tile_local(jax.random.fold_in(keys[8], 71), 0),
        "tile_remote": draw_tile_remote(jax.random.fold_in(keys[8], 71), 0),
        "tile_count": draw_tile_count(jax.random.fold_in(keys[8], 71), 0),
    }


highest = lax.Precision.HIGHEST

def coupling_sum(direction, coupling_tiles, tile_local, tile_remote, tile_count):
    barrier = lax.optimization_barrier(direction.astype(jnp.bfloat16))
    rounded = barrier.astype(jnp.float32).reshape(WIDTH, ALL_BLOCKS, BLOCK)
    tile_sets = coupling_tiles.reshape(N_ROWS, SLOTS_DEV, BLOCK, BLOCK)
    local_sets = tile_local.reshape(N_ROWS, SLOTS_DEV)
    remote_sets = tile_remote.reshape(N_ROWS, SLOTS_DEV)

    def one_device(inputs):
        tile_set, local_set, remote_set, live_count = inputs
        sources = rounded[:, remote_set, :]
        products = jnp.einsum('ekj,kji->eki', sources, tile_set.astype(jnp.float32), precision=highest)
        active_slot = jnp.arange(SLOTS_DEV, dtype=jnp.int32) < live_count
        placing = ((local_set[:, None] == jnp.arange(BLOCKS_DEV, dtype=jnp.int32)[None, :]) & active_slot[:, None]).astype(jnp.float32)
        return jnp.einsum('eki,kb->ebi', products, placing, precision=highest)
    pieces = lax.map(one_device, (tile_sets, local_sets, remote_sets, tile_count))
    return jnp.transpose(pieces, (1, 0, 2, 3)).reshape(WIDTH, ALL_ROWS)

def reference(gradient, width_factor, diag_blocks, jacobi_inverse, coupling_tiles, tile_local, tile_remote, tile_count):

    def apply_fisher(direction):
        blocks = direction.reshape(WIDTH, ALL_BLOCKS, BLOCK)
        local_part = jnp.einsum('enj,nji->eni', blocks, diag_blocks, precision=highest).reshape(WIDTH, ALL_ROWS)
        mixed_rows = local_part + coupling_sum(direction, coupling_tiles, tile_local, tile_remote, tile_count)
        return jnp.dot(width_factor, mixed_rows, precision=highest)

    def precondition(vector):
        blocks = vector.reshape(WIDTH, ALL_BLOCKS, BLOCK)
        return jnp.einsum('enj,nji->eni', blocks, jacobi_inverse, precision=highest).reshape(WIDTH, ALL_ROWS)
    solution = jnp.zeros_like(gradient)
    residual = gradient
    precond_res = precondition(residual)
    direction = precond_res
    res_norm = jnp.sum(residual * precond_res)
    for iteration in range(ITERS):
        fisher_dir = apply_fisher(direction)
        step_size = res_norm / jnp.sum(direction * fisher_dir)
        solution = solution + step_size * direction
        residual = residual - step_size * fisher_dir
        if iteration + 1 < ITERS:
            precond_res = precondition(residual)
            next_norm = jnp.sum(residual * precond_res)
            direction = precond_res + next_norm / res_norm * direction
            res_norm = next_norm
    return (solution, residual)
```

```python
import functools

import jax
import jax.numpy as jnp
from jax import lax
from jax.experimental import pallas as pl
from jax.experimental.pallas import tpu as pltpu
from jax.sharding import PartitionSpec as P

BLOCK = 128
ITERS = 6
STRETCH = 1.1
GATHER_BYTES = 8 * 2**20

highest = lax.Precision.HIGHEST
f32 = jnp.float32
VMEM = pl.BlockSpec(memory_space=pltpu.VMEM)
SMEM = pl.BlockSpec(memory_space=pltpu.SMEM)


def dot(a, b):
    return jnp.dot(a, b, precision=highest, preferred_element_type=f32)


def call(kernel, outs, *args, scalars=0, scratch=()):
    specs = [SMEM] * scalars + [VMEM] * (len(args) - scalars)
    many = isinstance(outs, tuple)
    return pl.pallas_call(
        kernel,
        out_shape=outs,
        in_specs=specs,
        out_specs=tuple([VMEM] * len(outs)) if many else VMEM,
        scratch_shapes=list(scratch),
    )(*args)


def split(x):
    high = x.astype(jnp.bfloat16)
    return high, (x - high.astype(f32)).astype(jnp.bfloat16)


def pack_kernel(local, gradient, jacobi, tiles, packed):
    for slot in range(packed.shape[0]):
        block = local[slot]
        tile = tiles[slot].astype(f32)
        packed[slot, :BLOCK, :] = lax.dot_general(
            jacobi[block],
            tile,
            (((1,), (1,)), ((), ())),
            precision=highest,
            preferred_element_type=f32,
        )
        columns = pl.ds(pl.multiple_of(block * BLOCK, BLOCK), BLOCK)
        packed[slot, BLOCK:, :] = gradient[:, columns]


def chain_kernel(sources, near, far, chain, high, low, held, out):
    groups, slots = near.shape[:2]
    half = groups * slots
    total = 2 * half
    width = near.shape[2] - BLOCK
    for q in range(total):
        ref = near if q < half else far
        group, slot = divmod(q % half, slots)
        high[q], low[q] = split(ref[group, slot, :BLOCK, :])
        held[q] = ref[group, slot, BLOCK:, :]
    out[total] = jnp.zeros((width, BLOCK), f32)

    def step(j, carry):
        for q in range(total):
            first, second = split(held[q])
            both = jnp.dot(
                jnp.concatenate([first, second], 0), high[q], preferred_element_type=f32
            )
            rest = jnp.dot(first, low[q], preferred_element_type=f32)
            out[q] = both[:width] + both[width:] + rest
        for q in range(total):
            value = out[sources[q * slots]]
            for i in range(1, slots):
                value += out[sources[q * slots + i]]
            held[q] = value
        for slot in range(slots):
            chain[j, slot] = held[slot]
        return carry

    lax.fori_loop(0, ITERS, step, 0)


def shift(x, axis, by):
    size = lax.axis_size(axis)
    return lax.ppermute(x, axis, [(i, (i - by) % size) for i in range(size)])


def chain_gathered(gradient, jacobi, tiles, local, remote, live):
    width = gradient.shape[0]
    blocks, slots = jacobi.shape[0], local.shape[0]
    devices = lax.axis_size("rows")
    groups = devices // 2
    packed = call(
        pack_kernel,
        jax.ShapeDtypeStruct((slots, BLOCK + width, BLOCK), f32),
        local,
        gradient,
        jacobi,
        tiles,
        scalars=1,
    )
    near = jnp.stack([packed] + [shift(packed, "rows", 2 * o) for o in range(1, groups)])
    far = lax.ppermute(near, "rows", [(i, i ^ 1) for i in range(devices)])

    own = jnp.concatenate([local, remote, live.astype(jnp.int32)])
    own = jnp.pad(own, (0, BLOCK - own.shape[0]))
    told = jnp.broadcast_to(own[None, None, :], (devices, 1, BLOCK))
    told = lax.all_to_all(told, "rows", 0, 0, tiled=True)[:, 0]
    me = lax.axis_index("rows")
    position = jnp.arange(devices, dtype=jnp.int32)
    base = me ^ (position // groups)
    device = (base + 2 * (position % groups)) % devices
    pick = (device[:, None] == jnp.arange(devices, dtype=jnp.int32)[None, :]).astype(jnp.int32)
    told = jnp.sum(pick[:, :, None] * told[None, :, :], axis=1)
    locals_, remotes, lives = (
        told[:, i * slots : (i + 1) * slots] for i in range(3)
    )
    owner = (remotes // blocks).reshape(-1)
    holder = jnp.broadcast_to(device[:, None], locals_.shape).reshape(-1)
    alive = lives.reshape(-1) > 0
    meets = (
        (owner[:, None] == holder[None, :])
        & (owner[None, :] == holder[:, None])
        & alive[None, :]
    )
    total = devices * slots
    numbers = jnp.arange(total, dtype=jnp.int32)
    partner = jnp.sum(jnp.where(meets, numbers[None, :], 0), axis=1).reshape(devices, slots)
    same = (
        (locals_[:, :, None] == locals_[:, None, :])
        & (lives[:, None, :] > 0)
        & (lives[:, :, None] > 0)
    )
    sources = jnp.where(same, partner[:, None, :], total).reshape(-1)
    return call(
        chain_kernel,
        jax.ShapeDtypeStruct((ITERS, slots, width, BLOCK), f32),
        sources,
        near,
        far,
        scalars=1,
        scratch=[
            pltpu.VMEM((total, BLOCK, BLOCK), jnp.bfloat16),
            pltpu.VMEM((total, BLOCK, BLOCK), jnp.bfloat16),
            pltpu.VMEM((total, width, BLOCK), f32),
            pltpu.VMEM((total + 1, width, BLOCK), f32),
        ],
    )


def chain_exchanged(gradient, jacobi, tiles, local, remote, live):
    width = gradient.shape[0]
    blocks = jacobi.shape[0]
    devices = lax.axis_size("rows")
    owner = remote // blocks
    placing = (
        (local[:, None] == jnp.arange(blocks, dtype=jnp.int32)[None, :]) & live[:, None]
    ).astype(f32)
    meets = live[:, None] & (owner[:, None] == jnp.arange(devices, dtype=jnp.int32)[None, :])
    granted = jnp.sum(jnp.where(meets, local[:, None], 0), axis=0)
    vector = jnp.transpose(gradient.reshape(width, blocks, BLOCK), (1, 0, 2))
    steps = []
    for _ in range(ITERS):
        sent = jnp.einsum("nej,nji->nei", vector, jacobi, precision=highest)[granted]
        incoming = lax.all_to_all(sent, "rows", 0, 0, tiled=True)
        products = jnp.einsum(
            "kej,kji->kei", incoming[owner], tiles.astype(f32), precision=highest
        )
        vector = jnp.einsum("kei,kn->nei", products, placing, precision=highest)
        steps.append(vector)
    return jnp.stack(steps)


def basis_kernel(turn, *refs):
    devices = len(refs) - 5
    pieces, jacobi = refs[:devices], refs[devices]
    mixes, plain, smooth, scale = refs[devices + 1 :]
    width = pieces[0].shape[0]
    blocks = jacobi.shape[0]
    rows = blocks * BLOCK
    factor = jnp.concatenate([piece[:, rows:] for piece in pieces], 0)
    factor = pltpu.roll(factor, turn[0], 1)
    norm = jnp.max(jnp.sum(jnp.abs(factor), axis=1, keepdims=True), axis=0, keepdims=True)
    power = factor / norm
    for _ in range(3):
        power = dot(power, power)
    bound = jnp.sum(jnp.sum(power * power, axis=1, keepdims=True), axis=0, keepdims=True)
    for _ in range(4):
        bound = jnp.sqrt(bound)
    ratio = 2.0 / (STRETCH * bound * norm)
    scale[...] = jnp.broadcast_to(ratio, scale.shape)
    factor = factor * ratio

    row = lax.broadcasted_iota(jnp.int32, (width, BLOCK), 0)
    lane = lax.broadcasted_iota(jnp.int32, (width, BLOCK), 1)
    kept = [[(row == lane).astype(f32)]]
    for k in range(ITERS):
        last = kept[k]
        terms = [last[0]] + [last[j] + last[j - 1] for j in range(1, k + 1)] + [last[k]]
        image = dot(jnp.concatenate(terms, 0), factor)
        fresh = []
        for j in range(k + 2):
            value = image[j * width : (j + 1) * width]
            if j <= k:
                value = value - last[j]
            if k:
                value = 2.0 * value
                if j <= k - 1:
                    value = value - kept[k - 1][j]
            fresh.append(value)
        kept.append(fresh)
    at = 0
    for j in range(1, ITERS + 1):
        for k in range(j, ITERS + 1):
            mixes[at : at + width, :] = kept[k][j]
            at += width
    first = jnp.concatenate([kept[k][0] for k in range(ITERS + 1)], 0)
    for b in range(blocks):
        columns = slice(b * BLOCK, (b + 1) * BLOCK)
        whole = jnp.concatenate([piece[:, columns] for piece in pieces], 0)
        value = dot(first, whole)
        plain[b] = value
        smooth[b] = dot(value[: ITERS * width], jacobi[b])


def mix_kernel(local, used, *refs):
    devices = len(refs) - 10
    chains = refs[:devices]
    gradient, mixes, plain, smooth, jacobi = refs[devices : devices + 5]
    images, precond, gram, basis, added = refs[devices + 5 :]
    slots, width = chains[0].shape[1:3]
    blocks = jacobi.shape[0]
    tall = ITERS * width
    basis[...] = plain[...]
    precond[...] = smooth[...]
    for slot in range(slots):
        added[...] = jnp.zeros(added.shape, f32)
        at = 0
        for j in range(1, ITERS + 1):
            count = (ITERS + 1 - j) * width
            whole = jnp.concatenate([chain[j - 1, slot] for chain in chains], 0)
            added[j * width :, :] += dot(mixes[at : at + count, :], whole)
            at += count

        @pl.when(used[slot] > 0)
        def _():
            block = local[slot]
            basis[block] += added[...]
            precond[block] += dot(added[:tall, :], jacobi[block])

    sums = {}
    for b in range(blocks):
        for r in range(0, width, 8):
            s = [basis[b, k * width + r : k * width + r + 8, :] for k in range(ITERS + 1)]
            y = [precond[b, k * width + r : k * width + r + 8, :] for k in range(ITERS)]
            g = gradient[r : r + 8, b * BLOCK : (b + 1) * BLOCK]
            f = [s[0] + s[1]]
            for j in range(1, ITERS):
                f.append(0.5 * (s[j - 1] + s[j + 1]) + s[j])
            for j in range(ITERS):
                images[b, j * width + r : j * width + r + 8, :] = f[j]
            for i in range(ITERS):
                for j in range(i + 1):
                    sums[i, j] = sums.get((i, j), 0.0) + y[i] * f[j]
                sums[i, ITERS] = sums.get((i, ITERS), 0.0) + y[i] * g
    lane = lax.broadcasted_iota(jnp.int32, (1, BLOCK), 1)
    result = jnp.zeros((1, BLOCK), f32)
    for (i, j), value in sums.items():
        value = jnp.sum(jnp.sum(value, axis=0, keepdims=True), axis=1, keepdims=True)
        here = lane == 16 * i + j
        if j < ITERS:
            here = here | (lane == 16 * j + i)
        result = jnp.where(here, value, result)
    gram[...] = result


def finish_kernel(grams, scale, gradient, precond, images, solution, residual):
    width = gradient.shape[0]
    blocks = precond.shape[0]
    flat = jnp.sum(grams[:, 0, :], axis=0, keepdims=True)
    row = lax.broadcasted_iota(jnp.int32, (8, BLOCK), 0)
    lane = lax.broadcasted_iota(jnp.int32, (8, BLOCK), 1)
    table = jnp.zeros((8, BLOCK), f32)
    for i in range(ITERS):
        moved = flat if i == 0 else pltpu.roll(flat, BLOCK - 16 * i, 1)
        table = jnp.where((row == i) & (lane <= ITERS), moved, table)
    for p in range(ITERS):
        pivot = table[p : p + 1, :] / table[p : p + 1, p : p + 1]
        table = jnp.where(row == p, pivot, table - table[:, p : p + 1] * pivot)
    steps = [table[j : j + 1, ITERS : ITERS + 1] for j in range(ITERS)]
    longer = scale[0:1, 0:1]
    for b in range(blocks):
        columns = slice(b * BLOCK, (b + 1) * BLOCK)
        total = steps[0] * precond[b, :width, :]
        left = gradient[:, columns] - steps[0] * images[b, :width, :]
        for j in range(1, ITERS):
            part = slice(j * width, (j + 1) * width)
            total = total + steps[j] * precond[b, part, :]
            left = left - steps[j] * images[b, part, :]
        solution[:, columns] = longer * total
        residual[:, columns] = left


def on_device(
    gradient,
    width_factor,
    diag_blocks,
    jacobi_inverse,
    coupling_tiles,
    tile_local,
    tile_remote,
    tile_count,
    exchange=False,
):
    width, rows = gradient.shape
    blocks = diag_blocks.shape[0]
    columns = lax.axis_size("cols")
    devices = lax.axis_size("rows")
    slots = tile_local.shape[0] - 1
    local, remote, tiles = tile_local[:slots], tile_remote[:slots], coupling_tiles[:slots]
    live = jnp.arange(slots, dtype=jnp.int32) < tile_count[0]

    piece = jnp.concatenate([gradient, width_factor.T], axis=1)
    pieces = [piece] + [shift(piece, "cols", o) for o in range(1, columns)]

    gathered = devices * slots * BLOCK * (BLOCK + width) * 4
    if gathered <= GATHER_BYTES and devices % 2 == 0 and not exchange:
        chain = chain_gathered(gradient, jacobi_inverse, tiles, local, remote, live)
        earlier = jnp.arange(slots)[:, None] > jnp.arange(slots)[None, :]
        repeat = jnp.any(earlier & (local[:, None] == local[None, :]), axis=1)
        used = (live & ~repeat).astype(jnp.int32)
        at = local
    else:
        chain = chain_exchanged(gradient, jacobi_inverse, tiles, local, remote, live)
        at = jnp.arange(blocks, dtype=jnp.int32)
        used = jnp.ones((blocks,), jnp.int32)
    chains = [chain] + [shift(chain, "cols", o) for o in range(1, columns)]

    turn = (BLOCK - width * lax.axis_index("cols")) % BLOCK
    shape = jax.ShapeDtypeStruct
    count = ITERS * (ITERS + 1) // 2
    mixes, plain, smooth, scale = call(
        basis_kernel,
        (
            shape((count * width, BLOCK), f32),
            shape((blocks, (ITERS + 1) * width, BLOCK), f32),
            shape((blocks, ITERS * width, BLOCK), f32),
            shape((8, BLOCK), f32),
        ),
        turn.astype(jnp.int32).reshape(1),
        *pieces,
        jacobi_inverse,
        scalars=1,
    )
    images, precond, gram = call(
        mix_kernel,
        (
            shape((blocks, ITERS * width, BLOCK), f32),
            shape((blocks, ITERS * width, BLOCK), f32),
            shape((1, BLOCK), f32),
        ),
        at,
        used,
        *chains,
        gradient,
        mixes,
        plain,
        smooth,
        jacobi_inverse,
        scalars=2,
        scratch=[
            pltpu.VMEM((blocks, (ITERS + 1) * width, BLOCK), f32),
            pltpu.VMEM(((ITERS + 1) * width, BLOCK), f32),
        ],
    )
    everyone = columns * devices
    grams = lax.all_to_all(
        jnp.broadcast_to(gram[None], (everyone, 1, BLOCK)),
        ("cols", "rows"),
        0,
        0,
        tiled=True,
    )
    return call(
        finish_kernel,
        (shape((width, rows), f32), shape((width, rows), f32)),
        grams,
        scale,
        gradient,
        precond,
        images,
    )


def solution(mesh):
    placed = (
        P("cols", "rows"),
        P(None, "cols"),
        P("rows", None, None),
        P("rows", None, None),
        P("rows", None, None),
        P("rows"),
        P("rows"),
        P("rows"),
    )
    return jax.shard_map(
        on_device,
        mesh=mesh,
        in_specs=placed,
        out_specs=(P("cols", "rows"), P("cols", "rows")),
        check_vma=False,
    )
```

```python
import functools

import jax
import jax.numpy as jnp
from jax import lax
from jax.experimental import pallas as pl
from jax.experimental.pallas import tpu as pltpu
from jax.sharding import PartitionSpec as P

BLOCK = 128
ITERS = 6
STRETCH = 1.1
GATHER_BYTES = 8 * 2**20


GRANT_BYTES = 24 * 2**20

highest = lax.Precision.HIGHEST
f32 = jnp.float32
VMEM = pl.BlockSpec(memory_space=pltpu.VMEM)
SMEM = pl.BlockSpec(memory_space=pltpu.SMEM)


def dot(a, b):
    return jnp.dot(a, b, precision=highest, preferred_element_type=f32)


def call(kernel, outs, *args, scalars=0, scratch=()):
    specs = [SMEM] * scalars + [VMEM] * (len(args) - scalars)
    many = isinstance(outs, tuple)
    return pl.pallas_call(
        kernel,
        out_shape=outs,
        in_specs=specs,
        out_specs=tuple([VMEM] * len(outs)) if many else VMEM,
        scratch_shapes=list(scratch),
        compiler_params=pltpu.CompilerParams(vmem_limit_bytes=GRANT_BYTES),
    )(*args)


def split(x):
    high = x.astype(jnp.bfloat16)
    return high, (x - high.astype(f32)).astype(jnp.bfloat16)


def plain_dot(a, b):
    return jnp.dot(a, b, preferred_element_type=f32)


def dot3(a, b):
    tall = a.shape[0]
    high, low = split(a)
    right, rest = split(b)
    both = plain_dot(jnp.concatenate([high, low], 0), right)
    return both[:tall] + (both[tall:] + plain_dot(high, rest))


def pack_kernel(local, gradient, jacobi, tiles, packed):
    contract = (((1,), (1,)), ((), ()))
    for slot in range(packed.shape[0]):
        block = local[slot]
        halves = jnp.concatenate(split(jacobi[block]), 0)
        both = lax.dot_general(halves, tiles[slot], contract, preferred_element_type=f32)
        packed[slot, :BLOCK, :] = both[:BLOCK] + both[BLOCK:]
        columns = pl.ds(pl.multiple_of(block * BLOCK, BLOCK), BLOCK)
        packed[slot, BLOCK:, :] = gradient[:, columns]


def chain_kernel(sources, near, far, chain, high, low, held, out):
    groups, slots = near.shape[:2]
    half = groups * slots
    total = 2 * half
    width = near.shape[2] - BLOCK
    for q in range(total):
        ref = near if q < half else far
        group, slot = divmod(q % half, slots)
        high[q], low[q] = split(ref[group, slot, :BLOCK, :])
        held[q] = ref[group, slot, BLOCK:, :]
    out[total] = jnp.zeros((width, BLOCK), f32)

    def step(j, carry):
        for q in range(total):
            first, second = split(held[q])
            both = jnp.dot(
                jnp.concatenate([first, second], 0), high[q], preferred_element_type=f32
            )
            rest = jnp.dot(first, low[q], preferred_element_type=f32)
            out[q] = both[:width] + both[width:] + rest
        for q in range(total):
            value = out[sources[q * slots]]
            for i in range(1, slots):
                value += out[sources[q * slots + i]]
            held[q] = value
        for slot in range(slots):
            chain[j, slot] = held[slot]
        return carry

    lax.fori_loop(0, ITERS, step, 0)


def shift(x, axis, by):
    size = lax.axis_size(axis)
    return lax.ppermute(x, axis, [(i, (i - by) % size) for i in range(size)])


def whole_pieces(gradient, factor):
    piece = jnp.concatenate([gradient, factor.T], axis=1)
    return [piece] + [shift(piece, "cols", o) for o in range(1, lax.axis_size("cols"))]


def chain_gathered(gradient, factor, jacobi, tiles, whole_local, local, remote, live):
    width = gradient.shape[0]
    blocks, slots = jacobi.shape[0], local.shape[0]
    devices = lax.axis_size("rows")
    groups = devices // 2
    packed = call(
        pack_kernel,
        jax.ShapeDtypeStruct((slots, BLOCK + width, BLOCK), f32),
        whole_local,
        gradient,
        jacobi,
        tiles,
        scalars=1,
    )
    near = [packed] + [shift(packed, "rows", 2 * o) for o in range(1, groups)]
    gradient, factor, _ = lax.optimization_barrier((gradient, factor, packed))
    pieces = whole_pieces(gradient, factor)
    own = jnp.concatenate([local, remote, live.astype(jnp.int32)])
    own = jnp.pad(own, (0, BLOCK - own.shape[0]))
    told = jnp.broadcast_to(own[None, None, :], (devices, 1, BLOCK))
    told = lax.all_to_all(told, "rows", 0, 0, tiled=True)[:, 0]
    near, pieces, told = lax.optimization_barrier((near, pieces, told))
    near = jnp.stack(near)
    far = lax.ppermute(near, "rows", [(i, i ^ 1) for i in range(devices)])

    me = lax.axis_index("rows")
    position = jnp.arange(devices, dtype=jnp.int32)
    base = me ^ (position // groups)
    device = (base + 2 * (position % groups)) % devices
    pick = (device[:, None] == jnp.arange(devices, dtype=jnp.int32)[None, :]).astype(jnp.int32)
    told = jnp.sum(pick[:, :, None] * told[None, :, :], axis=1)
    locals_, remotes, lives = (
        told[:, i * slots : (i + 1) * slots] for i in range(3)
    )
    owner = (remotes // blocks).reshape(-1)
    holder = jnp.broadcast_to(device[:, None], locals_.shape).reshape(-1)
    alive = lives.reshape(-1) > 0
    meets = (
        (owner[:, None] == holder[None, :])
        & (owner[None, :] == holder[:, None])
        & alive[None, :]
    )
    total = devices * slots
    numbers = jnp.arange(total, dtype=jnp.int32)
    partner = jnp.sum(jnp.where(meets, numbers[None, :], 0), axis=1).reshape(devices, slots)
    same = (
        (locals_[:, :, None] == locals_[:, None, :])
        & (lives[:, None, :] > 0)
        & (lives[:, :, None] > 0)
    )
    sources = jnp.where(same, partner[:, None, :], total).reshape(-1)
    chain = call(
        chain_kernel,
        jax.ShapeDtypeStruct((ITERS, slots, width, BLOCK), f32),
        sources,
        near,
        far,
        scalars=1,
        scratch=[
            pltpu.VMEM((total, BLOCK, BLOCK), jnp.bfloat16),
            pltpu.VMEM((total, BLOCK, BLOCK), jnp.bfloat16),
            pltpu.VMEM((total, width, BLOCK), f32),
            pltpu.VMEM((total + 1, width, BLOCK), f32),
        ],
    )
    return chain, pieces


def chain_exchanged(gradient, jacobi, tiles, local, remote, live):
    width = gradient.shape[0]
    blocks = jacobi.shape[0]
    devices = lax.axis_size("rows")
    owner = remote // blocks
    placing = (
        (local[:, None] == jnp.arange(blocks, dtype=jnp.int32)[None, :]) & live[:, None]
    ).astype(f32)
    meets = live[:, None] & (owner[:, None] == jnp.arange(devices, dtype=jnp.int32)[None, :])
    granted = jnp.sum(jnp.where(meets, local[:, None], 0), axis=0)
    vector = jnp.transpose(gradient.reshape(width, blocks, BLOCK), (1, 0, 2))
    steps = []
    for _ in range(ITERS):
        sent = jnp.einsum("nej,nji->nei", vector, jacobi, precision=highest)[granted]
        incoming = lax.all_to_all(sent, "rows", 0, 0, tiled=True)
        products = jnp.einsum(
            "kej,kji->kei", incoming[owner], tiles.astype(f32), precision=highest
        )
        vector = jnp.einsum("kei,kn->nei", products, placing, precision=highest)
        steps.append(vector)
    return jnp.stack(steps)


def basis_kernel(turn, *refs):
    devices = len(refs) - 5
    pieces, jacobi = refs[:devices], refs[devices]
    mixes, plain, smooth, scale = refs[devices + 1 :]
    width = pieces[0].shape[0]
    blocks = jacobi.shape[0]
    rows = blocks * BLOCK
    factor = jnp.concatenate([piece[:, rows:] for piece in pieces], 0)
    factor = pltpu.roll(factor, turn[0], 1)
    norm = jnp.max(jnp.sum(jnp.abs(factor), axis=1, keepdims=True), axis=0, keepdims=True)
    power = factor / norm
    for _ in range(3):
        power = dot(power, power)
    bound = jnp.sum(jnp.sum(power * power, axis=1, keepdims=True), axis=0, keepdims=True)
    for _ in range(4):
        bound = jnp.sqrt(bound)
    ratio = 2.0 / (STRETCH * bound * norm)
    scale[...] = jnp.broadcast_to(ratio, scale.shape)
    factor = factor * ratio

    row = lax.broadcasted_iota(jnp.int32, (width, BLOCK), 0)
    lane = lax.broadcasted_iota(jnp.int32, (width, BLOCK), 1)
    kept = [[(row == lane).astype(f32)]]
    for k in range(ITERS):
        last = kept[k]
        terms = [last[0]] + [last[j] + last[j - 1] for j in range(1, k + 1)] + [last[k]]
        image = dot(jnp.concatenate(terms, 0), factor)
        fresh = []
        for j in range(k + 2):
            value = image[j * width : (j + 1) * width]
            if j <= k:
                value = value - last[j]
            if k:
                value = 2.0 * value
                if j <= k - 1:
                    value = value - kept[k - 1][j]
            fresh.append(value)
        kept.append(fresh)
    at = 0
    for j in range(1, ITERS + 1):
        for k in range(j, ITERS + 1):
            mixes[at : at + width, :] = kept[k][j]
            at += width
    first = jnp.concatenate([kept[k][0] for k in range(ITERS + 1)], 0)
    for b in range(blocks):
        columns = slice(b * BLOCK, (b + 1) * BLOCK)
        whole = jnp.concatenate([piece[:, columns] for piece in pieces], 0)
        value = dot(first, whole)
        plain[b] = value
        smooth[b] = dot(value[: ITERS * width], jacobi[b])


def mix_kernel(local, index, *refs):
    devices = len(refs) - 8
    chains = refs[:devices]
    gradient, mixes, plain, smooth, jacobi = refs[devices : devices + 5]
    added, smoothed, gram = refs[devices + 5 :]
    slots, width = chains[0].shape[1:3]
    blocks = jacobi.shape[0]
    short = (ITERS - 1) * width
    totals = [0.0] * ITERS
    at = 0
    for j in range(1, ITERS + 1):
        count = (ITERS + 1 - j) * width
        whole = jnp.concatenate(
            [
                jnp.concatenate([chain[j - 1, slot] for chain in chains], 0)
                for slot in range(slots)
            ],
            1,
        )
        part = dot3(mixes[at : at + count, :], whole)
        at += count
        for k in range(j, ITERS + 1):
            totals[k - 1] += part[(k - j) * width : (k - j + 1) * width]
    for slot in range(slots):
        columns = slice(slot * BLOCK, (slot + 1) * BLOCK)
        value = jnp.concatenate([total[:, columns] for total in totals], 0)
        added[slot] = value
        smoothed[slot] = dot3(value[:short], jacobi[local[slot]])
    added[slots] = jnp.zeros(added.shape[1:], f32)
    smoothed[slots] = jnp.zeros(smoothed.shape[1:], f32)

    sums = {}
    for b in range(blocks):
        slot = index[b]
        for r in range(0, width, 8):
            s = [plain[b, k * width + r : k * width + r + 8, :] for k in range(ITERS + 1)]
            y = [smooth[b, k * width + r : k * width + r + 8, :] for k in range(ITERS)]
            for k in range(1, ITERS + 1):
                rows = slice((k - 1) * width + r, (k - 1) * width + r + 8)
                s[k] = s[k] + added[slot, rows, :]
                if k < ITERS:
                    y[k] = y[k] + smoothed[slot, rows, :]
            g = gradient[r : r + 8, b * BLOCK : (b + 1) * BLOCK]
            f = [s[0] + s[1]]
            for j in range(1, ITERS):
                f.append(0.5 * (s[j - 1] + s[j + 1]) + s[j])
            for i in range(ITERS):
                for j in range(i + 1):
                    sums[i, j] = sums.get((i, j), 0.0) + y[i] * f[j]
                sums[i, ITERS] = sums.get((i, ITERS), 0.0) + y[i] * g
    lane = lax.broadcasted_iota(jnp.int32, (1, BLOCK), 1)
    result = jnp.zeros((1, BLOCK), f32)
    for (i, j), value in sums.items():
        value = jnp.sum(jnp.sum(value, axis=0, keepdims=True), axis=1, keepdims=True)
        here = lane == 16 * i + j
        if j < ITERS:
            here = here | (lane == 16 * j + i)
        result = jnp.where(here, value, result)
    gram[...] = result


def finish_kernel(
    index, grams, scale, gradient, plain, smooth, added, smoothed, solution, residual, extra, less
):
    width = gradient.shape[0]
    blocks = plain.shape[0]
    slots = added.shape[0] - 1
    flat = jnp.sum(grams[:, 0, :], axis=0, keepdims=True)
    row = lax.broadcasted_iota(jnp.int32, (8, BLOCK), 0)
    lane = lax.broadcasted_iota(jnp.int32, (8, BLOCK), 1)
    table = jnp.zeros((8, BLOCK), f32)
    for i in range(ITERS):
        moved = flat if i == 0 else pltpu.roll(flat, BLOCK - 16 * i, 1)
        table = jnp.where((row == i) & (lane <= ITERS), moved, table)
    for p in range(ITERS):
        pivot = table[p : p + 1, :] / table[p : p + 1, p : p + 1]
        table = jnp.where(row == p, pivot, table - table[:, p : p + 1] * pivot)
    steps = [table[j : j + 1, ITERS : ITERS + 1] for j in range(ITERS)]
    takes = []
    for k in range(ITERS + 1):
        value = 0.0
        if k > 0:
            value += steps[k - 1] * (1.0 if k == 1 else 0.5)
        if k < ITERS:
            value += steps[k]
        if k + 1 < ITERS:
            value += 0.5 * steps[k + 1]
        takes.append(jnp.broadcast_to(value, (width, BLOCK)))
    longer = scale[0:1, 0:1]
    gives = [jnp.broadcast_to(longer * step, (width, BLOCK)) for step in steps]

    def combine(weights, ref, b, start):
        total = None
        for j, weight in enumerate(weights):
            term = weight * ref[b, (start + j) * width : (start + j + 1) * width, :]
            total = term if total is None else total + term
        return total

    for slot in range(slots):
        extra[slot] = combine(gives[1:], smoothed, slot, 0)
        less[slot] = combine(takes[1:], added, slot, 0)
    extra[slots] = jnp.zeros((width, BLOCK), f32)
    less[slots] = jnp.zeros((width, BLOCK), f32)
    for b in range(blocks):
        columns = slice(b * BLOCK, (b + 1) * BLOCK)
        slot = index[b]
        solution[:, columns] = combine(gives, smooth, b, 0) + extra[slot]
        residual[:, columns] = gradient[:, columns] - combine(takes, plain, b, 0) - less[slot]


def on_device(
    gradient,
    width_factor,
    diag_blocks,
    jacobi_inverse,
    coupling_tiles,
    tile_local,
    tile_remote,
    tile_count,
    exchange=False,
):
    width, rows = gradient.shape
    blocks = diag_blocks.shape[0]
    columns = lax.axis_size("cols")
    devices = lax.axis_size("rows")
    slots = tile_local.shape[0] - 1
    live = jnp.arange(slots, dtype=jnp.int32) < tile_count[0]
    lists = (tile_local[:slots], tile_remote[:slots], live)

    numbers = jnp.arange(blocks, dtype=jnp.int32)
    gathered = devices * slots * BLOCK * (BLOCK + width) * 4
    if gathered <= GATHER_BYTES and devices % 2 == 0 and not exchange:
        chain, pieces = chain_gathered(
            gradient, width_factor, jacobi_inverse, coupling_tiles, tile_local, *lists
        )
        at = tile_local
        here = (lists[0][None, :] == numbers[:, None]) & live[None, :]
        order = jnp.arange(slots, dtype=jnp.int32)[None, :]
        index = jnp.min(jnp.where(here, order, slots), axis=1)
    else:
        chain = chain_exchanged(gradient, jacobi_inverse, coupling_tiles[:slots], *lists)
        pieces = whole_pieces(gradient, width_factor)
        at, index = numbers, numbers
    units = chain.shape[1]
    chains = [chain] + [shift(chain, "cols", o) for o in range(1, columns)]

    turn = (BLOCK - width * lax.axis_index("cols")) % BLOCK
    shape = jax.ShapeDtypeStruct
    count = ITERS * (ITERS + 1) // 2
    mixes, plain, smooth, scale = call(
        basis_kernel,
        (
            shape((count * width, BLOCK), f32),
            shape((blocks, (ITERS + 1) * width, BLOCK), f32),
            shape((blocks, ITERS * width, BLOCK), f32),
            shape((8, BLOCK), f32),
        ),
        turn.astype(jnp.int32).reshape(1),
        *pieces,
        jacobi_inverse,
        scalars=1,
    )
    added, smoothed, gram = call(
        mix_kernel,
        (
            shape((units + 1, ITERS * width, BLOCK), f32),
            shape((units + 1, (ITERS - 1) * width, BLOCK), f32),
            shape((1, BLOCK), f32),
        ),
        at,
        index,
        *chains,
        gradient,
        mixes,
        plain,
        smooth,
        jacobi_inverse,
        scalars=2,
    )
    everyone = columns * devices
    grams = lax.all_to_all(
        jnp.broadcast_to(gram[None], (everyone, 1, BLOCK)),
        ("cols", "rows"),
        0,
        0,
        tiled=True,
    )
    return call(
        finish_kernel,
        (shape((width, rows), f32), shape((width, rows), f32)),
        index,
        grams,
        scale,
        gradient,
        plain,
        smooth,
        added,
        smoothed,
        scalars=1,
        scratch=[pltpu.VMEM((units + 1, width, BLOCK), f32)] * 2,
    )


def solution(mesh):
    placed = (
        P("cols", "rows"),
        P(None, "cols"),
        P("rows", None, None),
        P("rows", None, None),
        P("rows", None, None),
        P("rows"),
        P("rows"),
        P("rows"),
    )
    return jax.shard_map(
        on_device,
        mesh=mesh,
        in_specs=placed,
        out_specs=(P("cols", "rows"), P("cols", "rows")),
        check_vma=False,
    )
```

```python
import jax
import jax.numpy as jnp
from jax import lax
from jax.experimental import pallas as pl
from jax.experimental.pallas import tpu as pltpu
from jax.sharding import PartitionSpec as P


BLOCK = 128
ITERS = 6
STRETCH = 1.1
GATHER_BYTES = 8 * 2**20


GRANT_BYTES = 24 * 2**20
WHOLE_BYTES = 60 * 2**20

highest = lax.Precision.HIGHEST
f32 = jnp.float32
VMEM = pl.BlockSpec(memory_space=pltpu.VMEM)
SMEM = pl.BlockSpec(memory_space=pltpu.SMEM)


def dot(a, b):
    return jnp.dot(a, b, precision=highest, preferred_element_type=f32)


def call(kernel, outs, *args, scalars=0, scratch=(), place=VMEM, grant=GRANT_BYTES):
    specs = [SMEM] * scalars + [place] * (len(args) - scalars)
    many = isinstance(outs, tuple)
    return pl.pallas_call(
        kernel,
        out_shape=outs,
        in_specs=specs,
        out_specs=tuple([VMEM] * len(outs)) if many else VMEM,
        scratch_shapes=list(scratch),
        compiler_params=pltpu.CompilerParams(vmem_limit_bytes=grant),
    )(*args)


def split(x):
    high = x.astype(jnp.bfloat16)
    return high, (x - high.astype(f32)).astype(jnp.bfloat16)


def plain_dot(a, b):
    return jnp.dot(a, b, preferred_element_type=f32)


def dot3(a, b):
    tall = a.shape[0]
    high, low = split(a)
    right, rest = split(b)
    both = plain_dot(jnp.concatenate([high, low], 0), right)
    return both[:tall] + (both[tall:] + plain_dot(high, rest))


def pack_kernel(local, gradient, jacobi, tiles, packed, inverse, coupling, part, done):
    slots = packed.shape[0]
    contract = (((1,), (1,)), ((), ()))
    copies = []
    for slot in range(slots):
        block = local[slot]
        columns = pl.ds(pl.multiple_of(block * BLOCK, BLOCK), BLOCK)
        moves = [
            (jacobi.at[block], inverse.at[slot]),
            (tiles.at[slot], coupling.at[slot]),
            (gradient.at[:, columns], part.at[slot]),
        ]
        for i, (source, target) in enumerate(moves):
            copy = pltpu.make_async_copy(source, target, done.at[slot, i])
            copy.start()
            copies.append(copy)
    for slot in range(slots):
        for copy in copies[3 * slot : 3 * slot + 3]:
            copy.wait()
        halves = jnp.concatenate(split(inverse[slot]), 0)
        both = lax.dot_general(halves, coupling[slot], contract, preferred_element_type=f32)
        packed[slot, :BLOCK, :] = both[:BLOCK] + both[BLOCK:]
        packed[slot, BLOCK:, :] = part[slot]


def chain_kernel(sources, near, far, chain, high, low, held, out):
    groups, slots = near.shape[:2]
    half = groups * slots
    total = 2 * half
    width = near.shape[2] - BLOCK
    for q in range(total):
        ref = near if q < half else far
        group, slot = divmod(q % half, slots)
        high[q], low[q] = split(ref[group, slot, :BLOCK, :])
        held[q] = ref[group, slot, BLOCK:, :]
    out[total] = jnp.zeros((width, BLOCK), f32)

    def step(j, carry):
        for q in range(total):
            first, second = split(held[q])
            both = jnp.dot(
                jnp.concatenate([first, second], 0), high[q], preferred_element_type=f32
            )
            rest = jnp.dot(first, low[q], preferred_element_type=f32)
            out[q] = both[:width] + both[width:] + rest
        for q in range(total):
            value = out[sources[q * slots]]
            for i in range(1, slots):
                value += out[sources[q * slots + i]]
            held[q] = value
        for slot in range(slots):
            chain[j, slot] = held[slot]
        return carry

    lax.fori_loop(0, ITERS, step, 0)


def shift(x, axis, by):
    size = lax.axis_size(axis)
    return lax.ppermute(x, axis, [(i, (i - by) % size) for i in range(size)])


def whole_pieces(gradient, factor):
    piece = jnp.concatenate([gradient, factor.T], axis=1)
    others = range(1, lax.axis_size("cols"))
    return [piece] + [shift(piece, "cols", o) for o in others]


def chain_gathered(gradient, factor, jacobi, tiles, whole_local, local, remote, live):
    width = gradient.shape[0]
    blocks, slots = jacobi.shape[0], local.shape[0]
    devices = lax.axis_size("rows")
    groups = devices // 2
    packed = call(
        pack_kernel,
        jax.ShapeDtypeStruct((slots, BLOCK + width, BLOCK), f32),
        whole_local,
        gradient,
        jacobi,
        tiles,
        scalars=1,
        scratch=[
            pltpu.VMEM((slots, BLOCK, BLOCK), f32),
            pltpu.VMEM((slots, BLOCK, BLOCK), tiles.dtype),
            pltpu.VMEM((slots, width, BLOCK), f32),
            pltpu.SemaphoreType.DMA((slots, 3)),
        ],
        place=pl.BlockSpec(memory_space=pl.ANY),
        grant=WHOLE_BYTES,
    )
    near = [packed] + [shift(packed, "rows", 2 * o) for o in range(1, groups)]
    gradient, factor, _ = lax.optimization_barrier((gradient, factor, packed))
    pieces = whole_pieces(gradient, factor)
    own = jnp.concatenate([local, remote, live.astype(jnp.int32)])
    own = jnp.pad(own, (0, BLOCK - own.shape[0]))
    told = jnp.broadcast_to(own[None, None, :], (devices, 1, BLOCK))
    told = lax.all_to_all(told, "rows", 0, 0, tiled=True)[:, 0]
    near, pieces, told = lax.optimization_barrier((near, pieces, told))
    near = jnp.stack(near)
    far = lax.ppermute(near, "rows", [(i, i ^ 1) for i in range(devices)])

    me = lax.axis_index("rows")
    position = jnp.arange(devices, dtype=jnp.int32)
    base = me ^ (position // groups)
    device = (base + 2 * (position % groups)) % devices
    pick = (device[:, None] == jnp.arange(devices, dtype=jnp.int32)[None, :]).astype(jnp.int32)
    told = jnp.sum(pick[:, :, None] * told[None, :, :], axis=1)
    locals_, remotes, lives = (
        told[:, i * slots : (i + 1) * slots] for i in range(3)
    )
    owner = (remotes // blocks).reshape(-1)
    holder = jnp.broadcast_to(device[:, None], locals_.shape).reshape(-1)
    alive = lives.reshape(-1) > 0
    meets = (
        (owner[:, None] == holder[None, :])
        & (owner[None, :] == holder[:, None])
        & alive[None, :]
    )
    total = devices * slots
    numbers = jnp.arange(total, dtype=jnp.int32)
    partner = jnp.sum(jnp.where(meets, numbers[None, :], 0), axis=1).reshape(devices, slots)
    same = (
        (locals_[:, :, None] == locals_[:, None, :])
        & (lives[:, None, :] > 0)
        & (lives[:, :, None] > 0)
    )
    sources = jnp.where(same, partner[:, None, :], total).reshape(-1)
    chain = call(
        chain_kernel,
        jax.ShapeDtypeStruct((ITERS, slots, width, BLOCK), f32),
        sources,
        near,
        far,
        scalars=1,
        scratch=[
            pltpu.VMEM((total, BLOCK, BLOCK), jnp.bfloat16),
            pltpu.VMEM((total, BLOCK, BLOCK), jnp.bfloat16),
            pltpu.VMEM((total, width, BLOCK), f32),
            pltpu.VMEM((total + 1, width, BLOCK), f32),
        ],
    )
    return chain, pieces


def chain_exchanged(gradient, jacobi, tiles, local, remote, live):
    width = gradient.shape[0]
    blocks = jacobi.shape[0]
    devices = lax.axis_size("rows")
    owner = remote // blocks
    placing = (
        (local[:, None] == jnp.arange(blocks, dtype=jnp.int32)[None, :]) & live[:, None]
    ).astype(f32)
    meets = live[:, None] & (owner[:, None] == jnp.arange(devices, dtype=jnp.int32)[None, :])
    granted = jnp.sum(jnp.where(meets, local[:, None], 0), axis=0)
    vector = jnp.transpose(gradient.reshape(width, blocks, BLOCK), (1, 0, 2))
    steps = []
    for _ in range(ITERS):
        sent = jnp.einsum("nej,nji->nei", vector, jacobi, precision=highest)[granted]
        incoming = lax.all_to_all(sent, "rows", 0, 0, tiled=True)
        products = jnp.einsum(
            "kej,kji->kei", incoming[owner], tiles.astype(f32), precision=highest
        )
        vector = jnp.einsum("kei,kn->nei", products, placing, precision=highest)
        steps.append(vector)
    return jnp.stack(steps)


def basis_kernel(turn, *refs):
    devices = len(refs) - 5
    pieces, jacobi = refs[:devices], refs[devices]
    mixes, plain, smooth, scale = refs[devices + 1 :]
    width = pieces[0].shape[0]
    blocks = jacobi.shape[0]
    rows = blocks * BLOCK
    factor = jnp.concatenate([piece[:, rows:] for piece in pieces], 0)
    factor = pltpu.roll(factor, turn[0], 1)
    norm = jnp.max(jnp.sum(jnp.abs(factor), axis=1, keepdims=True), axis=0, keepdims=True)
    power = factor / norm
    for _ in range(3):
        power = dot(power, power)
    bound = jnp.sum(jnp.sum(power * power, axis=1, keepdims=True), axis=0, keepdims=True)
    for _ in range(4):
        bound = jnp.sqrt(bound)
    ratio = 2.0 / (STRETCH * bound * norm)
    scale[...] = jnp.broadcast_to(ratio, scale.shape)
    factor = factor * ratio

    row = lax.broadcasted_iota(jnp.int32, (width, BLOCK), 0)
    lane = lax.broadcasted_iota(jnp.int32, (width, BLOCK), 1)
    kept = [[(row == lane).astype(f32)]]
    for k in range(ITERS):
        last = kept[k]
        terms = [last[0]] + [last[j] + last[j - 1] for j in range(1, k + 1)] + [last[k]]
        image = dot(jnp.concatenate(terms, 0), factor)
        fresh = []
        for j in range(k + 2):
            value = image[j * width : (j + 1) * width]
            if j <= k:
                value = value - last[j]
            if k:
                value = 2.0 * value
                if j <= k - 1:
                    value = value - kept[k - 1][j]
            fresh.append(value)
        kept.append(fresh)
    at = 0
    for j in range(1, ITERS + 1):
        for k in range(j, ITERS + 1):
            mixes[at : at + width, :] = kept[k][j]
            at += width
    first = jnp.concatenate([kept[k][0] for k in range(ITERS + 1)], 0)
    for b in range(blocks):
        columns = slice(b * BLOCK, (b + 1) * BLOCK)
        whole = jnp.concatenate([piece[:, columns] for piece in pieces], 0)
        value = dot(first, whole)
        plain[b] = value
        smooth[b] = dot(value[: ITERS * width], jacobi[b])


def mix_kernel(local, index, *refs):
    devices = len(refs) - 8
    chains = refs[:devices]
    gradient, mixes, plain, smooth, jacobi = refs[devices : devices + 5]
    added, smoothed, gram = refs[devices + 5 :]
    slots, width = chains[0].shape[1:3]
    blocks = jacobi.shape[0]
    short = (ITERS - 1) * width
    totals = [0.0] * ITERS
    at = 0
    for j in range(1, ITERS + 1):
        count = (ITERS + 1 - j) * width
        whole = jnp.concatenate(
            [
                jnp.concatenate([chain[j - 1, slot] for chain in chains], 0)
                for slot in range(slots)
            ],
            1,
        )
        part = dot3(mixes[at : at + count, :], whole)
        at += count
        for k in range(j, ITERS + 1):
            totals[k - 1] += part[(k - j) * width : (k - j + 1) * width]
    for slot in range(slots):
        columns = slice(slot * BLOCK, (slot + 1) * BLOCK)
        value = jnp.concatenate([total[:, columns] for total in totals], 0)
        added[slot] = value
        smoothed[slot] = dot3(value[:short], jacobi[local[slot]])
    added[slots] = jnp.zeros(added.shape[1:], f32)
    smoothed[slots] = jnp.zeros(smoothed.shape[1:], f32)

    sums = {}
    for b in range(blocks):
        slot = index[b]
        for r in range(0, width, 8):
            s = [plain[b, k * width + r : k * width + r + 8, :] for k in range(ITERS + 1)]
            y = [smooth[b, k * width + r : k * width + r + 8, :] for k in range(ITERS)]
            for k in range(1, ITERS + 1):
                rows = slice((k - 1) * width + r, (k - 1) * width + r + 8)
                s[k] = s[k] + added[slot, rows, :]
                if k < ITERS:
                    y[k] = y[k] + smoothed[slot, rows, :]
            g = gradient[r : r + 8, b * BLOCK : (b + 1) * BLOCK]
            f = [s[0] + s[1]]
            for j in range(1, ITERS):
                f.append(0.5 * (s[j - 1] + s[j + 1]) + s[j])
            for i in range(ITERS):
                for j in range(i + 1):
                    sums[i, j] = sums.get((i, j), 0.0) + y[i] * f[j]
                sums[i, ITERS] = sums.get((i, ITERS), 0.0) + y[i] * g
    lane = lax.broadcasted_iota(jnp.int32, (1, BLOCK), 1)
    result = jnp.zeros((1, BLOCK), f32)
    for (i, j), value in sums.items():
        value = jnp.sum(jnp.sum(value, axis=0, keepdims=True), axis=1, keepdims=True)
        here = lane == 16 * i + j
        if j < ITERS:
            here = here | (lane == 16 * j + i)
        result = jnp.where(here, value, result)
    gram[...] = result


def finish_kernel(
    index, grams, scale, gradient, plain, smooth, added, smoothed, solution, residual, extra, less
):
    width = gradient.shape[0]
    blocks = plain.shape[0]
    slots = added.shape[0] - 1
    flat = jnp.sum(grams[:, 0, :], axis=0, keepdims=True)
    row = lax.broadcasted_iota(jnp.int32, (8, BLOCK), 0)
    lane = lax.broadcasted_iota(jnp.int32, (8, BLOCK), 1)
    table = jnp.zeros((8, BLOCK), f32)
    for i in range(ITERS):
        moved = flat if i == 0 else pltpu.roll(flat, BLOCK - 16 * i, 1)
        table = jnp.where((row == i) & (lane <= ITERS), moved, table)
    for p in range(ITERS):
        pivot = table[p : p + 1, :] / table[p : p + 1, p : p + 1]
        table = jnp.where(row == p, pivot, table - table[:, p : p + 1] * pivot)
    steps = [table[j : j + 1, ITERS : ITERS + 1] for j in range(ITERS)]
    takes = []
    for k in range(ITERS + 1):
        value = 0.0
        if k > 0:
            value += steps[k - 1] * (1.0 if k == 1 else 0.5)
        if k < ITERS:
            value += steps[k]
        if k + 1 < ITERS:
            value += 0.5 * steps[k + 1]
        takes.append(jnp.broadcast_to(value, (width, BLOCK)))
    longer = scale[0:1, 0:1]
    gives = [jnp.broadcast_to(longer * step, (width, BLOCK)) for step in steps]

    def combine(weights, ref, b, start):
        total = None
        for j, weight in enumerate(weights):
            term = weight * ref[b, (start + j) * width : (start + j + 1) * width, :]
            total = term if total is None else total + term
        return total

    for slot in range(slots):
        extra[slot] = combine(gives[1:], smoothed, slot, 0)
        less[slot] = combine(takes[1:], added, slot, 0)
    extra[slots] = jnp.zeros((width, BLOCK), f32)
    less[slots] = jnp.zeros((width, BLOCK), f32)
    for b in range(blocks):
        columns = slice(b * BLOCK, (b + 1) * BLOCK)
        slot = index[b]
        solution[:, columns] = combine(gives, smooth, b, 0) + extra[slot]
        residual[:, columns] = gradient[:, columns] - combine(takes, plain, b, 0) - less[slot]


def on_device(
    gradient,
    width_factor,
    diag_blocks,
    jacobi_inverse,
    coupling_tiles,
    tile_local,
    tile_remote,
    tile_count,
    exchange=False,
):
    width, rows = gradient.shape
    blocks = diag_blocks.shape[0]
    columns = lax.axis_size("cols")
    devices = lax.axis_size("rows")
    slots = tile_local.shape[0] - 1
    live = jnp.arange(slots, dtype=jnp.int32) < tile_count[0]
    lists = (tile_local[:slots], tile_remote[:slots], live)

    numbers = jnp.arange(blocks, dtype=jnp.int32)
    gathered = devices * slots * BLOCK * (BLOCK + width) * 4
    if gathered <= GATHER_BYTES and devices % 2 == 0 and not exchange:
        chain, pieces = chain_gathered(
            gradient, width_factor, jacobi_inverse, coupling_tiles, tile_local, *lists
        )
        at = tile_local
        here = (lists[0][None, :] == numbers[:, None]) & live[None, :]
        order = jnp.arange(slots, dtype=jnp.int32)[None, :]
        index = jnp.min(jnp.where(here, order, slots), axis=1)
    else:
        chain = chain_exchanged(gradient, jacobi_inverse, coupling_tiles[:slots], *lists)
        pieces = whole_pieces(gradient, width_factor)
        at, index = numbers, numbers
    units = chain.shape[1]
    chains = [chain] + [shift(chain, "cols", o) for o in range(1, columns)]

    turn = (BLOCK - width * lax.axis_index("cols")) % BLOCK
    shape = jax.ShapeDtypeStruct
    count = ITERS * (ITERS + 1) // 2
    mixes, plain, smooth, scale = call(
        basis_kernel,
        (
            shape((count * width, BLOCK), f32),
            shape((blocks, (ITERS + 1) * width, BLOCK), f32),
            shape((blocks, ITERS * width, BLOCK), f32),
            shape((8, BLOCK), f32),
        ),
        turn.astype(jnp.int32).reshape(1),
        *pieces,
        jacobi_inverse,
        scalars=1,
    )
    added, smoothed, gram = call(
        mix_kernel,
        (
            shape((units + 1, ITERS * width, BLOCK), f32),
            shape((units + 1, (ITERS - 1) * width, BLOCK), f32),
            shape((1, BLOCK), f32),
        ),
        at,
        index,
        *chains,
        gradient,
        mixes,
        plain,
        smooth,
        jacobi_inverse,
        scalars=2,
    )
    everyone = columns * devices
    grams = lax.all_to_all(
        jnp.broadcast_to(gram[None], (everyone, 1, BLOCK)),
        ("cols", "rows"),
        0,
        0,
        tiled=True,
    )
    return call(
        finish_kernel,
        (shape((width, rows), f32), shape((width, rows), f32)),
        index,
        grams,
        scale,
        gradient,
        plain,
        smooth,
        added,
        smoothed,
        scalars=1,
        scratch=[pltpu.VMEM((units + 1, width, BLOCK), f32)] * 2,
    )


def solution(mesh):
    placed = (
        P("cols", "rows"),
        P(None, "cols"),
        P("rows", None, None),
        P("rows", None, None),
        P("rows", None, None),
        P("rows"),
        P("rows"),
        P("rows"),
    )

    return jax.shard_map(
        on_device,
        mesh=mesh,
        in_specs=placed,
        out_specs=(P("cols", "rows"), P("cols", "rows")),
        check_vma=False,
    )
```

```python
import jax
import jax.numpy as jnp
from jax import lax
from jax.experimental import pallas as pl
from jax.experimental.pallas import tpu as pltpu
from jax.sharding import PartitionSpec as P


BLOCK = 128
ITERS = 6
STRETCH = 1.1
GATHER_BYTES = 8 * 2**20


GRANT_BYTES = 24 * 2**20
WHOLE_BYTES = 60 * 2**20

highest = lax.Precision.HIGHEST
f32 = jnp.float32
VMEM = pl.BlockSpec(memory_space=pltpu.VMEM)
SMEM = pl.BlockSpec(memory_space=pltpu.SMEM)


def dot(a, b):
    return jnp.dot(a, b, precision=highest, preferred_element_type=f32)


def call(kernel, outs, *args, scalars=0, scratch=(), place=VMEM, grant=GRANT_BYTES):
    specs = [SMEM] * scalars + [place] * (len(args) - scalars)
    many = isinstance(outs, tuple)
    return pl.pallas_call(
        kernel,
        out_shape=outs,
        in_specs=specs,
        out_specs=tuple([VMEM] * len(outs)) if many else VMEM,
        scratch_shapes=list(scratch),
        compiler_params=pltpu.CompilerParams(vmem_limit_bytes=grant),
    )(*args)


def split(x):
    high = x.astype(jnp.bfloat16)
    return high, (x - high.astype(f32)).astype(jnp.bfloat16)


def plain_dot(a, b):
    return jnp.dot(a, b, preferred_element_type=f32)


def dot3(a, b):
    tall = a.shape[0]
    high, low = split(a)
    right, rest = split(b)
    both = plain_dot(jnp.concatenate([high, low], 0), right)
    return both[:tall] + (both[tall:] + plain_dot(high, rest))


def pack_kernel(local, gradient, jacobi, tiles, packed, inverse, coupling, part, done):
    slots = packed.shape[0]
    contract = (((1,), (1,)), ((), ()))
    copies = []
    for slot in range(slots):
        block = local[slot]
        columns = pl.ds(pl.multiple_of(block * BLOCK, BLOCK), BLOCK)
        moves = [
            (jacobi.at[block], inverse.at[slot]),
            (tiles.at[slot], coupling.at[slot]),
            (gradient.at[:, columns], part.at[slot]),
        ]
        for i, (source, target) in enumerate(moves):
            copy = pltpu.make_async_copy(source, target, done.at[slot, i])
            copy.start()
            copies.append(copy)
    for slot in range(slots):
        for copy in copies[3 * slot : 3 * slot + 3]:
            copy.wait()
        halves = jnp.concatenate(split(inverse[slot]), 0)
        both = lax.dot_general(halves, coupling[slot], contract, preferred_element_type=f32)
        packed[slot, :BLOCK, :] = both[:BLOCK] + both[BLOCK:]
        packed[slot, BLOCK:, :] = part[slot]


def advance(sources, high, low, held, out, chain):
    total, width = held.shape[:2]
    steps, slots = chain.shape[:2]
    out[total] = jnp.zeros((width, BLOCK), f32)

    def step(j, carry):
        for q in range(total):
            first, second = split(held[q])
            both = plain_dot(jnp.concatenate([first, second], 0), high[q])
            out[q] = both[:width] + both[width:] + plain_dot(first, low[q])
        for q in range(total):
            value = out[sources[q * slots]]
            for i in range(1, slots):
                value += out[sources[q * slots + i]]
            held[q] = value
        for slot in range(slots):
            chain[j, slot] = held[slot]
        return carry

    lax.fori_loop(0, steps, step, 0)


def begin_kernel(sources, near, far, chain, high, low, held, out):
    groups, slots = near.shape[:2]
    half = groups * slots
    for q in range(2 * half):
        ref = near if q < half else far
        group, slot = divmod(q % half, slots)
        high[q], low[q] = split(ref[group, slot, :BLOCK, :])
        held[q] = ref[group, slot, BLOCK:, :]
    advance(sources, high, low, held, out, chain)


def go_on_kernel(sources, high, low, start, chain, held, out):
    held[...] = start[...]
    advance(sources, high, low, held, out, chain)


def shift(x, axis, by):
    size = lax.axis_size(axis)
    return lax.ppermute(x, axis, [(i, (i - by) % size) for i in range(size)])


def whole_pieces(gradient, factor):
    piece = jnp.concatenate([gradient, factor.T], axis=1)
    others = range(1, lax.axis_size("cols"))
    return [piece] + [shift(piece, "cols", o) for o in others]


def chain_gathered(gradient, factor, jacobi, tiles, whole_local, local, remote, live):
    width = gradient.shape[0]
    blocks, slots = jacobi.shape[0], local.shape[0]
    devices = lax.axis_size("rows")
    groups = devices // 2
    packed = call(
        pack_kernel,
        jax.ShapeDtypeStruct((slots, BLOCK + width, BLOCK), f32),
        whole_local,
        gradient,
        jacobi,
        tiles,
        scalars=1,
        scratch=[
            pltpu.VMEM((slots, BLOCK, BLOCK), f32),
            pltpu.VMEM((slots, BLOCK, BLOCK), tiles.dtype),
            pltpu.VMEM((slots, width, BLOCK), f32),
            pltpu.SemaphoreType.DMA((slots, 3)),
        ],
        place=pl.BlockSpec(memory_space=pl.ANY),
        grant=WHOLE_BYTES,
    )
    near = [packed] + [shift(packed, "rows", 2 * o) for o in range(1, groups)]
    gradient, factor, _ = lax.optimization_barrier((gradient, factor, packed))
    pieces = whole_pieces(gradient, factor)
    own = jnp.concatenate([local, remote, live.astype(jnp.int32)])
    own = jnp.pad(own, (0, BLOCK - own.shape[0]))
    told = jnp.broadcast_to(own[None, None, :], (devices, 1, BLOCK))
    told = lax.all_to_all(told, "rows", 0, 0, tiled=True)[:, 0]
    near, pieces, told = lax.optimization_barrier((near, pieces, told))
    near = jnp.stack(near)
    far = lax.ppermute(near, "rows", [(i, i ^ 1) for i in range(devices)])

    me = lax.axis_index("rows")
    position = jnp.arange(devices, dtype=jnp.int32)
    base = me ^ (position // groups)
    device = (base + 2 * (position % groups)) % devices
    pick = (device[:, None] == jnp.arange(devices, dtype=jnp.int32)[None, :]).astype(jnp.int32)
    told = jnp.sum(pick[:, :, None] * told[None, :, :], axis=1)
    locals_, remotes, lives = (
        told[:, i * slots : (i + 1) * slots] for i in range(3)
    )
    owner = (remotes // blocks).reshape(-1)
    holder = jnp.broadcast_to(device[:, None], locals_.shape).reshape(-1)
    alive = lives.reshape(-1) > 0
    meets = (
        (owner[:, None] == holder[None, :])
        & (owner[None, :] == holder[:, None])
        & alive[None, :]
    )
    total = devices * slots
    numbers = jnp.arange(total, dtype=jnp.int32)
    partner = jnp.sum(jnp.where(meets, numbers[None, :], 0), axis=1).reshape(devices, slots)
    same = (
        (locals_[:, :, None] == locals_[:, None, :])
        & (lives[:, None, :] > 0)
        & (lives[:, :, None] > 0)
    )
    sources = jnp.where(same, partner[:, None, :], total).reshape(-1)
    early = ITERS - ITERS // 3
    shape = jax.ShapeDtypeStruct
    operators = shape((total, BLOCK, BLOCK), jnp.bfloat16)
    spare = pltpu.VMEM((total + 1, width, BLOCK), f32)
    chain, high, low, held = call(
        begin_kernel,
        (
            shape((early, slots, width, BLOCK), f32),
            operators,
            operators,
            shape((total, width, BLOCK), f32),
        ),
        sources,
        near,
        far,
        scalars=1,
        scratch=[spare],
    )
    later = call(
        go_on_kernel,
        shape((ITERS - early, slots, width, BLOCK), f32),
        sources,
        high,
        low,
        held,
        scalars=1,
        scratch=[pltpu.VMEM((total, width, BLOCK), f32), spare],
    )
    return [chain, later], pieces


def chain_exchanged(gradient, jacobi, tiles, local, remote, live):
    width = gradient.shape[0]
    blocks = jacobi.shape[0]
    devices = lax.axis_size("rows")
    owner = remote // blocks
    placing = (
        (local[:, None] == jnp.arange(blocks, dtype=jnp.int32)[None, :]) & live[:, None]
    ).astype(f32)
    meets = live[:, None] & (owner[:, None] == jnp.arange(devices, dtype=jnp.int32)[None, :])
    granted = jnp.sum(jnp.where(meets, local[:, None], 0), axis=0)
    vector = jnp.transpose(gradient.reshape(width, blocks, BLOCK), (1, 0, 2))
    steps = []
    for _ in range(ITERS):
        sent = jnp.einsum("nej,nji->nei", vector, jacobi, precision=highest)[granted]
        incoming = lax.all_to_all(sent, "rows", 0, 0, tiled=True)
        products = jnp.einsum(
            "kej,kji->kei", incoming[owner], tiles.astype(f32), precision=highest
        )
        vector = jnp.einsum("kei,kn->nei", products, placing, precision=highest)
        steps.append(vector)
    return [jnp.stack(steps)]


def basis_kernel(turn, *refs):
    devices = len(refs) - 5
    pieces, jacobi = refs[:devices], refs[devices]
    mixes, plain, smooth, scale = refs[devices + 1 :]
    width = pieces[0].shape[0]
    blocks = jacobi.shape[0]
    rows = blocks * BLOCK
    factor = jnp.concatenate([piece[:, rows:] for piece in pieces], 0)
    factor = pltpu.roll(factor, turn[0], 1)
    norm = jnp.max(jnp.sum(jnp.abs(factor), axis=1, keepdims=True), axis=0, keepdims=True)
    power = factor / norm
    for _ in range(3):
        power = dot(power, power)
    bound = jnp.sum(jnp.sum(power * power, axis=1, keepdims=True), axis=0, keepdims=True)
    for _ in range(4):
        bound = jnp.sqrt(bound)
    ratio = 2.0 / (STRETCH * bound * norm)
    scale[...] = jnp.broadcast_to(ratio, scale.shape)
    factor = factor * ratio

    row = lax.broadcasted_iota(jnp.int32, (width, BLOCK), 0)
    lane = lax.broadcasted_iota(jnp.int32, (width, BLOCK), 1)
    kept = [[(row == lane).astype(f32)]]
    for k in range(ITERS):
        last = kept[k]
        terms = [last[0]] + [last[j] + last[j - 1] for j in range(1, k + 1)] + [last[k]]
        image = dot(jnp.concatenate(terms, 0), factor)
        fresh = []
        for j in range(k + 2):
            value = image[j * width : (j + 1) * width]
            if j <= k:
                value = value - last[j]
            if k:
                value = 2.0 * value
                if j <= k - 1:
                    value = value - kept[k - 1][j]
            fresh.append(value)
        kept.append(fresh)
    at = 0
    for j in range(1, ITERS + 1):
        for k in range(j, ITERS + 1):
            mixes[at : at + width, :] = kept[k][j]
            at += width
    first = jnp.concatenate([kept[k][0] for k in range(ITERS + 1)], 0)
    for b in range(blocks):
        columns = slice(b * BLOCK, (b + 1) * BLOCK)
        whole = jnp.concatenate([piece[:, columns] for piece in pieces], 0)
        value = dot(first, whole)
        plain[b] = value
        smooth[b] = dot(value[: ITERS * width], jacobi[b])


def make_basis(pieces, jacobi):
    width = pieces[0].shape[0]
    blocks = jacobi.shape[0]
    shape = jax.ShapeDtypeStruct
    count = ITERS * (ITERS + 1) // 2
    turn = (BLOCK - width * lax.axis_index("cols")) % BLOCK
    return call(
        basis_kernel,
        (
            shape((count * width, BLOCK), f32),
            shape((blocks, (ITERS + 1) * width, BLOCK), f32),
            shape((blocks, ITERS * width, BLOCK), f32),
            shape((8, BLOCK), f32),
        ),
        turn.astype(jnp.int32).reshape(1),
        *pieces,
        jacobi,
        scalars=1,
    )


def mix_kernel(local, index, *refs):
    parts = len(refs) - 8
    chains = refs[:parts]
    gradient, mixes, plain, smooth, jacobi = refs[parts : parts + 5]
    added, smoothed, gram = refs[parts + 5 :]
    slots, width = chains[0].shape[1:3]
    devices = BLOCK // width
    steps = []
    for part in range(0, parts, devices):
        for j in range(chains[part].shape[0]):
            steps.append([(chain, j) for chain in chains[part : part + devices]])
    blocks = jacobi.shape[0]
    short = (ITERS - 1) * width
    totals = [0.0] * ITERS
    at = 0
    for j in range(1, ITERS + 1):
        count = (ITERS + 1 - j) * width
        whole = jnp.concatenate(
            [
                jnp.concatenate([chain[i, slot] for chain, i in steps[j - 1]], 0)
                for slot in range(slots)
            ],
            1,
        )
        part = dot3(mixes[at : at + count, :], whole)
        at += count
        for k in range(j, ITERS + 1):
            totals[k - 1] += part[(k - j) * width : (k - j + 1) * width]
    for slot in range(slots):
        columns = slice(slot * BLOCK, (slot + 1) * BLOCK)
        value = jnp.concatenate([total[:, columns] for total in totals], 0)
        added[slot] = value
        smoothed[slot] = dot3(value[:short], jacobi[local[slot]])
    added[slots] = jnp.zeros(added.shape[1:], f32)
    smoothed[slots] = jnp.zeros(smoothed.shape[1:], f32)

    sums = {}
    for b in range(blocks):
        slot = index[b]
        for r in range(0, width, 8):
            s = [plain[b, k * width + r : k * width + r + 8, :] for k in range(ITERS + 1)]
            y = [smooth[b, k * width + r : k * width + r + 8, :] for k in range(ITERS)]
            for k in range(1, ITERS + 1):
                rows = slice((k - 1) * width + r, (k - 1) * width + r + 8)
                s[k] = s[k] + added[slot, rows, :]
                if k < ITERS:
                    y[k] = y[k] + smoothed[slot, rows, :]
            g = gradient[r : r + 8, b * BLOCK : (b + 1) * BLOCK]
            f = [s[0] + s[1]]
            for j in range(1, ITERS):
                f.append(0.5 * (s[j - 1] + s[j + 1]) + s[j])
            for i in range(ITERS):
                for j in range(i + 1):
                    sums[i, j] = sums.get((i, j), 0.0) + y[i] * f[j]
                sums[i, ITERS] = sums.get((i, ITERS), 0.0) + y[i] * g
    lane = lax.broadcasted_iota(jnp.int32, (1, BLOCK), 1)
    result = jnp.zeros((1, BLOCK), f32)
    for (i, j), value in sums.items():
        value = jnp.sum(jnp.sum(value, axis=0, keepdims=True), axis=1, keepdims=True)
        here = lane == 16 * i + j
        if j < ITERS:
            here = here | (lane == 16 * j + i)
        result = jnp.where(here, value, result)
    gram[...] = result


def finish_kernel(
    index, grams, scale, gradient, plain, smooth, added, smoothed, solution, residual, extra, less
):
    width = gradient.shape[0]
    blocks = plain.shape[0]
    slots = added.shape[0] - 1
    flat = jnp.sum(grams[:, 0, :], axis=0, keepdims=True)
    row = lax.broadcasted_iota(jnp.int32, (8, BLOCK), 0)
    lane = lax.broadcasted_iota(jnp.int32, (8, BLOCK), 1)
    table = jnp.zeros((8, BLOCK), f32)
    for i in range(ITERS):
        moved = flat if i == 0 else pltpu.roll(flat, BLOCK - 16 * i, 1)
        table = jnp.where((row == i) & (lane <= ITERS), moved, table)
    for p in range(ITERS):
        pivot = table[p : p + 1, :] / table[p : p + 1, p : p + 1]
        table = jnp.where(row == p, pivot, table - table[:, p : p + 1] * pivot)
    steps = [table[j : j + 1, ITERS : ITERS + 1] for j in range(ITERS)]
    takes = []
    for k in range(ITERS + 1):
        value = 0.0
        if k > 0:
            value += steps[k - 1] * (1.0 if k == 1 else 0.5)
        if k < ITERS:
            value += steps[k]
        if k + 1 < ITERS:
            value += 0.5 * steps[k + 1]
        takes.append(jnp.broadcast_to(value, (width, BLOCK)))
    longer = scale[0:1, 0:1]
    gives = [jnp.broadcast_to(longer * step, (width, BLOCK)) for step in steps]

    def combine(weights, ref, b, start):
        total = None
        for j, weight in enumerate(weights):
            term = weight * ref[b, (start + j) * width : (start + j + 1) * width, :]
            total = term if total is None else total + term
        return total

    for slot in range(slots):
        extra[slot] = combine(gives[1:], smoothed, slot, 0)
        less[slot] = combine(takes[1:], added, slot, 0)
    extra[slots] = jnp.zeros((width, BLOCK), f32)
    less[slots] = jnp.zeros((width, BLOCK), f32)
    for b in range(blocks):
        columns = slice(b * BLOCK, (b + 1) * BLOCK)
        slot = index[b]
        solution[:, columns] = combine(gives, smooth, b, 0) + extra[slot]
        residual[:, columns] = gradient[:, columns] - combine(takes, plain, b, 0) - less[slot]


def on_device(
    gradient,
    width_factor,
    diag_blocks,
    jacobi_inverse,
    coupling_tiles,
    tile_local,
    tile_remote,
    tile_count,
    exchange=False,
):
    width, rows = gradient.shape
    blocks = diag_blocks.shape[0]
    columns = lax.axis_size("cols")
    devices = lax.axis_size("rows")
    slots = tile_local.shape[0] - 1
    live = jnp.arange(slots, dtype=jnp.int32) < tile_count[0]
    lists = (tile_local[:slots], tile_remote[:slots], live)

    numbers = jnp.arange(blocks, dtype=jnp.int32)
    gathered = devices * slots * BLOCK * (BLOCK + width) * 4
    if gathered <= GATHER_BYTES and devices % 2 == 0 and not exchange:
        chains, pieces = chain_gathered(
            gradient, width_factor, jacobi_inverse, coupling_tiles, tile_local, *lists
        )
        at = tile_local
        here = (lists[0][None, :] == numbers[:, None]) & live[None, :]
        order = jnp.arange(slots, dtype=jnp.int32)[None, :]
        index = jnp.min(jnp.where(here, order, slots), axis=1)
    else:
        chains = chain_exchanged(gradient, jacobi_inverse, coupling_tiles[:slots], *lists)
        pieces = whole_pieces(gradient, width_factor)
        at, index = numbers, numbers
    mixes, plain, smooth, scale = make_basis(pieces, jacobi_inverse)
    units = chains[0].shape[1]
    parts = []
    for chain in chains:
        others = range(1, columns)
        parts += [chain] + [shift(chain, "cols", o) for o in others]

    shape = jax.ShapeDtypeStruct
    added, smoothed, gram = call(
        mix_kernel,
        (
            shape((units + 1, ITERS * width, BLOCK), f32),
            shape((units + 1, (ITERS - 1) * width, BLOCK), f32),
            shape((1, BLOCK), f32),
        ),
        at,
        index,
        *parts,
        gradient,
        mixes,
        plain,
        smooth,
        jacobi_inverse,
        scalars=2,
    )
    everyone = columns * devices
    grams = lax.all_to_all(
        jnp.broadcast_to(gram[None], (everyone, 1, BLOCK)),
        ("cols", "rows"),
        0,
        0,
        tiled=True,
    )
    return call(
        finish_kernel,
        (shape((width, rows), f32), shape((width, rows), f32)),
        index,
        grams,
        scale,
        gradient,
        plain,
        smooth,
        added,
        smoothed,
        scalars=1,
        scratch=[pltpu.VMEM((units + 1, width, BLOCK), f32)] * 2,
    )


def solution(mesh):
    placed = (
        P("cols", "rows"),
        P(None, "cols"),
        P("rows", None, None),
        P("rows", None, None),
        P("rows", None, None),
        P("rows"),
        P("rows"),
        P("rows"),
    )

    return jax.shard_map(
        on_device,
        mesh=mesh,
        in_specs=placed,
        out_specs=(P("cols", "rows"), P("cols", "rows")),
        check_vma=False,
    )
```

```python
import jax
import jax.numpy as jnp
from jax import lax
from jax.experimental import pallas as pl
from jax.experimental.pallas import tpu as pltpu
from jax.sharding import PartitionSpec as P


BLOCK = 128
ITERS = 6
STRETCH = 1.1
GATHER_BYTES = 8 * 2**20


GRANT_BYTES = 24 * 2**20
WHOLE_BYTES = 60 * 2**20

highest = lax.Precision.HIGHEST
f32 = jnp.float32
VMEM = pl.BlockSpec(memory_space=pltpu.VMEM)
SMEM = pl.BlockSpec(memory_space=pltpu.SMEM)


def dot(a, b):
    return jnp.dot(a, b, precision=highest, preferred_element_type=f32)


def call(kernel, outs, *args, scalars=0, scratch=(), place=VMEM, grant=GRANT_BYTES):
    specs = [SMEM] * scalars + [place] * (len(args) - scalars)
    many = isinstance(outs, tuple)
    return pl.pallas_call(
        kernel,
        out_shape=outs,
        in_specs=specs,
        out_specs=tuple([VMEM] * len(outs)) if many else VMEM,
        scratch_shapes=list(scratch),
        compiler_params=pltpu.CompilerParams(vmem_limit_bytes=grant),
    )(*args)


def split(x):
    high = x.astype(jnp.bfloat16)
    return high, (x - high.astype(f32)).astype(jnp.bfloat16)


def plain_dot(a, b):
    return jnp.dot(a, b, preferred_element_type=f32)


def dot3(a, b):
    tall = a.shape[0]
    high, low = split(a)
    right, rest = split(b)
    both = plain_dot(jnp.concatenate([high, low], 0), right)
    return both[:tall] + (both[tall:] + plain_dot(high, rest))


def pack_kernel(local, gradient, jacobi, tiles, packed, inverse, coupling, part, done):
    slots = packed.shape[0]
    contract = (((1,), (1,)), ((), ()))
    copies = []
    for slot in range(slots):
        block = local[slot]
        columns = pl.ds(pl.multiple_of(block * BLOCK, BLOCK), BLOCK)
        moves = [
            (jacobi.at[block], inverse.at[slot]),
            (tiles.at[slot], coupling.at[slot]),
            (gradient.at[:, columns], part.at[slot]),
        ]
        for i, (source, target) in enumerate(moves):
            copy = pltpu.make_async_copy(source, target, done.at[slot, i])
            copy.start()
            copies.append(copy)
    for slot in range(slots):
        for copy in copies[3 * slot : 3 * slot + 3]:
            copy.wait()
        halves = jnp.concatenate(split(inverse[slot]), 0)
        both = lax.dot_general(halves, coupling[slot], contract, preferred_element_type=f32)
        packed[slot, :BLOCK, :] = both[:BLOCK] + both[BLOCK:]
        packed[slot, BLOCK:, :] = part[slot]


def chain_kernel(sources, give, near, far, *refs):
    sends, (high, low, held, out) = refs[:-4], refs[-4:]
    groups, slots = near.shape[:2]
    half = groups * slots
    total = 2 * half
    width = held.shape[1]
    share = sends[0].shape[1]
    for q in range(total):
        ref = near if q < half else far
        group, slot = divmod(q % half, slots)
        high[q], low[q] = split(ref[group, slot, :BLOCK, :])
        held[q] = ref[group, slot, BLOCK:, :]
    held[total] = jnp.zeros((width, BLOCK), f32)
    out[total] = jnp.zeros((width, BLOCK), f32)

    def step(j, carry):
        for q in range(total):
            first, second = split(held[q])
            both = plain_dot(jnp.concatenate([first, second], 0), high[q])
            out[q] = both[:width] + both[width:] + plain_dot(first, low[q])
        for q in range(total):
            value = out[sources[q * slots]]
            for i in range(1, slots):
                value += out[sources[q * slots + i]]
            held[q] = value
        for o, send in enumerate(sends):
            for p in range(share):
                send[j, p] = held[give[o * share + p]]
        return carry

    lax.fori_loop(0, ITERS, step, 0)


def shift(x, axis, by):
    size = lax.axis_size(axis)
    return lax.ppermute(x, axis, [(i, (i - by) % size) for i in range(size)])


def whole_pieces(gradient, factor):
    piece = jnp.concatenate([gradient, factor.T], axis=1)
    others = range(1, lax.axis_size("cols"))
    return [piece] + [shift(piece, "cols", o) for o in others]


def chain_gathered(gradient, factor, jacobi, tiles, whole_local, order, local, remote, live):
    width = gradient.shape[0]
    blocks, slots = jacobi.shape[0], local.shape[0]
    devices = lax.axis_size("rows")
    columns = lax.axis_size("cols")
    groups = devices // 2
    packed = call(
        pack_kernel,
        jax.ShapeDtypeStruct((slots, BLOCK + width, BLOCK), f32),
        whole_local,
        gradient,
        jacobi,
        tiles,
        scalars=1,
        scratch=[
            pltpu.VMEM((slots, BLOCK, BLOCK), f32),
            pltpu.VMEM((slots, BLOCK, BLOCK), tiles.dtype),
            pltpu.VMEM((slots, width, BLOCK), f32),
            pltpu.SemaphoreType.DMA((slots, 3)),
        ],
        place=pl.BlockSpec(memory_space=pl.ANY),
        grant=WHOLE_BYTES,
    )
    near = [packed] + [shift(packed, "rows", 2 * o) for o in range(1, groups)]
    gradient, factor, _ = lax.optimization_barrier((gradient, factor, packed))
    pieces = whole_pieces(gradient, factor)
    own = jnp.concatenate([local, remote, live.astype(jnp.int32)])
    own = jnp.pad(own, (0, BLOCK - own.shape[0]))
    told = jnp.broadcast_to(own[None, None, :], (devices, 1, BLOCK))
    told = lax.all_to_all(told, "rows", 0, 0, tiled=True)[:, 0]
    near, pieces, told = lax.optimization_barrier((near, pieces, told))
    near = jnp.stack(near)
    far = lax.ppermute(near, "rows", [(i, i ^ 1) for i in range(devices)])

    me = lax.axis_index("rows")
    position = jnp.arange(devices, dtype=jnp.int32)
    base = me ^ (position // groups)
    device = (base + 2 * (position % groups)) % devices
    pick = (device[:, None] == jnp.arange(devices, dtype=jnp.int32)[None, :]).astype(jnp.int32)
    told = jnp.sum(pick[:, :, None] * told[None, :, :], axis=1)
    locals_, remotes, lives = (
        told[:, i * slots : (i + 1) * slots] for i in range(3)
    )
    owner = (remotes // blocks).reshape(-1)
    holder = jnp.broadcast_to(device[:, None], locals_.shape).reshape(-1)
    alive = lives.reshape(-1) > 0
    meets = (
        (owner[:, None] == holder[None, :])
        & (owner[None, :] == holder[:, None])
        & alive[None, :]
    )
    total = devices * slots
    numbers = jnp.arange(total, dtype=jnp.int32)
    partner = jnp.sum(jnp.where(meets, numbers[None, :], 0), axis=1).reshape(devices, slots)
    same = (
        (locals_[:, :, None] == locals_[:, None, :])
        & (lives[:, None, :] > 0)
        & (lives[:, :, None] > 0)
    )
    sources = jnp.where(same, partner[:, None, :], total).reshape(-1)
    share = order.shape[0] // columns
    shape = jax.ShapeDtypeStruct
    sends = call(
        chain_kernel,
        tuple([shape((ITERS, share, width, BLOCK), f32)] * columns),
        sources,
        jnp.where(order < slots, order, total),
        near,
        far,
        scalars=2,
        scratch=[
            pltpu.VMEM((total, BLOCK, BLOCK), jnp.bfloat16),
            pltpu.VMEM((total, BLOCK, BLOCK), jnp.bfloat16),
            pltpu.VMEM((total + 1, width, BLOCK), f32),
            pltpu.VMEM((total + 1, width, BLOCK), f32),
        ],
    )
    return list(sends), pieces


def chain_exchanged(gradient, jacobi, tiles, order, local, remote, live):
    width = gradient.shape[0]
    blocks = jacobi.shape[0]
    devices = lax.axis_size("rows")
    owner = remote // blocks
    placing = (
        (local[:, None] == jnp.arange(blocks, dtype=jnp.int32)[None, :]) & live[:, None]
    ).astype(f32)
    meets = live[:, None] & (owner[:, None] == jnp.arange(devices, dtype=jnp.int32)[None, :])
    granted = jnp.sum(jnp.where(meets, local[:, None], 0), axis=0)
    vector = jnp.transpose(gradient.reshape(width, blocks, BLOCK), (1, 0, 2))
    steps = []
    for _ in range(ITERS):
        sent = jnp.einsum("nej,nji->nei", vector, jacobi, precision=highest)[granted]
        incoming = lax.all_to_all(sent, "rows", 0, 0, tiled=True)
        products = jnp.einsum(
            "kej,kji->kei", incoming[owner], tiles.astype(f32), precision=highest
        )
        vector = jnp.einsum("kei,kn->nei", products, placing, precision=highest)
        steps.append(vector)
    columns = lax.axis_size("cols")
    share = order.shape[0] // columns
    chain = jnp.pad(jnp.stack(steps), ((0, 0), (0, share * columns - blocks), (0, 0), (0, 0)))
    return [
        lax.dynamic_slice_in_dim(chain, order[o * share], share, 1) for o in range(columns)
    ]


def basis_kernel(turn, *refs):
    devices = len(refs) - 5
    pieces, jacobi = refs[:devices], refs[devices]
    scaled, plain, smooth, scale = refs[devices + 1 :]
    width = pieces[0].shape[0]
    blocks = jacobi.shape[0]
    rows = blocks * BLOCK
    factor = jnp.concatenate([piece[:, rows:] for piece in pieces], 0)
    factor = pltpu.roll(factor, turn[0], 1)
    norm = jnp.max(jnp.sum(jnp.abs(factor), axis=1, keepdims=True), axis=0, keepdims=True)
    power = factor / norm
    for _ in range(3):
        power = dot(power, power)
    bound = jnp.sum(jnp.sum(power * power, axis=1, keepdims=True), axis=0, keepdims=True)
    for _ in range(4):
        bound = jnp.sqrt(bound)
    ratio = 2.0 / (STRETCH * bound * norm)
    scale[...] = jnp.broadcast_to(ratio, scale.shape)
    factor = factor * ratio
    scaled[...] = factor

    row = lax.broadcasted_iota(jnp.int32, (width, BLOCK), 0)
    lane = lax.broadcasted_iota(jnp.int32, (width, BLOCK), 1)
    kept = [(row == lane).astype(f32)]
    for k in range(ITERS):
        value = dot(kept[k], factor) - kept[k]
        kept.append(2.0 * value - kept[k - 1] if k else value)
    first = jnp.concatenate(kept, 0)
    for b in range(blocks):
        columns = slice(b * BLOCK, (b + 1) * BLOCK)
        whole = jnp.concatenate([piece[:, columns] for piece in pieces], 0)
        value = dot(first, whole)
        plain[b] = value
        smooth[b] = dot(value[: ITERS * width], jacobi[b])


def make_basis(pieces, jacobi):
    width = pieces[0].shape[0]
    blocks = jacobi.shape[0]
    shape = jax.ShapeDtypeStruct
    turn = (BLOCK - width * lax.axis_index("cols")) % BLOCK
    return call(
        basis_kernel,
        (
            shape((BLOCK, BLOCK), f32),
            shape((blocks, (ITERS + 1) * width, BLOCK), f32),
            shape((blocks, ITERS * width, BLOCK), f32),
            shape((8, BLOCK), f32),
        ),
        turn.astype(jnp.int32).reshape(1),
        *pieces,
        jacobi,
        scalars=1,
    )


def mix_kernel(held, used, where, *refs):
    devices = (len(refs) - 5) // 3
    parts, pieces = refs[:devices], refs[devices : 2 * devices]
    scaled, jacobi, plain, smooth = refs[2 * devices : 2 * devices + 4]
    gram, backs = refs[2 * devices + 4], refs[2 * devices + 5 :]
    share, width = parts[0].shape[1:3]
    blocks = jacobi.shape[0]
    none = devices * share
    sums = {}

    def gather(s, y, weight):
        y = [weight * value for value in y]
        f = [s[0] + s[1]]
        for j in range(1, ITERS):
            f.append(0.5 * (s[j - 1] + s[j + 1]) + s[j])
        for i in range(ITERS):
            for j in range(i + 1):
                sums[i, j] = sums.get((i, j), 0.0) + y[i] * f[j]
            sums[i, ITERS] = sums.get((i, ITERS), 0.0) + y[i] * s[0]

    for p in range(share):
        block = held[p]
        columns = pl.ds(pl.multiple_of(block * BLOCK, BLOCK), BLOCK)
        now = [jnp.concatenate([piece[:, columns] for piece in pieces], 0)]
        for j in range(ITERS):
            now.append(jnp.concatenate([part[j, p] for part in parts], 0))
        past = None
        chosen = [now[0]]
        for k in range(ITERS):
            left = ITERS - k
            image = dot3(
                scaled[...], jnp.concatenate([now[i] + now[i + 1] for i in range(left)], 1)
            )
            fresh = []
            for i in range(left):
                value = image[:, i * BLOCK : (i + 1) * BLOCK] - now[i]
                fresh.append(2.0 * value - past[i] if k else value)
            past, now = now, fresh
            chosen.append(now[0])
        for o, back in enumerate(backs):
            for k in range(ITERS):
                back[k, p] = chosen[k + 1][o * width : (o + 1) * width]
        soft = dot3(jnp.concatenate(chosen[:ITERS], 0), jacobi[block])
        weight = jnp.where(used[p] > 0, 1.0, 0.0)
        for r in range(0, BLOCK, 8):
            gather(
                [value[r : r + 8] for value in chosen],
                [soft[k * BLOCK + r : k * BLOCK + r + 8] for k in range(ITERS)],
                weight,
            )
    for b in range(blocks):
        weight = jnp.where(where[b] < none, 0.0, 1.0)
        for r in range(0, width, 8):
            gather(
                [plain[b, k * width + r : k * width + r + 8, :] for k in range(ITERS + 1)],
                [smooth[b, k * width + r : k * width + r + 8, :] for k in range(ITERS)],
                weight,
            )
    lane = lax.broadcasted_iota(jnp.int32, (1, BLOCK), 1)
    result = jnp.zeros((1, BLOCK), f32)
    for (i, j), value in sums.items():
        value = jnp.sum(jnp.sum(value, axis=0, keepdims=True), axis=1, keepdims=True)
        here = lane == 16 * i + j
        if j < ITERS:
            here = here | (lane == 16 * j + i)
        result = jnp.where(here, value, result)
    gram[...] = result


def finish_kernel(held, where, grams, scale, gradient, plain, smooth, jacobi, *refs):
    backs, (solution, residual, extra, less) = refs[:-4], refs[-4:]
    width = gradient.shape[0]
    blocks = plain.shape[0]
    share = backs[0].shape[1]
    none = len(backs) * share
    flat = jnp.sum(grams[:, 0, :], axis=0, keepdims=True)
    row = lax.broadcasted_iota(jnp.int32, (8, BLOCK), 0)
    lane = lax.broadcasted_iota(jnp.int32, (8, BLOCK), 1)
    table = jnp.zeros((8, BLOCK), f32)
    for i in range(ITERS):
        moved = flat if i == 0 else pltpu.roll(flat, BLOCK - 16 * i, 1)
        table = jnp.where((row == i) & (lane <= ITERS), moved, table)
    for p in range(ITERS):
        pivot = table[p : p + 1, :] / table[p : p + 1, p : p + 1]
        table = jnp.where(row == p, pivot, table - table[:, p : p + 1] * pivot)
    steps = [table[j : j + 1, ITERS : ITERS + 1] for j in range(ITERS)]
    takes = []
    for k in range(ITERS + 1):
        value = 0.0
        if k > 0:
            value += steps[k - 1] * (1.0 if k == 1 else 0.5)
        if k < ITERS:
            value += steps[k]
        if k + 1 < ITERS:
            value += 0.5 * steps[k + 1]
        takes.append(jnp.broadcast_to(value, (width, BLOCK)))
    longer = scale[0:1, 0:1]
    gives = [jnp.broadcast_to(longer * step, (width, BLOCK)) for step in steps]

    def combine(weights, ref, b, start):
        total = None
        for j, weight in enumerate(weights):
            term = weight * ref[b, (start + j) * width : (start + j + 1) * width, :]
            total = term if total is None else total + term
        return total

    for n in range(none):
        back = backs[n // share]
        total, left = 0.0, 0.0
        for k in range(ITERS):
            value = back[k, n % share]
            left = left + takes[k + 1] * value
            if k + 1 < ITERS:
                total = total + gives[k + 1] * value
        less[n] = left
        extra[n] = dot3(total, jacobi[held[n]])
    extra[none] = jnp.zeros((width, BLOCK), f32)
    less[none] = jnp.zeros((width, BLOCK), f32)
    for b in range(blocks):
        columns = slice(b * BLOCK, (b + 1) * BLOCK)
        n = where[b]
        own = n >= none
        rest = jnp.where(own, combine(gives[1:], smooth, b, 1), extra[n])
        solution[:, columns] = gives[0] * smooth[b, :width, :] + rest
        rest = jnp.where(own, combine(takes[1:], plain, b, 1), less[n])
        start = gradient[:, columns]
        residual[:, columns] = start - takes[0] * start - rest


def on_device(
    gradient,
    width_factor,
    diag_blocks,
    jacobi_inverse,
    coupling_tiles,
    tile_local,
    tile_remote,
    tile_count,
    exchange=False,
):
    width, rows = gradient.shape
    blocks = diag_blocks.shape[0]
    columns = lax.axis_size("cols")
    devices = lax.axis_size("rows")
    slots = tile_local.shape[0] - 1
    live = jnp.arange(slots, dtype=jnp.int32) < tile_count[0]
    lists = (tile_local[:slots], tile_remote[:slots], live)

    gathered = devices * slots * BLOCK * (BLOCK + width) * 4
    whole = gathered <= GATHER_BYTES and devices % 2 == 0 and not exchange
    units = slots if whole else blocks
    share = -(-units // columns)
    numbers = jnp.arange(columns * share, dtype=jnp.int32)
    dealer = (lax.axis_index("cols") + columns - numbers // share) % columns
    order = dealer * share + numbers % share
    if whole:
        sends, pieces = chain_gathered(
            gradient, width_factor, jacobi_inverse, coupling_tiles, tile_local, order, *lists
        )
        local = lists[0]
        earlier = jnp.arange(slots)[:, None] > jnp.arange(slots)[None, :]
        repeat = jnp.any(earlier & (local[:, None] == local[None, :]), axis=1)
        fit = order[:, None] == jnp.arange(slots, dtype=jnp.int32)[None, :]
        held = jnp.sum(jnp.where(fit, local[None, :], 0), axis=1)
        used = jnp.sum(jnp.where(fit & (live & ~repeat)[None, :], 1, 0), axis=1)
    else:
        sends = chain_exchanged(
            gradient, jacobi_inverse, coupling_tiles[:slots], order, *lists
        )
        pieces = whole_pieces(gradient, width_factor)
        held = jnp.minimum(order, blocks - 1)
        used = (order < blocks).astype(jnp.int32)
    mine = (held[None, :] == jnp.arange(blocks, dtype=jnp.int32)[:, None]) & (used > 0)[None, :]
    where = jnp.min(jnp.where(mine, numbers[None, :], columns * share), axis=1)
    parts = [sends[0]]
    for o in range(1, columns):
        parts.append(shift(sends[o], "cols", o))

    shape = jax.ShapeDtypeStruct
    scaled, plain, smooth, scale = make_basis(pieces, jacobi_inverse)
    gram, *backs = call(
        mix_kernel,
        tuple(
            [shape((1, BLOCK), f32)]
            + [shape((ITERS, share, width, BLOCK), f32)] * columns
        ),
        held,
        used,
        where,
        *parts,
        *pieces,
        scaled,
        jacobi_inverse,
        plain,
        smooth,
        scalars=3,
    )
    everyone = columns * devices
    grams = lax.all_to_all(
        jnp.broadcast_to(gram[None], (everyone, 1, BLOCK)),
        ("cols", "rows"),
        0,
        0,
        tiled=True,
    )
    for o in range(1, columns):
        backs[o] = shift(backs[o], "cols", -o)
    return call(
        finish_kernel,
        (shape((width, rows), f32), shape((width, rows), f32)),
        held,
        where,
        grams,
        scale,
        gradient,
        plain,
        smooth,
        jacobi_inverse,
        *backs,
        scalars=2,
        scratch=[pltpu.VMEM((columns * share + 1, width, BLOCK), f32)] * 2,
    )


def solution(mesh):
    placed = (
        P("cols", "rows"),
        P(None, "cols"),
        P("rows", None, None),
        P("rows", None, None),
        P("rows", None, None),
        P("rows"),
        P("rows"),
        P("rows"),
    )

    return jax.shard_map(
        on_device,
        mesh=mesh,
        in_specs=placed,
        out_specs=(P("cols", "rows"), P("cols", "rows")),
        check_vma=False,
    )
```

```python
import jax
import jax.numpy as jnp
from jax import lax
from jax.experimental import pallas as pl
from jax.experimental.pallas import tpu as pltpu
from jax.sharding import PartitionSpec as P


BLOCK = 128
ITERS = 6
STRETCH = 1.1
GATHER_BYTES = 8 * 2**20


NOWHERE = 2**20
GRANT_BYTES = 24 * 2**20
WHOLE_BYTES = 60 * 2**20

highest = lax.Precision.HIGHEST
f32 = jnp.float32
VMEM = pl.BlockSpec(memory_space=pltpu.VMEM)
SMEM = pl.BlockSpec(memory_space=pltpu.SMEM)


def dot(a, b):
    return jnp.dot(a, b, precision=highest, preferred_element_type=f32)


def call(kernel, outs, *args, scalars=0, scratch=(), place=VMEM, grant=GRANT_BYTES):
    specs = [SMEM] * scalars + [place] * (len(args) - scalars)
    many = isinstance(outs, tuple)
    return pl.pallas_call(
        kernel,
        out_shape=outs,
        in_specs=specs,
        out_specs=tuple([VMEM] * len(outs)) if many else VMEM,
        scratch_shapes=list(scratch),
        compiler_params=pltpu.CompilerParams(vmem_limit_bytes=grant),
    )(*args)


def split(x):
    high = x.astype(jnp.bfloat16)
    return high, (x - high.astype(f32)).astype(jnp.bfloat16)


def plain_dot(a, b):
    return jnp.dot(a, b, preferred_element_type=f32)


def dot3(a, b):
    tall = a.shape[0]
    high, low = split(a)
    right, rest = split(b)
    both = plain_dot(jnp.concatenate([high, low], 0), right)
    return both[:tall] + (both[tall:] + plain_dot(high, rest))


def pack_kernel(local, gradient, jacobi, tiles, packed, inverse, coupling, part, done):
    slots = packed.shape[0]
    contract = (((1,), (1,)), ((), ()))
    copies = []
    for slot in range(slots):
        block = local[slot]
        columns = pl.ds(pl.multiple_of(block * BLOCK, BLOCK), BLOCK)
        moves = [
            (jacobi.at[block], inverse.at[slot]),
            (tiles.at[slot], coupling.at[slot]),
            (gradient.at[:, columns], part.at[slot]),
        ]
        for i, (source, target) in enumerate(moves):
            copy = pltpu.make_async_copy(source, target, done.at[slot, i])
            copy.start()
            copies.append(copy)
    for slot in range(slots):
        for copy in copies[3 * slot : 3 * slot + 3]:
            copy.wait()
        halves = jnp.concatenate(split(inverse[slot]), 0)
        both = lax.dot_general(halves, coupling[slot], contract, preferred_element_type=f32)
        packed[slot, :BLOCK, :] = both[:BLOCK] + both[BLOCK:]
        packed[slot, BLOCK:, :] = part[slot]


def chain_kernel(sources, give, near, far, *refs):
    sends, (high, low, held, out) = refs[:-4], refs[-4:]
    groups, slots = near.shape[:2]
    half = groups * slots
    total = 2 * half
    width = held.shape[1]
    share = sends[0].shape[1]
    for q in range(total):
        ref = near if q < half else far
        group, slot = divmod(q % half, slots)
        high[q], low[q] = split(ref[group, slot, :BLOCK, :])
        held[q] = ref[group, slot, BLOCK:, :]
    held[total] = jnp.zeros((width, BLOCK), f32)
    out[total] = jnp.zeros((width, BLOCK), f32)

    def step(j, carry):
        for q in range(total):
            first, second = split(held[q])
            both = plain_dot(jnp.concatenate([first, second], 0), high[q])
            out[q] = both[:width] + both[width:] + plain_dot(first, low[q])
        for q in range(total):
            value = out[sources[q * slots]]
            for i in range(1, slots):
                value += out[sources[q * slots + i]]
            held[q] = value
        for o, send in enumerate(sends):
            for p in range(share):
                send[j, p] = held[give[o * share + p]]
        return carry

    lax.fori_loop(0, ITERS, step, 0)


def shift(x, axis, by):
    size = lax.axis_size(axis)
    return lax.ppermute(x, axis, [(i, (i - by) % size) for i in range(size)])


def whole_pieces(gradient, factor):
    piece = jnp.concatenate([gradient, factor.T], axis=1)
    others = range(1, lax.axis_size("cols"))
    return [piece] + [shift(piece, "cols", o) for o in others]


def chain_gathered(gradient, factor, jacobi, tiles, whole_local, order, where, local, remote, live):
    width = gradient.shape[0]
    blocks, slots = jacobi.shape[0], local.shape[0]
    devices = lax.axis_size("rows")
    columns = lax.axis_size("cols")
    groups = devices // 2
    packed = call(
        pack_kernel,
        jax.ShapeDtypeStruct((slots, BLOCK + width, BLOCK), f32),
        whole_local,
        gradient,
        jacobi,
        tiles,
        scalars=1,
        scratch=[
            pltpu.VMEM((slots, BLOCK, BLOCK), f32),
            pltpu.VMEM((slots, BLOCK, BLOCK), tiles.dtype),
            pltpu.VMEM((slots, width, BLOCK), f32),
            pltpu.SemaphoreType.DMA((slots, 3)),
        ],
        place=pl.BlockSpec(memory_space=pl.ANY),
        grant=WHOLE_BYTES,
    )
    near = [packed] + [shift(packed, "rows", 2 * o) for o in range(1, groups)]
    gradient, factor, _ = lax.optimization_barrier((gradient, factor, packed))
    pieces = whole_pieces(gradient, factor)
    own = jnp.concatenate([local, remote, live.astype(jnp.int32)])
    own = jnp.pad(own, (0, BLOCK - own.shape[0]))
    told = jnp.broadcast_to(own[None, None, :], (devices, 1, BLOCK))
    told = lax.all_to_all(told, "rows", 0, 0, tiled=True)
    told = told[:, 0]
    basis = make_basis(pieces, jacobi, where)
    near, basis, told = lax.optimization_barrier((near, basis, told))
    near = jnp.stack(near)
    far = lax.ppermute(near, "rows", [(i, i ^ 1) for i in range(devices)])

    me = lax.axis_index("rows")
    position = jnp.arange(devices, dtype=jnp.int32)
    base = me ^ (position // groups)
    device = (base + 2 * (position % groups)) % devices
    pick = (device[:, None] == jnp.arange(devices, dtype=jnp.int32)[None, :]).astype(jnp.int32)
    told = jnp.sum(pick[:, :, None] * told[None, :, :], axis=1)
    locals_, remotes, lives = (
        told[:, i * slots : (i + 1) * slots] for i in range(3)
    )
    owner = (remotes // blocks).reshape(-1)
    holder = jnp.broadcast_to(device[:, None], locals_.shape).reshape(-1)
    alive = lives.reshape(-1) > 0
    meets = (
        (owner[:, None] == holder[None, :])
        & (owner[None, :] == holder[:, None])
        & alive[None, :]
    )
    total = devices * slots
    numbers = jnp.arange(total, dtype=jnp.int32)
    partner = jnp.sum(jnp.where(meets, numbers[None, :], 0), axis=1).reshape(devices, slots)
    same = (
        (locals_[:, :, None] == locals_[:, None, :])
        & (lives[:, None, :] > 0)
        & (lives[:, :, None] > 0)
    )
    sources = jnp.where(same, partner[:, None, :], total).reshape(-1)
    share = order.shape[0] // columns
    shape = jax.ShapeDtypeStruct
    sends = call(
        chain_kernel,
        tuple([shape((ITERS, share, width, BLOCK), f32)] * columns),
        sources,
        jnp.where(order < slots, order, total),
        near,
        far,
        scalars=2,
        scratch=[
            pltpu.VMEM((total, BLOCK, BLOCK), jnp.bfloat16),
            pltpu.VMEM((total, BLOCK, BLOCK), jnp.bfloat16),
            pltpu.VMEM((total + 1, width, BLOCK), f32),
            pltpu.VMEM((total + 1, width, BLOCK), f32),
        ],
    )
    return list(sends), pieces, basis


def chain_exchanged(gradient, jacobi, tiles, order, local, remote, live):
    width = gradient.shape[0]
    blocks = jacobi.shape[0]
    devices = lax.axis_size("rows")
    owner = remote // blocks
    placing = (
        (local[:, None] == jnp.arange(blocks, dtype=jnp.int32)[None, :]) & live[:, None]
    ).astype(f32)
    meets = live[:, None] & (owner[:, None] == jnp.arange(devices, dtype=jnp.int32)[None, :])
    granted = jnp.sum(jnp.where(meets, local[:, None], 0), axis=0)
    vector = jnp.transpose(gradient.reshape(width, blocks, BLOCK), (1, 0, 2))
    steps = []
    for _ in range(ITERS):
        sent = jnp.einsum("nej,nji->nei", vector, jacobi, precision=highest)[granted]
        incoming = lax.all_to_all(sent, "rows", 0, 0, tiled=True)
        products = jnp.einsum(
            "kej,kji->kei", incoming[owner], tiles.astype(f32), precision=highest
        )
        vector = jnp.einsum("kei,kn->nei", products, placing, precision=highest)
        steps.append(vector)
    columns = lax.axis_size("cols")
    share = order.shape[0] // columns
    chain = jnp.pad(jnp.stack(steps), ((0, 0), (0, share * columns - blocks), (0, 0), (0, 0)))
    return [
        lax.dynamic_slice_in_dim(chain, order[o * share], share, 1) for o in range(columns)
    ]


def gather_sums(sums, s, y, weight):
    y = [weight * value for value in y]
    f = [s[0] + s[1]]
    for j in range(1, ITERS):
        f.append(0.5 * (s[j - 1] + s[j + 1]) + s[j])
    for i in range(ITERS):
        for j in range(i + 1):
            sums[i, j] = sums.get((i, j), 0.0) + y[i] * f[j]
        sums[i, ITERS] = sums.get((i, ITERS), 0.0) + y[i] * s[0]


def flat_sums(sums):
    lane = lax.broadcasted_iota(jnp.int32, (1, BLOCK), 1)
    result = jnp.zeros((1, BLOCK), f32)
    for (i, j), value in sums.items():
        value = jnp.sum(jnp.sum(value, axis=0, keepdims=True), axis=1, keepdims=True)
        here = lane == 16 * i + j
        if j < ITERS:
            here = here | (lane == 16 * j + i)
        result = jnp.where(here, value, result)
    return result


def basis_kernel(turn, where, *refs):
    devices = len(refs) - 5
    pieces, jacobi = refs[:devices], refs[devices]
    scaled, powers, gram, scale = refs[devices + 1 :]
    width = pieces[0].shape[0]
    blocks = jacobi.shape[0]
    rows = blocks * BLOCK
    factor = jnp.concatenate([piece[:, rows:] for piece in pieces], 0)
    factor = pltpu.roll(factor, turn[0], 1)
    norm = jnp.max(jnp.sum(jnp.abs(factor), axis=1, keepdims=True), axis=0, keepdims=True)
    power = factor / norm
    for _ in range(3):
        power = dot(power, power)
    bound = jnp.sum(jnp.sum(power * power, axis=1, keepdims=True), axis=0, keepdims=True)
    for _ in range(4):
        bound = jnp.sqrt(bound)
    ratio = 2.0 / (STRETCH * bound * norm)
    scale[...] = jnp.broadcast_to(ratio, scale.shape)
    factor = factor * ratio
    scaled[...] = factor

    row = lax.broadcasted_iota(jnp.int32, (width, BLOCK), 0)
    lane = lax.broadcasted_iota(jnp.int32, (width, BLOCK), 1)
    kept = [(row == lane).astype(f32)]
    for k in range(ITERS):
        value = dot(kept[k], factor) - kept[k]
        kept.append(2.0 * value - kept[k - 1] if k else value)
    first = jnp.concatenate(kept, 0)
    powers[...] = first
    sums = {}
    for b in range(blocks):
        columns = slice(b * BLOCK, (b + 1) * BLOCK)
        plain = dot(first, jnp.concatenate([piece[:, columns] for piece in pieces], 0))
        smooth = dot(plain[: ITERS * width], jacobi[b])
        weight = jnp.where(where[b] < NOWHERE, 0.0, 1.0)
        for r in range(0, width, 8):
            gather_sums(
                sums,
                [plain[k * width + r : k * width + r + 8] for k in range(ITERS + 1)],
                [smooth[k * width + r : k * width + r + 8] for k in range(ITERS)],
                weight,
            )
    gram[...] = flat_sums(sums)


def make_basis(pieces, jacobi, where):
    width = pieces[0].shape[0]
    shape = jax.ShapeDtypeStruct
    turn = (BLOCK - width * lax.axis_index("cols")) % BLOCK
    return call(
        basis_kernel,
        (
            shape((BLOCK, BLOCK), f32),
            shape(((ITERS + 1) * width, BLOCK), f32),
            shape((1, BLOCK), f32),
            shape((8, BLOCK), f32),
        ),
        turn.astype(jnp.int32).reshape(1),
        where,
        *pieces,
        jacobi,
        scalars=2,
    )


def mix_kernel(held, used, *refs):
    devices = (len(refs) - 4) // 3
    parts, pieces = refs[:devices], refs[devices : 2 * devices]
    scaled, jacobi, others = refs[2 * devices : 2 * devices + 3]
    gram, backs = refs[2 * devices + 3], refs[2 * devices + 4 :]
    share, width = parts[0].shape[1:3]
    sums = {}
    for p in range(share):
        block = held[p]
        columns = pl.ds(pl.multiple_of(block * BLOCK, BLOCK), BLOCK)
        now = [jnp.concatenate([piece[:, columns] for piece in pieces], 0)]
        for j in range(ITERS):
            now.append(jnp.concatenate([part[j, p] for part in parts], 0))
        past = None
        chosen = [now[0]]
        for k in range(ITERS):
            left = ITERS - k
            image = dot3(
                scaled[...], jnp.concatenate([now[i] + now[i + 1] for i in range(left)], 1)
            )
            fresh = []
            for i in range(left):
                value = image[:, i * BLOCK : (i + 1) * BLOCK] - now[i]
                fresh.append(2.0 * value - past[i] if k else value)
            past, now = now, fresh
            chosen.append(now[0])
        for o, back in enumerate(backs):
            for k in range(ITERS):
                back[k, p] = chosen[k + 1][o * width : (o + 1) * width]
        soft = dot3(jnp.concatenate(chosen[:ITERS], 0), jacobi[block])
        weight = jnp.where(used[p] > 0, 1.0, 0.0)
        for r in range(0, BLOCK, 8):
            gather_sums(
                sums,
                [value[r : r + 8] for value in chosen],
                [soft[k * BLOCK + r : k * BLOCK + r + 8] for k in range(ITERS)],
                weight,
            )
    gram[...] = flat_sums(sums) + others[...]


def finish_kernel(where, grams, scale, powers, jacobi, *refs):
    devices = (len(refs) - 4) // 2
    pieces, backs = refs[:devices], refs[devices : 2 * devices]
    solution, residual, extra, less = refs[2 * devices :]
    width = pieces[0].shape[0]
    blocks = jacobi.shape[0]
    share = backs[0].shape[1]
    none = devices * share
    flat = jnp.sum(grams[:, 0, :], axis=0, keepdims=True)
    row = lax.broadcasted_iota(jnp.int32, (8, BLOCK), 0)
    lane = lax.broadcasted_iota(jnp.int32, (8, BLOCK), 1)
    table = jnp.zeros((8, BLOCK), f32)
    for i in range(ITERS):
        moved = flat if i == 0 else pltpu.roll(flat, BLOCK - 16 * i, 1)
        table = jnp.where((row == i) & (lane <= ITERS), moved, table)
    for p in range(ITERS):
        pivot = table[p : p + 1, :] / table[p : p + 1, p : p + 1]
        table = jnp.where(row == p, pivot, table - table[:, p : p + 1] * pivot)
    steps = [table[j : j + 1, ITERS : ITERS + 1] for j in range(ITERS)]
    takes = []
    for k in range(ITERS + 1):
        value = 0.0
        if k > 0:
            value += steps[k - 1] * (1.0 if k == 1 else 0.5)
        if k < ITERS:
            value += steps[k]
        if k + 1 < ITERS:
            value += 0.5 * steps[k + 1]
        takes.append(jnp.broadcast_to(value, (width, BLOCK)))
    longer = scale[0:1, 0:1]
    gives = [jnp.broadcast_to(longer * step, (width, BLOCK)) for step in steps]
    pairs = [
        sum(
            weight * powers[k * width : (k + 1) * width, :]
            for k, weight in enumerate(weights)
        )
        for weights in (gives, takes)
    ]
    pairs = jnp.concatenate(pairs, 0)
    for n in range(none):
        back = backs[n // share]
        values = [back[k, n % share] for k in range(ITERS)]
        extra[n] = sum(weight * value for weight, value in zip(gives[1:], values))
        less[n] = sum(weight * value for weight, value in zip(takes[1:], values))
    for b in range(blocks):
        columns = slice(b * BLOCK, (b + 1) * BLOCK)
        whole = jnp.concatenate([piece[:, columns] for piece in pieces], 0)
        start = whole[:width]
        alone = dot(pairs, whole)
        n = jnp.minimum(where[b], none - 1)
        own = where[b] >= NOWHERE
        total = jnp.where(own, alone[:width], gives[0] * start + extra[n])
        solution[:, columns] = dot3(total, jacobi[b])
        left = jnp.where(own, alone[width:], takes[0] * start + less[n])
        residual[:, columns] = start - left


def on_device(
    gradient,
    width_factor,
    diag_blocks,
    jacobi_inverse,
    coupling_tiles,
    tile_local,
    tile_remote,
    tile_count,
    exchange=False,
):
    width, rows = gradient.shape
    blocks = diag_blocks.shape[0]
    columns = lax.axis_size("cols")
    devices = lax.axis_size("rows")
    slots = tile_local.shape[0] - 1
    live = jnp.arange(slots, dtype=jnp.int32) < tile_count[0]
    lists = (tile_local[:slots], tile_remote[:slots], live)

    gathered = devices * slots * BLOCK * (BLOCK + width) * 4
    whole = gathered <= GATHER_BYTES and devices % 2 == 0 and not exchange
    units = slots if whole else blocks
    share = -(-units // columns)
    numbers = jnp.arange(columns * share, dtype=jnp.int32)
    dealer = (lax.axis_index("cols") + columns - numbers // share) % columns
    order = dealer * share + numbers % share
    if whole:
        local = lists[0]
        earlier = jnp.arange(slots)[:, None] > jnp.arange(slots)[None, :]
        repeat = jnp.any(earlier & (local[:, None] == local[None, :]), axis=1)
        fit = order[:, None] == jnp.arange(slots, dtype=jnp.int32)[None, :]
        held = jnp.sum(jnp.where(fit, local[None, :], 0), axis=1)
        used = jnp.sum(jnp.where(fit & (live & ~repeat)[None, :], 1, 0), axis=1)
    else:
        held = jnp.minimum(order, blocks - 1)
        used = (order < blocks).astype(jnp.int32)
    mine = (held[None, :] == jnp.arange(blocks, dtype=jnp.int32)[:, None]) & (used > 0)[None, :]
    where = jnp.min(jnp.where(mine, numbers[None, :], NOWHERE), axis=1)
    if whole:
        sends, pieces, basis = chain_gathered(
            gradient,
            width_factor,
            jacobi_inverse,
            coupling_tiles,
            tile_local,
            order,
            where,
            *lists,
        )
    else:
        sends = chain_exchanged(
            gradient, jacobi_inverse, coupling_tiles[:slots], order, *lists
        )
        pieces = whole_pieces(gradient, width_factor)
        basis = make_basis(pieces, jacobi_inverse, where)
    parts = [sends[0]]
    for o in range(1, columns):
        parts.append(shift(sends[o], "cols", o))

    shape = jax.ShapeDtypeStruct
    scaled, powers, others, scale = basis
    gram, *backs = call(
        mix_kernel,
        tuple(
            [shape((1, BLOCK), f32)]
            + [shape((ITERS, share, width, BLOCK), f32)] * columns
        ),
        held,
        used,
        *parts,
        *pieces,
        scaled,
        jacobi_inverse,
        others,
        scalars=2,
    )
    everyone = columns * devices
    grams = jnp.broadcast_to(gram[None], (everyone, 1, BLOCK))
    grams = lax.all_to_all(grams, ("cols", "rows"), 0, 0, tiled=True)
    for o in range(1, columns):
        backs[o] = shift(backs[o], "cols", -o)
    return call(
        finish_kernel,
        (shape((width, rows), f32), shape((width, rows), f32)),
        where,
        grams,
        scale,
        powers,
        jacobi_inverse,
        *pieces,
        *backs,
        scalars=1,
        scratch=[pltpu.VMEM((columns * share, width, BLOCK), f32)] * 2,
    )


def solution(mesh):
    placed = (
        P("cols", "rows"),
        P(None, "cols"),
        P("rows", None, None),
        P("rows", None, None),
        P("rows", None, None),
        P("rows"),
        P("rows"),
        P("rows"),
    )

    return jax.shard_map(
        on_device,
        mesh=mesh,
        in_specs=placed,
        out_specs=(P("cols", "rows"), P("cols", "rows")),
        check_vma=False,
    )
```

```python
import jax
import jax.numpy as jnp
from jax import lax
from jax.experimental import pallas as pl
from jax.experimental.pallas import tpu as pltpu
from jax.sharding import PartitionSpec as P


BLOCK = 128
ITERS = 6
STRETCH = 1.1
GATHER_BYTES = 8 * 2**20


NOWHERE = 2**20
GRANT_BYTES = 24 * 2**20
WHOLE_BYTES = 60 * 2**20

highest = lax.Precision.HIGHEST
f32 = jnp.float32
VMEM = pl.BlockSpec(memory_space=pltpu.VMEM)
SMEM = pl.BlockSpec(memory_space=pltpu.SMEM)


def dot(a, b):
    return jnp.dot(a, b, precision=highest, preferred_element_type=f32)


def call(kernel, outs, *args, scalars=0, scratch=(), place=VMEM, grant=GRANT_BYTES):
    specs = [SMEM] * scalars + [place] * (len(args) - scalars)
    many = isinstance(outs, tuple)
    return pl.pallas_call(
        kernel,
        out_shape=outs,
        in_specs=specs,
        out_specs=tuple([VMEM] * len(outs)) if many else VMEM,
        scratch_shapes=list(scratch),
        compiler_params=pltpu.CompilerParams(vmem_limit_bytes=grant),
    )(*args)


def split(x):
    high = x.astype(jnp.bfloat16)
    return high, (x - high.astype(f32)).astype(jnp.bfloat16)


def plain_dot(a, b):
    return jnp.dot(a, b, preferred_element_type=f32)


def dot3(a, b):
    tall = a.shape[0]
    high, low = split(a)
    right, rest = split(b)
    both = plain_dot(jnp.concatenate([high, low], 0), right)
    return both[:tall] + (both[tall:] + plain_dot(high, rest))


def pack_kernel(
    local, gradient, jacobi, tiles, packed, blocks, whole, inverse, coupling, done
):
    slots = packed.shape[0]
    contract = (((1,), (1,)), ((), ()))
    moves = [(local, blocks), (jacobi, inverse), (tiles, coupling), (gradient, whole)]
    copies = [
        pltpu.make_async_copy(source, target, done.at[i])
        for i, (source, target) in enumerate(moves)
    ]
    for copy in copies:
        copy.start()
    for copy in copies:
        copy.wait()
    for slot in range(slots):
        block = blocks[slot]
        halves = jnp.concatenate(split(inverse[block]), 0)
        both = lax.dot_general(halves, coupling[slot], contract, preferred_element_type=f32)
        packed[slot, :BLOCK, :] = both[:BLOCK] + both[BLOCK:]
        columns = pl.ds(pl.multiple_of(block * BLOCK, BLOCK), BLOCK)
        packed[slot, BLOCK:, :] = whole[:, columns]


def chain_kernel(sources, give, near, far, *refs):
    sends, (high, low, held, out) = refs[:-4], refs[-4:]
    groups, slots = near.shape[:2]
    half = groups * slots
    total = 2 * half
    width = held.shape[1]
    share = sends[0].shape[1]
    for q in range(total):
        ref = near if q < half else far
        group, slot = divmod(q % half, slots)
        high[q], low[q] = split(ref[group, slot, :BLOCK, :])
        held[q] = ref[group, slot, BLOCK:, :]
    held[total] = jnp.zeros((width, BLOCK), f32)
    out[total] = jnp.zeros((width, BLOCK), f32)

    def step(j, carry):
        for q in range(total):
            first, second = split(held[q])
            both = plain_dot(jnp.concatenate([first, second], 0), high[q])
            out[q] = both[:width] + both[width:] + plain_dot(first, low[q])
        for q in range(total):
            value = out[sources[q * slots]]
            for i in range(1, slots):
                value += out[sources[q * slots + i]]
            held[q] = value
        for o, send in enumerate(sends):
            for p in range(share):
                send[j, p] = held[give[o * share + p]]
        return carry

    lax.fori_loop(0, ITERS, step, 0)


def shift(x, axis, by):
    size = lax.axis_size(axis)
    return lax.ppermute(x, axis, [(i, (i - by) % size) for i in range(size)])


def whole_pieces(gradient, factor):
    piece = jnp.concatenate([gradient, factor.T], axis=1)
    others = range(1, lax.axis_size("cols"))
    return [piece] + [shift(piece, "cols", o) for o in others]


def chain_gathered(gradient, factor, jacobi, tiles, whole_local, order, local, remote, live):
    width = gradient.shape[0]
    blocks, slots = jacobi.shape[0], local.shape[0]
    devices = lax.axis_size("rows")
    columns = lax.axis_size("cols")
    groups = devices // 2
    packed = call(
        pack_kernel,
        jax.ShapeDtypeStruct((slots, BLOCK + width, BLOCK), f32),
        whole_local,
        gradient,
        jacobi,
        tiles,
        scratch=[
            pltpu.SMEM(whole_local.shape, jnp.int32),
            pltpu.VMEM(gradient.shape, f32),
            pltpu.VMEM(jacobi.shape, f32),
            pltpu.VMEM(tiles.shape, tiles.dtype),
            pltpu.SemaphoreType.DMA((4,)),
        ],
        place=pl.BlockSpec(memory_space=pl.ANY),
        grant=WHOLE_BYTES,
    )
    near = [packed] + [shift(packed, "rows", 2 * o) for o in range(1, groups)]
    gradient, factor, _ = lax.optimization_barrier((gradient, factor, packed))
    pieces = whole_pieces(gradient, factor)
    own = jnp.concatenate([local, remote, live.astype(jnp.int32)])
    own = jnp.pad(own, (0, BLOCK - own.shape[0]))
    told = jnp.broadcast_to(own[None, None, :], (devices, 1, BLOCK))
    told = lax.all_to_all(told, "rows", 0, 0, tiled=True)
    told = told[:, 0]
    powers = make_powers(pieces)
    near, pieces, powers, told = lax.optimization_barrier((near, pieces, powers, told))
    near = jnp.stack(near)
    far = lax.ppermute(near, "rows", [(i, i ^ 1) for i in range(devices)])

    me = lax.axis_index("rows")
    position = jnp.arange(devices, dtype=jnp.int32)
    base = me ^ (position // groups)
    device = (base + 2 * (position % groups)) % devices
    pick = (device[:, None] == jnp.arange(devices, dtype=jnp.int32)[None, :]).astype(jnp.int32)
    told = jnp.sum(pick[:, :, None] * told[None, :, :], axis=1)
    locals_, remotes, lives = (
        told[:, i * slots : (i + 1) * slots] for i in range(3)
    )
    owner = (remotes // blocks).reshape(-1)
    holder = jnp.broadcast_to(device[:, None], locals_.shape).reshape(-1)
    alive = lives.reshape(-1) > 0
    meets = (
        (owner[:, None] == holder[None, :])
        & (owner[None, :] == holder[:, None])
        & alive[None, :]
    )
    total = devices * slots
    numbers = jnp.arange(total, dtype=jnp.int32)
    partner = jnp.sum(jnp.where(meets, numbers[None, :], 0), axis=1).reshape(devices, slots)
    same = (
        (locals_[:, :, None] == locals_[:, None, :])
        & (lives[:, None, :] > 0)
        & (lives[:, :, None] > 0)
    )
    sources = jnp.where(same, partner[:, None, :], total).reshape(-1)
    share = order.shape[0] // columns
    shape = jax.ShapeDtypeStruct
    sends = call(
        chain_kernel,
        tuple([shape((ITERS, share, width, BLOCK), f32)] * columns),
        sources,
        jnp.where(order < slots, order, total),
        near,
        far,
        scalars=2,
        scratch=[
            pltpu.VMEM((total, BLOCK, BLOCK), jnp.bfloat16),
            pltpu.VMEM((total, BLOCK, BLOCK), jnp.bfloat16),
            pltpu.VMEM((total + 1, width, BLOCK), f32),
            pltpu.VMEM((total + 1, width, BLOCK), f32),
        ],
    )
    return list(sends), pieces, powers


def chain_exchanged(gradient, jacobi, tiles, order, local, remote, live):
    width = gradient.shape[0]
    blocks = jacobi.shape[0]
    devices = lax.axis_size("rows")
    owner = remote // blocks
    placing = (
        (local[:, None] == jnp.arange(blocks, dtype=jnp.int32)[None, :]) & live[:, None]
    ).astype(f32)
    meets = live[:, None] & (owner[:, None] == jnp.arange(devices, dtype=jnp.int32)[None, :])
    granted = jnp.sum(jnp.where(meets, local[:, None], 0), axis=0)
    vector = jnp.transpose(gradient.reshape(width, blocks, BLOCK), (1, 0, 2))
    steps = []
    for _ in range(ITERS):
        sent = jnp.einsum("nej,nji->nei", vector, jacobi, precision=highest)[granted]
        incoming = lax.all_to_all(sent, "rows", 0, 0, tiled=True)
        products = jnp.einsum(
            "kej,kji->kei", incoming[owner], tiles.astype(f32), precision=highest
        )
        vector = jnp.einsum("kei,kn->nei", products, placing, precision=highest)
        steps.append(vector)
    columns = lax.axis_size("cols")
    share = order.shape[0] // columns
    chain = jnp.pad(jnp.stack(steps), ((0, 0), (0, share * columns - blocks), (0, 0), (0, 0)))
    return [
        lax.dynamic_slice_in_dim(chain, order[o * share], share, 1) for o in range(columns)
    ]


def gather_sums(sums, s, y, weight):
    y = [weight * value for value in y]
    f = [s[0] + s[1]]
    for j in range(1, ITERS):
        f.append(0.5 * (s[j - 1] + s[j + 1]) + s[j])
    for i in range(ITERS):
        for j in range(i + 1):
            sums[i, j] = sums.get((i, j), 0.0) + y[i] * f[j]
        sums[i, ITERS] = sums.get((i, ITERS), 0.0) + y[i] * s[0]


def flat_sums(sums):
    lane = lax.broadcasted_iota(jnp.int32, (1, BLOCK), 1)
    result = jnp.zeros((1, BLOCK), f32)
    for (i, j), value in sums.items():
        value = jnp.sum(jnp.sum(value, axis=0, keepdims=True), axis=1, keepdims=True)
        here = lane == 16 * i + j
        if j < ITERS:
            here = here | (lane == 16 * j + i)
        result = jnp.where(here, value, result)
    return result


def powers_kernel(turn, *refs):
    pieces, (scaled, powers, scale) = refs[:-3], refs[-3:]
    width = pieces[0].shape[0]
    factor = jnp.concatenate([piece[:, -BLOCK:] for piece in pieces], 0)
    factor = pltpu.roll(factor, turn[0], 1)
    norm = jnp.max(jnp.sum(jnp.abs(factor), axis=1, keepdims=True), axis=0, keepdims=True)
    power = factor / norm
    for _ in range(3):
        power = dot(power, power)
    bound = jnp.sum(jnp.sum(power * power, axis=1, keepdims=True), axis=0, keepdims=True)
    for _ in range(4):
        bound = jnp.sqrt(bound)
    ratio = 2.0 / (STRETCH * bound * norm)
    scale[...] = jnp.broadcast_to(ratio, scale.shape)
    factor = factor * ratio
    scaled[...] = factor

    row = lax.broadcasted_iota(jnp.int32, (width, BLOCK), 0)
    lane = lax.broadcasted_iota(jnp.int32, (width, BLOCK), 1)
    kept = [(row == lane).astype(f32)]
    for k in range(ITERS):
        value = dot(kept[k], factor) - kept[k]
        kept.append(2.0 * value - kept[k - 1] if k else value)
    powers[...] = jnp.concatenate(kept, 0)


def basis_kernel(where, held, powers, jacobi, *refs):
    pieces, (plain, smooth, gram, starts) = refs[:-4], refs[-4:]
    width = pieces[0].shape[0]
    for p in range(starts.shape[0]):
        columns = pl.ds(pl.multiple_of(held[p] * BLOCK, BLOCK), BLOCK)
        starts[p] = jnp.concatenate([piece[:, columns] for piece in pieces], 0)
    sums = {}
    for b in range(jacobi.shape[0]):
        columns = slice(b * BLOCK, (b + 1) * BLOCK)
        whole = jnp.concatenate([piece[:, columns] for piece in pieces], 0)
        s = dot(powers[...], whole)
        y = dot(s[: ITERS * width], jacobi[b])
        plain[b] = s[width:]
        smooth[b] = y
        weight = jnp.where(where[b] < NOWHERE, 0.0, 1.0)
        for r in range(0, width, 8):
            gather_sums(
                sums,
                [s[k * width + r : k * width + r + 8] for k in range(ITERS + 1)],
                [y[k * width + r : k * width + r + 8] for k in range(ITERS)],
                weight,
            )
    gram[...] = flat_sums(sums)


def make_powers(pieces):
    width = pieces[0].shape[0]
    shape = jax.ShapeDtypeStruct
    turn = (BLOCK - width * lax.axis_index("cols")) % BLOCK
    return call(
        powers_kernel,
        (
            shape((BLOCK, BLOCK), f32),
            shape(((ITERS + 1) * width, BLOCK), f32),
            shape((8, BLOCK), f32),
        ),
        turn.astype(jnp.int32).reshape(1),
        *pieces,
        scalars=1,
    )


def mix_kernel(held, used, *refs):
    devices = (len(refs) - 5) // 2
    parts = refs[:devices]
    starts, scaled, jacobi, others, gram = refs[devices : devices + 5]
    backs = refs[devices + 5 :]
    share, width = parts[0].shape[1:3]
    sums = {}
    for p in range(share):
        now = [starts[p]]
        for j in range(ITERS):
            now.append(jnp.concatenate([part[j, p] for part in parts], 0))
        past = None
        chosen = [now[0]]
        for k in range(ITERS):
            left = ITERS - k
            image = dot3(
                scaled[...], jnp.concatenate([now[i] + now[i + 1] for i in range(left)], 1)
            )
            fresh = []
            for i in range(left):
                value = image[:, i * BLOCK : (i + 1) * BLOCK] - now[i]
                fresh.append(2.0 * value - past[i] if k else value)
            past, now = now, fresh
            chosen.append(now[0])
        for o, back in enumerate(backs):
            for k in range(ITERS):
                back[k, p] = chosen[k + 1][o * width : (o + 1) * width]
        soft = dot3(jnp.concatenate(chosen[:ITERS], 0), jacobi[held[p]])
        weight = jnp.where(used[p] > 0, 1.0, 0.0)
        for r in range(0, BLOCK, 8):
            gather_sums(
                sums,
                [value[r : r + 8] for value in chosen],
                [soft[k * BLOCK + r : k * BLOCK + r + 8] for k in range(ITERS)],
                weight,
            )
    gram[...] = jnp.broadcast_to((flat_sums(sums) + others[...])[None], gram.shape)


def finish_kernel(held, where, grams, scale, gradient, plain, smooth, jacobi, *refs):
    backs, (solution, residual, extra, less) = refs[:-4], refs[-4:]
    width = gradient.shape[0]
    blocks = jacobi.shape[0]
    share = backs[0].shape[1]
    none = len(backs) * share
    flat = jnp.sum(grams[:, 0, :], axis=0, keepdims=True)
    row = lax.broadcasted_iota(jnp.int32, (8, BLOCK), 0)
    lane = lax.broadcasted_iota(jnp.int32, (8, BLOCK), 1)
    table = jnp.zeros((8, BLOCK), f32)
    for i in range(ITERS):
        moved = flat if i == 0 else pltpu.roll(flat, BLOCK - 16 * i, 1)
        table = jnp.where((row == i) & (lane <= ITERS), moved, table)
    for p in range(ITERS):
        pivot = table[p : p + 1, :] / table[p : p + 1, p : p + 1]
        table = jnp.where(row == p, pivot, table - table[:, p : p + 1] * pivot)
    steps = [table[j : j + 1, ITERS : ITERS + 1] for j in range(ITERS)]
    takes = []
    for k in range(ITERS + 1):
        value = 0.0
        if k > 0:
            value += steps[k - 1] * (1.0 if k == 1 else 0.5)
        if k < ITERS:
            value += steps[k]
        if k + 1 < ITERS:
            value += 0.5 * steps[k + 1]
        takes.append(jnp.broadcast_to(value, (width, BLOCK)))
    longer = scale[0:1, 0:1]
    gives = [jnp.broadcast_to(longer * step, (width, BLOCK)) for step in steps]

    def combine(weights, values):
        return sum(weight * value for weight, value in zip(weights, values))

    def cut(ref, b):
        return [ref[b, k * width : (k + 1) * width, :] for k in range(ITERS)]

    for n in range(none):
        values = [backs[n // share][k, n % share] for k in range(ITERS)]
        extra[n] = dot3(combine(gives[1:], values), jacobi[held[n]])
        less[n] = combine(takes[1:], values)
    for b in range(blocks):
        columns = slice(b * BLOCK, (b + 1) * BLOCK)
        n = jnp.minimum(where[b], none - 1)
        own = where[b] >= NOWHERE
        y = cut(smooth, b)
        rest = jnp.where(own, combine(gives[1:], y[1:]), extra[n])
        solution[:, columns] = gives[0] * y[0] + rest
        rest = jnp.where(own, combine(takes[1:], cut(plain, b)), less[n])
        start = gradient[:, columns]
        residual[:, columns] = start - takes[0] * start - rest


def on_device(
    gradient,
    width_factor,
    diag_blocks,
    jacobi_inverse,
    coupling_tiles,
    tile_local,
    tile_remote,
    tile_count,
    exchange=False,
):
    width, rows = gradient.shape
    blocks = diag_blocks.shape[0]
    columns = lax.axis_size("cols")
    devices = lax.axis_size("rows")
    slots = tile_local.shape[0] - 1
    live = jnp.arange(slots, dtype=jnp.int32) < tile_count[0]
    lists = (tile_local[:slots], tile_remote[:slots], live)

    gathered = devices * slots * BLOCK * (BLOCK + width) * 4
    whole = gathered <= GATHER_BYTES and devices % 2 == 0 and not exchange
    units = slots if whole else blocks
    share = -(-units // columns)
    numbers = jnp.arange(columns * share, dtype=jnp.int32)
    dealer = (lax.axis_index("cols") + columns - numbers // share) % columns
    order = dealer * share + numbers % share
    if whole:
        local = lists[0]
        earlier = jnp.arange(slots)[:, None] > jnp.arange(slots)[None, :]
        repeat = jnp.any(earlier & (local[:, None] == local[None, :]), axis=1)
        fit = order[:, None] == jnp.arange(slots, dtype=jnp.int32)[None, :]
        held = jnp.sum(jnp.where(fit, local[None, :], 0), axis=1)
        used = jnp.sum(jnp.where(fit & (live & ~repeat)[None, :], 1, 0), axis=1)
    else:
        held = jnp.minimum(order, blocks - 1)
        used = (order < blocks).astype(jnp.int32)
    mine = (held[None, :] == jnp.arange(blocks, dtype=jnp.int32)[:, None]) & (used > 0)[None, :]
    where = jnp.min(jnp.where(mine, numbers[None, :], NOWHERE), axis=1)
    if whole:
        sends, pieces, powers = chain_gathered(
            gradient,
            width_factor,
            jacobi_inverse,
            coupling_tiles,
            tile_local,
            order,
            *lists,
        )
    else:
        sends = chain_exchanged(
            gradient, jacobi_inverse, coupling_tiles[:slots], order, *lists
        )
        pieces = whole_pieces(gradient, width_factor)
        powers = make_powers(pieces)
    scaled, powers, scale = powers
    powers, sends = lax.optimization_barrier((powers, sends))
    parts = [sends[0]]
    for o in range(1, columns):
        parts.append(shift(sends[o], "cols", o))

    shape = jax.ShapeDtypeStruct
    plain, smooth, others, starts = call(
        basis_kernel,
        (
            shape((blocks, ITERS * width, BLOCK), f32),
            shape((blocks, ITERS * width, BLOCK), f32),
            shape((1, BLOCK), f32),
            shape((share, BLOCK, BLOCK), f32),
        ),
        where,
        held,
        powers,
        jacobi_inverse,
        *pieces,
        scalars=2,
    )
    gram, *backs = call(
        mix_kernel,
        tuple(
            [shape((columns * devices, 1, BLOCK), f32)]
            + [shape((ITERS, share, width, BLOCK), f32)] * columns
        ),
        held,
        used,
        *parts,
        starts,
        scaled,
        jacobi_inverse,
        others,
        scalars=2,
    )
    grams = lax.all_to_all(gram, ("cols", "rows"), 0, 0, tiled=True)
    for o in range(1, columns):
        backs[o] = shift(backs[o], "cols", -o)
    return call(
        finish_kernel,
        (shape((width, rows), f32), shape((width, rows), f32)),
        held,
        where,
        grams,
        scale,
        gradient,
        plain,
        smooth,
        jacobi_inverse,
        *backs,
        scalars=2,
        scratch=[pltpu.VMEM((columns * share, width, BLOCK), f32)] * 2,
    )


def solution(mesh):
    placed = (
        P("cols", "rows"),
        P(None, "cols"),
        P("rows", None, None),
        P("rows", None, None),
        P("rows", None, None),
        P("rows"),
        P("rows"),
        P("rows"),
    )

    return jax.shard_map(
        on_device,
        mesh=mesh,
        in_specs=placed,
        out_specs=(P("cols", "rows"), P("cols", "rows")),
        check_vma=False,
    )
```

```python
import jax
import jax.numpy as jnp
from jax import lax
from jax.experimental import pallas as pl
from jax.experimental.pallas import tpu as pltpu
from jax.sharding import PartitionSpec as P


BLOCK = 128
ITERS = 6
STRETCH = 1.1
GATHER_BYTES = 8 * 2**20


NOWHERE = 2**20
LEVELS = 32767.0
GRANT_BYTES = 24 * 2**20
WHOLE_BYTES = 60 * 2**20

highest = lax.Precision.HIGHEST
f32 = jnp.float32
VMEM = pl.BlockSpec(memory_space=pltpu.VMEM)
SMEM = pl.BlockSpec(memory_space=pltpu.SMEM)


def dot(a, b):
    return jnp.dot(a, b, precision=highest, preferred_element_type=f32)


def call(kernel, outs, *args, scalars=0, scratch=(), place=VMEM, grant=GRANT_BYTES):
    specs = [SMEM] * scalars + [place] * (len(args) - scalars)
    many = isinstance(outs, tuple)
    return pl.pallas_call(
        kernel,
        out_shape=outs,
        in_specs=specs,
        out_specs=tuple([VMEM] * len(outs)) if many else VMEM,
        scratch_shapes=list(scratch),
        compiler_params=pltpu.CompilerParams(vmem_limit_bytes=grant),
    )(*args)


def split(x):
    high = x.astype(jnp.bfloat16)
    return high, (x - high.astype(f32)).astype(jnp.bfloat16)


def plain_dot(a, b):
    return jnp.dot(a, b, preferred_element_type=f32)


def dot3(a, b):
    tall = a.shape[0]
    high, low = split(a)
    right, rest = split(b)
    both = plain_dot(jnp.concatenate([high, low], 0), right)
    return both[:tall] + (both[tall:] + plain_dot(high, rest))


def code(x, top):
    unit = LEVELS / jnp.where(top > 0, top, 1.0)
    return jnp.floor(x * unit + 0.5).astype(jnp.int32).astype(jnp.int16)


def pack_kernel(
    local, gradient, jacobi, tiles, packed, marks, blocks, whole, inverse, coupling, done
):
    slots = packed.shape[0]
    width = whole.shape[0]
    contract = (((1,), (1,)), ((), ()))
    moves = [(local, blocks), (jacobi, inverse), (tiles, coupling), (gradient, whole)]
    copies = [
        pltpu.make_async_copy(source, target, done.at[i])
        for i, (source, target) in enumerate(moves)
    ]
    for copy in copies:
        copy.start()
    for copy in copies:
        copy.wait()
    lane = lax.broadcasted_iota(jnp.int32, (width, BLOCK), 1)
    row = lax.broadcasted_iota(jnp.int32, (width, BLOCK), 0)
    noted = jnp.zeros((width, BLOCK), f32)
    for slot in range(slots):
        block = blocks[slot]
        halves = jnp.concatenate(split(inverse[block]), 0)
        both = lax.dot_general(halves, coupling[slot], contract, preferred_element_type=f32)
        operator = both[:BLOCK] + both[BLOCK:]
        top = jnp.max(jnp.max(jnp.abs(operator), axis=0, keepdims=True), axis=1, keepdims=True)
        packed[slot, :BLOCK, :] = code(operator, top)
        noted = jnp.where((lane == 3 * slots + slot) & (row == 0), top, noted)
        columns = pl.ds(pl.multiple_of(block * BLOCK, BLOCK), BLOCK)
        part = whole[:, columns]
        top = jnp.max(jnp.abs(part), axis=1, keepdims=True)
        packed[slot, BLOCK:, :] = code(part, top)
        noted = jnp.where(lane == 4 * slots + slot * width + row, top, noted)
    marks[...] = jnp.sum(noted, axis=0, keepdims=True)


def chain_kernel(sources, give, tops, told, near, far, *refs):
    sends, (operators, held, out) = refs[:-3], refs[-3:]
    groups, slots = near.shape[:2]
    half = groups * slots
    total = 2 * half
    width = held.shape[1]
    share = sends[0].shape[1]
    lane = lax.broadcasted_iota(jnp.int32, (width, BLOCK), 1)
    row = lax.broadcasted_iota(jnp.int32, (width, BLOCK), 0)
    for q in range(total):
        ref = near if q < half else far
        device, slot = divmod(q, slots)
        group = device % groups
        high, low = split(ref[group, slot, :BLOCK, :].astype(f32))
        operators[q, :, :BLOCK] = high
        operators[q, :, BLOCK:] = low
        here = lane == 4 * slots + slot * width + row
        top = jnp.where(here, told[device : device + 1, :], 0.0)
        top = jnp.sum(top, axis=1, keepdims=True) * (1.0 / LEVELS)
        held[q] = ref[group, slot, BLOCK:, :].astype(f32) * top
    held[total] = jnp.zeros((width, BLOCK), f32)
    out[total] = jnp.zeros((width, BLOCK), f32)

    def step(j, carry):
        for q in range(total):
            four = plain_dot(jnp.concatenate(split(held[q]), 0), operators[q])
            value = (four[:width, :BLOCK] + four[width:, :BLOCK]) + (
                four[:width, BLOCK:] + four[width:, BLOCK:]
            )
            out[q] = value * (tops[q] * (1.0 / LEVELS))
        for q in range(total):
            value = out[sources[q * slots]]
            for i in range(1, slots):
                value += out[sources[q * slots + i]]
            held[q] = value
        for o, send in enumerate(sends):
            for p in range(share):
                send[j, p] = held[give[o * share + p]]
        return carry

    lax.fori_loop(0, ITERS, step, 0)


def shift(x, axis, by):
    size = lax.axis_size(axis)
    return lax.ppermute(x, axis, [(i, (i - by) % size) for i in range(size)])


def whole_pieces(gradient, factor):
    piece = jnp.concatenate([gradient, factor.T], axis=1)
    others = range(1, lax.axis_size("cols"))
    return [piece] + [shift(piece, "cols", o) for o in others]


def chain_gathered(gradient, factor, jacobi, tiles, whole_local, order, local, remote, live):
    width = gradient.shape[0]
    blocks, slots = jacobi.shape[0], local.shape[0]
    devices = lax.axis_size("rows")
    columns = lax.axis_size("cols")
    groups = devices // 2
    packed, marks = call(
        pack_kernel,
        (
            jax.ShapeDtypeStruct((slots, BLOCK + width, BLOCK), jnp.int16),
            jax.ShapeDtypeStruct((1, BLOCK), f32),
        ),
        whole_local,
        gradient,
        jacobi,
        tiles,
        scratch=[
            pltpu.SMEM(whole_local.shape, jnp.int32),
            pltpu.VMEM(gradient.shape, f32),
            pltpu.VMEM(jacobi.shape, f32),
            pltpu.VMEM(tiles.shape, tiles.dtype),
            pltpu.SemaphoreType.DMA((4,)),
        ],
        place=pl.BlockSpec(memory_space=pl.ANY),
        grant=WHOLE_BYTES,
    )
    near = [packed] + [shift(packed, "rows", 2 * o) for o in range(1, groups)]
    gradient, factor, _ = lax.optimization_barrier((gradient, factor, packed))
    pieces = whole_pieces(gradient, factor)
    own = jnp.concatenate([local, remote, live.astype(jnp.int32)])
    own = jnp.pad(own.astype(f32), (0, BLOCK - own.shape[0])) + marks[0]
    told = jnp.broadcast_to(own[None, None, :], (devices, 1, BLOCK))
    told = lax.all_to_all(told, "rows", 0, 0, tiled=True)
    told = told[:, 0]
    powers = make_powers(pieces)
    near, pieces, powers, told = lax.optimization_barrier((near, pieces, powers, told))
    near = jnp.stack(near)
    far = lax.ppermute(near, "rows", [(i, i ^ 1) for i in range(devices)])

    me = lax.axis_index("rows")
    position = jnp.arange(devices, dtype=jnp.int32)
    base = me ^ (position // groups)
    device = (base + 2 * (position % groups)) % devices
    pick = (device[:, None] == jnp.arange(devices, dtype=jnp.int32)[None, :])
    told = jnp.sum(jnp.where(pick[:, :, None], told[None, :, :], 0.0), axis=1)
    locals_, remotes, lives = (
        told[:, i * slots : (i + 1) * slots].astype(jnp.int32) for i in range(3)
    )
    tops = told[:, 3 * slots : 4 * slots].reshape(-1)
    owner = (remotes // blocks).reshape(-1)
    holder = jnp.broadcast_to(device[:, None], locals_.shape).reshape(-1)
    alive = lives.reshape(-1) > 0
    meets = (
        (owner[:, None] == holder[None, :])
        & (owner[None, :] == holder[:, None])
        & alive[None, :]
    )
    total = devices * slots
    numbers = jnp.arange(total, dtype=jnp.int32)
    partner = jnp.sum(jnp.where(meets, numbers[None, :], 0), axis=1).reshape(devices, slots)
    same = (
        (locals_[:, :, None] == locals_[:, None, :])
        & (lives[:, None, :] > 0)
        & (lives[:, :, None] > 0)
    )
    sources = jnp.where(same, partner[:, None, :], total).reshape(-1)
    share = order.shape[0] // columns
    shape = jax.ShapeDtypeStruct
    sends = call(
        chain_kernel,
        tuple([shape((ITERS, share, width, BLOCK), f32)] * columns),
        sources,
        jnp.where(order < slots, order, total),
        tops,
        told,
        near,
        far,
        scalars=3,
        scratch=[
            pltpu.VMEM((total, BLOCK, 2 * BLOCK), jnp.bfloat16),
            pltpu.VMEM((total + 1, width, BLOCK), f32),
            pltpu.VMEM((total + 1, width, BLOCK), f32),
        ],
    )
    return list(sends), pieces, powers


def chain_exchanged(gradient, jacobi, tiles, order, local, remote, live):
    width = gradient.shape[0]
    blocks = jacobi.shape[0]
    devices = lax.axis_size("rows")
    owner = remote // blocks
    placing = (
        (local[:, None] == jnp.arange(blocks, dtype=jnp.int32)[None, :]) & live[:, None]
    ).astype(f32)
    meets = live[:, None] & (owner[:, None] == jnp.arange(devices, dtype=jnp.int32)[None, :])
    granted = jnp.sum(jnp.where(meets, local[:, None], 0), axis=0)
    vector = jnp.transpose(gradient.reshape(width, blocks, BLOCK), (1, 0, 2))
    steps = []
    for _ in range(ITERS):
        sent = jnp.einsum("nej,nji->nei", vector, jacobi, precision=highest)[granted]
        incoming = lax.all_to_all(sent, "rows", 0, 0, tiled=True)
        products = jnp.einsum(
            "kej,kji->kei", incoming[owner], tiles.astype(f32), precision=highest
        )
        vector = jnp.einsum("kei,kn->nei", products, placing, precision=highest)
        steps.append(vector)
    columns = lax.axis_size("cols")
    share = order.shape[0] // columns
    chain = jnp.pad(jnp.stack(steps), ((0, 0), (0, share * columns - blocks), (0, 0), (0, 0)))
    return [
        lax.dynamic_slice_in_dim(chain, order[o * share], share, 1) for o in range(columns)
    ]


def gather_sums(sums, s, y, weight):
    y = [weight * value for value in y]
    f = [s[0] + s[1]]
    for j in range(1, ITERS):
        f.append(0.5 * (s[j - 1] + s[j + 1]) + s[j])
    for i in range(ITERS):
        for j in range(i + 1):
            sums[i, j] = sums.get((i, j), 0.0) + y[i] * f[j]
        sums[i, ITERS] = sums.get((i, ITERS), 0.0) + y[i] * s[0]


def flat_sums(sums):
    lane = lax.broadcasted_iota(jnp.int32, (1, BLOCK), 1)
    result = jnp.zeros((1, BLOCK), f32)
    for (i, j), value in sums.items():
        value = jnp.sum(jnp.sum(value, axis=0, keepdims=True), axis=1, keepdims=True)
        here = lane == 16 * i + j
        if j < ITERS:
            here = here | (lane == 16 * j + i)
        result = jnp.where(here, value, result)
    return result


def powers_kernel(turn, *refs):
    pieces, (scaled, powers, scale) = refs[:-3], refs[-3:]
    width = pieces[0].shape[0]
    factor = jnp.concatenate([piece[:, -BLOCK:] for piece in pieces], 0)
    factor = pltpu.roll(factor, turn[0], 1)
    norm = jnp.max(jnp.sum(jnp.abs(factor), axis=1, keepdims=True), axis=0, keepdims=True)
    power = factor / norm
    for _ in range(3):
        power = dot(power, power)
    bound = jnp.sum(jnp.sum(power * power, axis=1, keepdims=True), axis=0, keepdims=True)
    for _ in range(4):
        bound = jnp.sqrt(bound)
    ratio = 2.0 / (STRETCH * bound * norm)
    scale[...] = jnp.broadcast_to(ratio, scale.shape)
    factor = factor * ratio
    scaled[...] = factor

    row = lax.broadcasted_iota(jnp.int32, (width, BLOCK), 0)
    lane = lax.broadcasted_iota(jnp.int32, (width, BLOCK), 1)
    kept = [(row == lane).astype(f32)]
    for k in range(ITERS):
        value = dot(kept[k], factor) - kept[k]
        kept.append(2.0 * value - kept[k - 1] if k else value)
    powers[...] = jnp.concatenate(kept, 0)


def basis_kernel(where, held, powers, jacobi, *refs):
    pieces, (plain, smooth, gram, starts) = refs[:-4], refs[-4:]
    width = pieces[0].shape[0]
    for p in range(starts.shape[0]):
        columns = pl.ds(pl.multiple_of(held[p] * BLOCK, BLOCK), BLOCK)
        starts[p] = jnp.concatenate([piece[:, columns] for piece in pieces], 0)
    sums = {}
    for b in range(jacobi.shape[0]):
        columns = slice(b * BLOCK, (b + 1) * BLOCK)
        whole = jnp.concatenate([piece[:, columns] for piece in pieces], 0)
        s = dot(powers[...], whole)
        y = dot(s[: ITERS * width], jacobi[b])
        plain[b] = s[width:]
        smooth[b] = y
        weight = jnp.where(where[b] < NOWHERE, 0.0, 1.0)
        for r in range(0, width, 8):
            gather_sums(
                sums,
                [s[k * width + r : k * width + r + 8] for k in range(ITERS + 1)],
                [y[k * width + r : k * width + r + 8] for k in range(ITERS)],
                weight,
            )
    gram[...] = flat_sums(sums)


def make_powers(pieces):
    width = pieces[0].shape[0]
    shape = jax.ShapeDtypeStruct
    turn = (BLOCK - width * lax.axis_index("cols")) % BLOCK
    return call(
        powers_kernel,
        (
            shape((BLOCK, BLOCK), f32),
            shape(((ITERS + 1) * width, BLOCK), f32),
            shape((8, BLOCK), f32),
        ),
        turn.astype(jnp.int32).reshape(1),
        *pieces,
        scalars=1,
    )


def mix_kernel(held, used, *refs):
    devices = (len(refs) - 5) // 2
    parts = refs[:devices]
    starts, scaled, jacobi, others, gram = refs[devices : devices + 5]
    backs = refs[devices + 5 :]
    share, width = parts[0].shape[1:3]
    sums = {}
    for p in range(share):
        now = [starts[p]]
        for j in range(ITERS):
            now.append(jnp.concatenate([part[j, p] for part in parts], 0))
        past = None
        chosen = [now[0]]
        for k in range(ITERS):
            left = ITERS - k
            image = dot3(
                scaled[...], jnp.concatenate([now[i] + now[i + 1] for i in range(left)], 1)
            )
            fresh = []
            for i in range(left):
                value = image[:, i * BLOCK : (i + 1) * BLOCK] - now[i]
                fresh.append(2.0 * value - past[i] if k else value)
            past, now = now, fresh
            chosen.append(now[0])
        for o, back in enumerate(backs):
            for k in range(ITERS):
                back[k, p] = chosen[k + 1][o * width : (o + 1) * width]
        soft = dot3(jnp.concatenate(chosen[:ITERS], 0), jacobi[held[p]])
        weight = jnp.where(used[p] > 0, 1.0, 0.0)
        for r in range(0, BLOCK, 8):
            gather_sums(
                sums,
                [value[r : r + 8] for value in chosen],
                [soft[k * BLOCK + r : k * BLOCK + r + 8] for k in range(ITERS)],
                weight,
            )
    gram[...] = jnp.broadcast_to((flat_sums(sums) + others[...])[None], gram.shape)


def finish_kernel(held, where, grams, scale, gradient, plain, smooth, jacobi, *refs):
    backs, (solution, residual, extra, less) = refs[:-4], refs[-4:]
    width = gradient.shape[0]
    blocks = jacobi.shape[0]
    share = backs[0].shape[1]
    none = len(backs) * share
    flat = jnp.sum(grams[:, 0, :], axis=0, keepdims=True)
    row = lax.broadcasted_iota(jnp.int32, (8, BLOCK), 0)
    lane = lax.broadcasted_iota(jnp.int32, (8, BLOCK), 1)
    table = jnp.zeros((8, BLOCK), f32)
    for i in range(ITERS):
        moved = flat if i == 0 else pltpu.roll(flat, BLOCK - 16 * i, 1)
        table = jnp.where((row == i) & (lane <= ITERS), moved, table)
    for p in range(ITERS):
        pivot = table[p : p + 1, :] / table[p : p + 1, p : p + 1]
        table = jnp.where(row == p, pivot, table - table[:, p : p + 1] * pivot)
    steps = [table[j : j + 1, ITERS : ITERS + 1] for j in range(ITERS)]
    takes = []
    for k in range(ITERS + 1):
        value = 0.0
        if k > 0:
            value += steps[k - 1] * (1.0 if k == 1 else 0.5)
        if k < ITERS:
            value += steps[k]
        if k + 1 < ITERS:
            value += 0.5 * steps[k + 1]
        takes.append(jnp.broadcast_to(value, (width, BLOCK)))
    longer = scale[0:1, 0:1]
    gives = [jnp.broadcast_to(longer * step, (width, BLOCK)) for step in steps]

    def combine(weights, values):
        return sum(weight * value for weight, value in zip(weights, values))

    def cut(ref, b):
        return [ref[b, k * width : (k + 1) * width, :] for k in range(ITERS)]

    for n in range(none):
        values = [backs[n // share][k, n % share] for k in range(ITERS)]
        extra[n] = dot3(combine(gives[1:], values), jacobi[held[n]])
        less[n] = combine(takes[1:], values)
    for b in range(blocks):
        columns = slice(b * BLOCK, (b + 1) * BLOCK)
        n = jnp.minimum(where[b], none - 1)
        own = where[b] >= NOWHERE
        y = cut(smooth, b)
        rest = jnp.where(own, combine(gives[1:], y[1:]), extra[n])
        solution[:, columns] = gives[0] * y[0] + rest
        rest = jnp.where(own, combine(takes[1:], cut(plain, b)), less[n])
        start = gradient[:, columns]
        residual[:, columns] = start - takes[0] * start - rest


def on_device(
    gradient,
    width_factor,
    diag_blocks,
    jacobi_inverse,
    coupling_tiles,
    tile_local,
    tile_remote,
    tile_count,
    exchange=False,
):
    width, rows = gradient.shape
    blocks = diag_blocks.shape[0]
    columns = lax.axis_size("cols")
    devices = lax.axis_size("rows")
    slots = tile_local.shape[0] - 1
    live = jnp.arange(slots, dtype=jnp.int32) < tile_count[0]
    lists = (tile_local[:slots], tile_remote[:slots], live)

    gathered = devices * slots * BLOCK * (BLOCK + width) * 2
    noted = slots * (4 + width) <= BLOCK
    whole = gathered <= GATHER_BYTES and noted and devices % 2 == 0 and not exchange
    units = slots if whole else blocks
    share = -(-units // columns)
    numbers = jnp.arange(columns * share, dtype=jnp.int32)
    dealer = (lax.axis_index("cols") + columns - numbers // share) % columns
    order = dealer * share + numbers % share
    if whole:
        local = lists[0]
        earlier = jnp.arange(slots)[:, None] > jnp.arange(slots)[None, :]
        repeat = jnp.any(earlier & (local[:, None] == local[None, :]), axis=1)
        fit = order[:, None] == jnp.arange(slots, dtype=jnp.int32)[None, :]
        held = jnp.sum(jnp.where(fit, local[None, :], 0), axis=1)
        used = jnp.sum(jnp.where(fit & (live & ~repeat)[None, :], 1, 0), axis=1)
    else:
        held = jnp.minimum(order, blocks - 1)
        used = (order < blocks).astype(jnp.int32)
    mine = (held[None, :] == jnp.arange(blocks, dtype=jnp.int32)[:, None]) & (used > 0)[None, :]
    where = jnp.min(jnp.where(mine, numbers[None, :], NOWHERE), axis=1)
    if whole:
        sends, pieces, powers = chain_gathered(
            gradient,
            width_factor,
            jacobi_inverse,
            coupling_tiles,
            tile_local,
            order,
            *lists,
        )
    else:
        sends = chain_exchanged(
            gradient, jacobi_inverse, coupling_tiles[:slots], order, *lists
        )
        pieces = whole_pieces(gradient, width_factor)
        powers = make_powers(pieces)
    scaled, powers, scale = powers
    powers, sends = lax.optimization_barrier((powers, sends))
    parts = [sends[0]]
    for o in range(1, columns):
        parts.append(shift(sends[o], "cols", o))

    shape = jax.ShapeDtypeStruct
    plain, smooth, others, starts = call(
        basis_kernel,
        (
            shape((blocks, ITERS * width, BLOCK), f32),
            shape((blocks, ITERS * width, BLOCK), f32),
            shape((1, BLOCK), f32),
            shape((share, BLOCK, BLOCK), f32),
        ),
        where,
        held,
        powers,
        jacobi_inverse,
        *pieces,
        scalars=2,
    )
    gram, *backs = call(
        mix_kernel,
        tuple(
            [shape((columns * devices, 1, BLOCK), f32)]
            + [shape((ITERS, share, width, BLOCK), f32)] * columns
        ),
        held,
        used,
        *parts,
        starts,
        scaled,
        jacobi_inverse,
        others,
        scalars=2,
    )
    grams = lax.all_to_all(gram, ("cols", "rows"), 0, 0, tiled=True)
    for o in range(1, columns):
        backs[o] = shift(backs[o], "cols", -o)
    return call(
        finish_kernel,
        (shape((width, rows), f32), shape((width, rows), f32)),
        held,
        where,
        grams,
        scale,
        gradient,
        plain,
        smooth,
        jacobi_inverse,
        *backs,
        scalars=2,
        scratch=[pltpu.VMEM((columns * share, width, BLOCK), f32)] * 2,
    )


def solution(mesh):
    placed = (
        P("cols", "rows"),
        P(None, "cols"),
        P("rows", None, None),
        P("rows", None, None),
        P("rows", None, None),
        P("rows"),
        P("rows"),
        P("rows"),
    )

    return jax.shard_map(
        on_device,
        mesh=mesh,
        in_specs=placed,
        out_specs=(P("cols", "rows"), P("cols", "rows")),
        check_vma=False,
    )
```

```python
import jax
import jax.numpy as jnp
from jax import lax
from jax.experimental import pallas as pl
from jax.experimental.pallas import tpu as pltpu
from jax.sharding import PartitionSpec as P


BLOCK = 128
ITERS = 6
STRETCH = 1.1
GATHER_BYTES = 8 * 2**20


NOWHERE = 2**20
LEVELS = 32700.0
NOTES = 256 / 0.6931471805599453
NOTE_ROWS = 16
GRANT_BYTES = 24 * 2**20
WHOLE_BYTES = 60 * 2**20

highest = lax.Precision.HIGHEST
f32 = jnp.float32
VMEM = pl.BlockSpec(memory_space=pltpu.VMEM)
SMEM = pl.BlockSpec(memory_space=pltpu.SMEM)


def dot(a, b):
    return jnp.dot(a, b, precision=highest, preferred_element_type=f32)


def call(kernel, outs, *args, scalars=0, scratch=(), place=VMEM, grant=GRANT_BYTES):
    specs = [SMEM] * scalars + [place] * (len(args) - scalars)
    many = isinstance(outs, tuple)
    return pl.pallas_call(
        kernel,
        out_shape=outs,
        in_specs=specs,
        out_specs=tuple([VMEM] * len(outs)) if many else VMEM,
        scratch_shapes=list(scratch),
        compiler_params=pltpu.CompilerParams(vmem_limit_bytes=grant),
    )(*args)


def split(x):
    high = x.astype(jnp.bfloat16)
    return high, (x - high.astype(f32)).astype(jnp.bfloat16)


def plain_dot(a, b):
    return jnp.dot(a, b, preferred_element_type=f32)


def dot3(a, b):
    tall = a.shape[0]
    high, low = split(a)
    right, rest = split(b)
    both = plain_dot(jnp.concatenate([high, low], 0), right)
    return both[:tall] + (both[tall:] + plain_dot(high, rest))


def note(top):
    return jnp.floor(jnp.log(jnp.maximum(top, 1e-30)) * NOTES).astype(jnp.int32) + 1


def noted_range(number):
    return jnp.exp(number.astype(f32) * (1.0 / NOTES))


def code(x, number):
    unit = LEVELS / noted_range(number)
    return jnp.floor(x * unit + 0.5).astype(jnp.int32).astype(jnp.int16)


def pack_kernel(local, remote, count, gradient, jacobi, tiles, packed, *scratch):
    blocks, others, lives, whole, inverse, coupling, done = scratch
    width = whole.shape[0]
    height = BLOCK + width
    slots = packed.shape[0] // height
    contract = (((1,), (1,)), ((), ()))
    sources = [local, remote, count, jacobi, tiles, gradient]
    targets = [blocks, others, lives, inverse, coupling, whole]
    copies = [
        pltpu.make_async_copy(source, target, done.at[i])
        for i, (source, target) in enumerate(zip(sources, targets))
    ]
    for copy in copies:
        copy.start()
    for copy in copies:
        copy.wait()
    lane = lax.broadcasted_iota(jnp.int32, (width, BLOCK), 1)
    row = lax.broadcasted_iota(jnp.int32, (width, BLOCK), 0)
    notes = jnp.zeros((width, BLOCK), jnp.int32)
    for slot in range(slots):
        block = blocks[slot]
        halves = jnp.concatenate(split(inverse[block]), 0)
        both = lax.dot_general(halves, coupling[slot], contract, preferred_element_type=f32)
        operator = both[:BLOCK] + both[BLOCK:]
        top = jnp.max(jnp.max(jnp.abs(operator), axis=0, keepdims=True), axis=1, keepdims=True)
        columns = pl.ds(pl.multiple_of(block * BLOCK, BLOCK), BLOCK)
        part = whole[:, columns]
        tops = jnp.max(jnp.abs(part), axis=1, keepdims=True)
        at = slot * height
        packed[at : at + BLOCK, :] = code(operator, note(top))
        packed[at + BLOCK : at + height, :] = code(part, note(tops))
        live = jnp.where(slot < lives[0], 1, 0)
        for place, value in enumerate((block, others[slot], live, note(top))):
            here = (lane == place * slots + slot) & (row == 0)
            notes = jnp.where(here, value, notes)
        notes = jnp.where(lane == 4 * slots + slot * width + row, note(tops), notes)
    notes = jnp.sum(notes, axis=0, keepdims=True)
    packed[slots * height :, :] = jnp.broadcast_to(notes, (NOTE_ROWS, BLOCK)).astype(jnp.int16)


def chain_kernel(sources, give, near, far, *refs):
    sends, (operators, tops, held, out) = refs[:-4], refs[-4:]
    groups = near.shape[0]
    width = held.shape[1]
    height = BLOCK + width
    slots = near.shape[1] // height
    half = groups * slots
    total = 2 * half
    share = sends[0].shape[1]
    lane = lax.broadcasted_iota(jnp.int32, (width, BLOCK), 1)
    row = lax.broadcasted_iota(jnp.int32, (width, BLOCK), 0)
    for q in range(total):
        ref = near if q < half else far
        group, slot = divmod(q % half, slots)
        at = slot * height
        high, low = split(ref[group, at : at + BLOCK, :].astype(f32))
        operators[q, :, :BLOCK] = high
        operators[q, :, BLOCK:] = low
        notes = ref[group, slots * height :, :].astype(f32)
        notes = jnp.concatenate([notes] * (width // NOTE_ROWS), 0)
        scale = noted_range(
            jnp.sum(jnp.where(lane == 3 * slots + slot, notes, 0.0), axis=1, keepdims=True)
        )
        tops[q] = jnp.broadcast_to(scale * (1.0 / LEVELS), (width, BLOCK))
        here = lane == 4 * slots + slot * width + row
        scale = noted_range(jnp.sum(jnp.where(here, notes, 0.0), axis=1, keepdims=True))
        part = ref[group, at + BLOCK : at + height, :].astype(f32)
        held[q] = part * (scale * (1.0 / LEVELS))
    held[total] = jnp.zeros((width, BLOCK), f32)
    out[total] = jnp.zeros((width, BLOCK), f32)

    def step(j, carry):
        for q in range(total):
            four = plain_dot(jnp.concatenate(split(held[q]), 0), operators[q])
            value = (four[:width, :BLOCK] + four[width:, :BLOCK]) + (
                four[:width, BLOCK:] + four[width:, BLOCK:]
            )
            out[q] = value * tops[q]
        for q in range(total):
            value = out[sources[q * slots]]
            for i in range(1, slots):
                value += out[sources[q * slots + i]]
            held[q] = value
        for o, send in enumerate(sends):
            for p in range(share):
                send[j, p] = held[give[o * share + p]]
        return carry

    lax.fori_loop(0, ITERS, step, 0)


def shift(x, axis, by):
    size = lax.axis_size(axis)
    return lax.ppermute(x, axis, [(i, (i - by) % size) for i in range(size)])


def whole_pieces(gradient, factor):
    piece = jnp.concatenate([gradient, factor.T], axis=1)
    others = range(1, lax.axis_size("cols"))
    return [piece] + [shift(piece, "cols", o) for o in others]


def chain_gathered(
    gradient, factor, jacobi, tiles, whole_local, whole_remote, count, order, slots
):
    width = gradient.shape[0]
    blocks = jacobi.shape[0]
    devices = lax.axis_size("rows")
    columns = lax.axis_size("cols")
    groups = devices // 2
    height = BLOCK + width
    packed = call(
        pack_kernel,
        jax.ShapeDtypeStruct((slots * height + NOTE_ROWS, BLOCK), jnp.int16),
        whole_local,
        whole_remote,
        count,
        gradient,
        jacobi,
        tiles,
        scratch=[
            pltpu.SMEM(whole_local.shape, jnp.int32),
            pltpu.SMEM(whole_remote.shape, jnp.int32),
            pltpu.SMEM(count.shape, jnp.int32),
            pltpu.VMEM(gradient.shape, f32),
            pltpu.VMEM(jacobi.shape, f32),
            pltpu.VMEM(tiles.shape, tiles.dtype),
            pltpu.SemaphoreType.DMA((6,)),
        ],
        place=pl.BlockSpec(memory_space=pl.ANY),
        grant=WHOLE_BYTES,
    )
    near = [packed] + [shift(packed, "rows", 2 * o) for o in range(1, groups)]
    gradient, factor, _ = lax.optimization_barrier((gradient, factor, packed))
    pieces = whole_pieces(gradient, factor)
    powers = make_powers(pieces)
    near, pieces, powers = lax.optimization_barrier((near, pieces, powers))
    near = jnp.stack(near)
    far = lax.ppermute(near, "rows", [(i, i ^ 1) for i in range(devices)])

    me = lax.axis_index("rows")
    position = jnp.arange(devices, dtype=jnp.int32)
    base = me ^ (position // groups)
    device = (base + 2 * (position % groups)) % devices
    told = jnp.concatenate([x[:, slots * height, :] for x in (near, far)], 0)
    locals_, remotes, lives = (
        told[:, i * slots : (i + 1) * slots].astype(jnp.int32) for i in range(3)
    )
    owner = (remotes // blocks).reshape(-1)
    holder = jnp.broadcast_to(device[:, None], locals_.shape).reshape(-1)
    alive = lives.reshape(-1) > 0
    meets = (
        (owner[:, None] == holder[None, :])
        & (owner[None, :] == holder[:, None])
        & alive[None, :]
    )
    total = devices * slots
    numbers = jnp.arange(total, dtype=jnp.int32)
    partner = jnp.sum(jnp.where(meets, numbers[None, :], 0), axis=1).reshape(devices, slots)
    same = (
        (locals_[:, :, None] == locals_[:, None, :])
        & (lives[:, None, :] > 0)
        & (lives[:, :, None] > 0)
    )
    sources = jnp.where(same, partner[:, None, :], total).reshape(-1)
    share = order.shape[0] // columns
    shape = jax.ShapeDtypeStruct
    sends = call(
        chain_kernel,
        tuple([shape((ITERS, share, width, BLOCK), f32)] * columns),
        sources,
        jnp.where(order < slots, order, total),
        near,
        far,
        scalars=2,
        scratch=[
            pltpu.VMEM((total, BLOCK, 2 * BLOCK), jnp.bfloat16),
            pltpu.VMEM((total, width, BLOCK), f32),
            pltpu.VMEM((total + 1, width, BLOCK), f32),
            pltpu.VMEM((total + 1, width, BLOCK), f32),
        ],
    )
    return list(sends), pieces, powers


def chain_exchanged(gradient, jacobi, tiles, order, local, remote, live):
    width = gradient.shape[0]
    blocks = jacobi.shape[0]
    devices = lax.axis_size("rows")
    owner = remote // blocks
    placing = (
        (local[:, None] == jnp.arange(blocks, dtype=jnp.int32)[None, :]) & live[:, None]
    ).astype(f32)
    meets = live[:, None] & (owner[:, None] == jnp.arange(devices, dtype=jnp.int32)[None, :])
    granted = jnp.sum(jnp.where(meets, local[:, None], 0), axis=0)
    vector = jnp.transpose(gradient.reshape(width, blocks, BLOCK), (1, 0, 2))
    steps = []
    for _ in range(ITERS):
        sent = jnp.einsum("nej,nji->nei", vector, jacobi, precision=highest)[granted]
        incoming = lax.all_to_all(sent, "rows", 0, 0, tiled=True)
        products = jnp.einsum(
            "kej,kji->kei", incoming[owner], tiles.astype(f32), precision=highest
        )
        vector = jnp.einsum("kei,kn->nei", products, placing, precision=highest)
        steps.append(vector)
    columns = lax.axis_size("cols")
    share = order.shape[0] // columns
    chain = jnp.pad(jnp.stack(steps), ((0, 0), (0, share * columns - blocks), (0, 0), (0, 0)))
    return [
        lax.dynamic_slice_in_dim(chain, order[o * share], share, 1) for o in range(columns)
    ]


def gather_sums(sums, s, y, weight):
    y = [weight * value for value in y]
    f = [s[0] + s[1]]
    for j in range(1, ITERS):
        f.append(0.5 * (s[j - 1] + s[j + 1]) + s[j])
    for i in range(ITERS):
        for j in range(i + 1):
            sums[i, j] = sums.get((i, j), 0.0) + y[i] * f[j]
        sums[i, ITERS] = sums.get((i, ITERS), 0.0) + y[i] * s[0]


def flat_sums(sums):
    lane = lax.broadcasted_iota(jnp.int32, (1, BLOCK), 1)
    result = jnp.zeros((1, BLOCK), f32)
    for (i, j), value in sums.items():
        value = jnp.sum(jnp.sum(value, axis=0, keepdims=True), axis=1, keepdims=True)
        here = lane == 16 * i + j
        if j < ITERS:
            here = here | (lane == 16 * j + i)
        result = jnp.where(here, value, result)
    return result


def powers_kernel(turn, *refs):
    pieces, (scaled, powers, scale) = refs[:-3], refs[-3:]
    width = pieces[0].shape[0]
    factor = jnp.concatenate([piece[:, -BLOCK:] for piece in pieces], 0)
    factor = pltpu.roll(factor, turn[0], 1)
    norm = jnp.max(jnp.sum(jnp.abs(factor), axis=1, keepdims=True), axis=0, keepdims=True)
    power = factor / norm
    for _ in range(3):
        power = dot(power, power)
    bound = jnp.sum(jnp.sum(power * power, axis=1, keepdims=True), axis=0, keepdims=True)
    for _ in range(4):
        bound = jnp.sqrt(bound)
    ratio = 2.0 / (STRETCH * bound * norm)
    scale[...] = jnp.broadcast_to(ratio, scale.shape)
    factor = factor * ratio
    scaled[...] = factor

    row = lax.broadcasted_iota(jnp.int32, (width, BLOCK), 0)
    lane = lax.broadcasted_iota(jnp.int32, (width, BLOCK), 1)
    kept = [(row == lane).astype(f32)]
    for k in range(ITERS):
        value = dot(kept[k], factor) - kept[k]
        kept.append(2.0 * value - kept[k - 1] if k else value)
    powers[...] = jnp.concatenate(kept, 0)


def basis_kernel(where, held, powers, jacobi, *refs):
    pieces, (plain, smooth, gram, starts) = refs[:-4], refs[-4:]
    width = pieces[0].shape[0]
    for p in range(starts.shape[0]):
        columns = pl.ds(pl.multiple_of(held[p] * BLOCK, BLOCK), BLOCK)
        starts[p] = jnp.concatenate([piece[:, columns] for piece in pieces], 0)
    sums = {}
    for b in range(jacobi.shape[0]):
        columns = slice(b * BLOCK, (b + 1) * BLOCK)
        whole = jnp.concatenate([piece[:, columns] for piece in pieces], 0)
        s = dot(powers[...], whole)
        y = dot(s[: ITERS * width], jacobi[b])
        plain[b] = s[width:]
        smooth[b] = y
        weight = jnp.where(where[b] < NOWHERE, 0.0, 1.0)
        for r in range(0, width, 8):
            gather_sums(
                sums,
                [s[k * width + r : k * width + r + 8] for k in range(ITERS + 1)],
                [y[k * width + r : k * width + r + 8] for k in range(ITERS)],
                weight,
            )
    gram[...] = flat_sums(sums)


def make_powers(pieces):
    width = pieces[0].shape[0]
    shape = jax.ShapeDtypeStruct
    turn = (BLOCK - width * lax.axis_index("cols")) % BLOCK
    return call(
        powers_kernel,
        (
            shape((BLOCK, BLOCK), f32),
            shape(((ITERS + 1) * width, BLOCK), f32),
            shape((8, BLOCK), f32),
        ),
        turn.astype(jnp.int32).reshape(1),
        *pieces,
        scalars=1,
    )


def mix_kernel(held, used, *refs):
    devices = (len(refs) - 5) // 2
    parts = refs[:devices]
    starts, scaled, jacobi, others, gram = refs[devices : devices + 5]
    backs = refs[devices + 5 :]
    share, width = parts[0].shape[1:3]
    sums = {}
    for p in range(share):
        now = [starts[p]]
        for j in range(ITERS):
            now.append(jnp.concatenate([part[j, p] for part in parts], 0))
        past = None
        chosen = [now[0]]
        for k in range(ITERS):
            left = ITERS - k
            image = dot3(
                scaled[...], jnp.concatenate([now[i] + now[i + 1] for i in range(left)], 1)
            )
            fresh = []
            for i in range(left):
                value = image[:, i * BLOCK : (i + 1) * BLOCK] - now[i]
                fresh.append(2.0 * value - past[i] if k else value)
            past, now = now, fresh
            chosen.append(now[0])
        for o, back in enumerate(backs):
            for k in range(ITERS):
                back[k, p] = chosen[k + 1][o * width : (o + 1) * width]
        soft = dot3(jnp.concatenate(chosen[:ITERS], 0), jacobi[held[p]])
        weight = jnp.where(used[p] > 0, 1.0, 0.0)
        for r in range(0, BLOCK, 8):
            gather_sums(
                sums,
                [value[r : r + 8] for value in chosen],
                [soft[k * BLOCK + r : k * BLOCK + r + 8] for k in range(ITERS)],
                weight,
            )
    gram[...] = jnp.broadcast_to((flat_sums(sums) + others[...])[None], gram.shape)


def finish_kernel(held, where, grams, scale, gradient, plain, smooth, jacobi, *refs):
    backs, (solution, residual, extra, less) = refs[:-4], refs[-4:]
    width = gradient.shape[0]
    blocks = jacobi.shape[0]
    share = backs[0].shape[1]
    none = len(backs) * share
    flat = jnp.sum(grams[:, 0, :], axis=0, keepdims=True)
    row = lax.broadcasted_iota(jnp.int32, (8, BLOCK), 0)
    lane = lax.broadcasted_iota(jnp.int32, (8, BLOCK), 1)
    table = jnp.zeros((8, BLOCK), f32)
    for i in range(ITERS):
        moved = flat if i == 0 else pltpu.roll(flat, BLOCK - 16 * i, 1)
        table = jnp.where((row == i) & (lane <= ITERS), moved, table)
    for p in range(ITERS):
        pivot = table[p : p + 1, :] / table[p : p + 1, p : p + 1]
        table = jnp.where(row == p, pivot, table - table[:, p : p + 1] * pivot)
    steps = [table[j : j + 1, ITERS : ITERS + 1] for j in range(ITERS)]
    takes = []
    for k in range(ITERS + 1):
        value = 0.0
        if k > 0:
            value += steps[k - 1] * (1.0 if k == 1 else 0.5)
        if k < ITERS:
            value += steps[k]
        if k + 1 < ITERS:
            value += 0.5 * steps[k + 1]
        takes.append(jnp.broadcast_to(value, (width, BLOCK)))
    longer = scale[0:1, 0:1]
    gives = [jnp.broadcast_to(longer * step, (width, BLOCK)) for step in steps]

    def combine(weights, values):
        return sum(weight * value for weight, value in zip(weights, values))

    def cut(ref, b):
        return [ref[b, k * width : (k + 1) * width, :] for k in range(ITERS)]

    for n in range(none):
        values = [backs[n // share][k, n % share] for k in range(ITERS)]
        extra[n] = dot3(combine(gives[1:], values), jacobi[held[n]])
        less[n] = combine(takes[1:], values)
    for b in range(blocks):
        columns = slice(b * BLOCK, (b + 1) * BLOCK)
        n = jnp.minimum(where[b], none - 1)
        own = where[b] >= NOWHERE
        y = cut(smooth, b)
        rest = jnp.where(own, combine(gives[1:], y[1:]), extra[n])
        solution[:, columns] = gives[0] * y[0] + rest
        rest = jnp.where(own, combine(takes[1:], cut(plain, b)), less[n])
        start = gradient[:, columns]
        residual[:, columns] = start - takes[0] * start - rest


def on_device(
    gradient,
    width_factor,
    diag_blocks,
    jacobi_inverse,
    coupling_tiles,
    tile_local,
    tile_remote,
    tile_count,
    exchange=False,
):
    width, rows = gradient.shape
    blocks = diag_blocks.shape[0]
    columns = lax.axis_size("cols")
    devices = lax.axis_size("rows")
    slots = tile_local.shape[0] - 1
    live = jnp.arange(slots, dtype=jnp.int32) < tile_count[0]
    lists = (tile_local[:slots], tile_remote[:slots], live)

    gathered = devices * slots * BLOCK * (BLOCK + width) * 2
    noted = slots * (4 + width) <= BLOCK and width % NOTE_ROWS == 0 and devices * blocks < 2**15
    whole = gathered <= GATHER_BYTES and noted and devices % 2 == 0 and not exchange
    units = slots if whole else blocks
    share = -(-units // columns)
    numbers = jnp.arange(columns * share, dtype=jnp.int32)
    dealer = (lax.axis_index("cols") + columns - numbers // share) % columns
    order = dealer * share + numbers % share
    if whole:
        local = lists[0]
        earlier = jnp.arange(slots)[:, None] > jnp.arange(slots)[None, :]
        repeat = jnp.any(earlier & (local[:, None] == local[None, :]), axis=1)
        fit = order[:, None] == jnp.arange(slots, dtype=jnp.int32)[None, :]
        held = jnp.sum(jnp.where(fit, local[None, :], 0), axis=1)
        used = jnp.sum(jnp.where(fit & (live & ~repeat)[None, :], 1, 0), axis=1)
    else:
        held = jnp.minimum(order, blocks - 1)
        used = (order < blocks).astype(jnp.int32)
    mine = (held[None, :] == jnp.arange(blocks, dtype=jnp.int32)[:, None]) & (used > 0)[None, :]
    where = jnp.min(jnp.where(mine, numbers[None, :], NOWHERE), axis=1)
    if whole:
        sends, pieces, powers = chain_gathered(
            gradient,
            width_factor,
            jacobi_inverse,
            coupling_tiles,
            tile_local,
            tile_remote,
            tile_count,
            order,
            slots,
        )
    else:
        sends = chain_exchanged(
            gradient, jacobi_inverse, coupling_tiles[:slots], order, *lists
        )
        pieces = whole_pieces(gradient, width_factor)
        powers = make_powers(pieces)
    scaled, powers, scale = powers
    powers, sends = lax.optimization_barrier((powers, sends))
    parts = [sends[0]]
    for o in range(1, columns):
        parts.append(shift(sends[o], "cols", o))

    shape = jax.ShapeDtypeStruct
    plain, smooth, others, starts = call(
        basis_kernel,
        (
            shape((blocks, ITERS * width, BLOCK), f32),
            shape((blocks, ITERS * width, BLOCK), f32),
            shape((1, BLOCK), f32),
            shape((share, BLOCK, BLOCK), f32),
        ),
        where,
        held,
        powers,
        jacobi_inverse,
        *pieces,
        scalars=2,
    )
    gram, *backs = call(
        mix_kernel,
        tuple(
            [shape((columns * devices, 1, BLOCK), f32)]
            + [shape((ITERS, share, width, BLOCK), f32)] * columns
        ),
        held,
        used,
        *parts,
        starts,
        scaled,
        jacobi_inverse,
        others,
        scalars=2,
    )
    grams = lax.all_to_all(gram, ("cols", "rows"), 0, 0, tiled=True)
    for o in range(1, columns):
        backs[o] = shift(backs[o], "cols", -o)
    return call(
        finish_kernel,
        (shape((width, rows), f32), shape((width, rows), f32)),
        held,
        where,
        grams,
        scale,
        gradient,
        plain,
        smooth,
        jacobi_inverse,
        *backs,
        scalars=2,
        scratch=[pltpu.VMEM((columns * share, width, BLOCK), f32)] * 2,
    )


def solution(mesh):
    placed = (
        P("cols", "rows"),
        P(None, "cols"),
        P("rows", None, None),
        P("rows", None, None),
        P("rows", None, None),
        P("rows"),
        P("rows"),
        P("rows"),
    )

    return jax.shard_map(
        on_device,
        mesh=mesh,
        in_specs=placed,
        out_specs=(P("cols", "rows"), P("cols", "rows")),
        check_vma=False,
    )
```

```python
import jax
import jax.numpy as jnp
from jax import lax
from jax.experimental import pallas as pl
from jax.experimental.pallas import tpu as pltpu
from jax.sharding import PartitionSpec as P


BLOCK = 128
ITERS = 6
STRETCH = 1.1
GATHER_BYTES = 8 * 2**20


NOWHERE = 2**20
LEVELS = 32700.0
NOTES = 256 / 0.6931471805599453
NOTE_ROWS = 16
GRANT_BYTES = 24 * 2**20
WHOLE_BYTES = 60 * 2**20

highest = lax.Precision.HIGHEST
f32 = jnp.float32
VMEM = pl.BlockSpec(memory_space=pltpu.VMEM)
SMEM = pl.BlockSpec(memory_space=pltpu.SMEM)


def dot(a, b):
    return jnp.dot(a, b, precision=highest, preferred_element_type=f32)


def call(kernel, outs, *args, scalars=0, scratch=(), place=VMEM, grant=GRANT_BYTES):
    specs = [SMEM] * scalars + [place] * (len(args) - scalars)
    many = isinstance(outs, tuple)
    return pl.pallas_call(
        kernel,
        out_shape=outs,
        in_specs=specs,
        out_specs=tuple([VMEM] * len(outs)) if many else VMEM,
        scratch_shapes=list(scratch),
        compiler_params=pltpu.CompilerParams(vmem_limit_bytes=grant),
    )(*args)


def split(x):
    high = x.astype(jnp.bfloat16)
    return high, (x - high.astype(f32)).astype(jnp.bfloat16)


def plain_dot(a, b):
    return jnp.dot(a, b, preferred_element_type=f32)


def dot3(a, b):
    tall = a.shape[0]
    high, low = split(a)
    right, rest = split(b)
    both = plain_dot(jnp.concatenate([high, low], 0), right)
    return both[:tall] + (both[tall:] + plain_dot(high, rest))


def note(top):
    return jnp.floor(jnp.log(jnp.maximum(top, 1e-30)) * NOTES).astype(jnp.int32) + 1


def noted_range(number):
    return jnp.exp(number.astype(f32) * (1.0 / NOTES))


def code(x, number):
    unit = LEVELS / noted_range(number)
    return jnp.floor(x * unit + 0.5).astype(jnp.int32).astype(jnp.int16)


def pack_kernel(local, remote, count, gradient, jacobi, tiles, packed, *scratch):
    blocks, others, lives, whole, inverse, coupling, done = scratch
    width = whole.shape[0]
    height = BLOCK + width
    slots = packed.shape[0] // height
    contract = (((1,), (1,)), ((), ()))
    sources = [local, remote, count, jacobi, tiles, gradient]
    targets = [blocks, others, lives, inverse, coupling, whole]
    copies = [
        pltpu.make_async_copy(source, target, done.at[i])
        for i, (source, target) in enumerate(zip(sources, targets))
    ]
    for copy in copies:
        copy.start()
    for copy in copies:
        copy.wait()
    lane = lax.broadcasted_iota(jnp.int32, (width, BLOCK), 1)
    row = lax.broadcasted_iota(jnp.int32, (width, BLOCK), 0)
    notes = jnp.zeros((width, BLOCK), jnp.int32)
    for slot in range(slots):
        block = blocks[slot]
        halves = jnp.concatenate(split(inverse[block]), 0)
        both = lax.dot_general(halves, coupling[slot], contract, preferred_element_type=f32)
        operator = both[:BLOCK] + both[BLOCK:]
        top = jnp.max(jnp.max(jnp.abs(operator), axis=0, keepdims=True), axis=1, keepdims=True)
        columns = pl.ds(pl.multiple_of(block * BLOCK, BLOCK), BLOCK)
        part = whole[:, columns]
        tops = jnp.max(jnp.abs(part), axis=1, keepdims=True)
        at = slot * height
        packed[at : at + BLOCK, :] = code(operator, note(top))
        packed[at + BLOCK : at + height, :] = code(part, note(tops))
        live = jnp.where(slot < lives[0], 1, 0)
        for place, value in enumerate((block, others[slot], live, note(top))):
            here = (lane == place * slots + slot) & (row == 0)
            notes = jnp.where(here, value, notes)
        notes = jnp.where(lane == 4 * slots + slot * width + row, note(tops), notes)
    notes = jnp.sum(notes, axis=0, keepdims=True)
    packed[slots * height :, :] = jnp.broadcast_to(notes, (NOTE_ROWS, BLOCK)).astype(jnp.int16)


def chain_kernel(sources, give, near, far, *refs):
    sends, (operators, tops, held, out) = refs[:-4], refs[-4:]
    groups = near.shape[0]
    width = held.shape[1]
    height = BLOCK + width
    slots = near.shape[1] // height
    half = groups * slots
    total = 2 * half
    share = sends[0].shape[1]
    lane = lax.broadcasted_iota(jnp.int32, (width, BLOCK), 1)
    row = lax.broadcasted_iota(jnp.int32, (width, BLOCK), 0)
    for q in range(total):
        ref = near if q < half else far
        group, slot = divmod(q % half, slots)
        at = slot * height
        high, low = split(ref[group, at : at + BLOCK, :].astype(f32))
        operators[q, :, :BLOCK] = high
        operators[q, :, BLOCK:] = low
        notes = ref[group, slots * height :, :].astype(f32)
        notes = jnp.concatenate([notes] * (width // NOTE_ROWS), 0)
        scale = noted_range(
            jnp.sum(jnp.where(lane == 3 * slots + slot, notes, 0.0), axis=1, keepdims=True)
        )
        tops[q] = jnp.broadcast_to(scale * (1.0 / LEVELS), (width, BLOCK))
        here = lane == 4 * slots + slot * width + row
        scale = noted_range(jnp.sum(jnp.where(here, notes, 0.0), axis=1, keepdims=True))
        part = ref[group, at + BLOCK : at + height, :].astype(f32)
        held[q] = part * (scale * (1.0 / LEVELS))
    held[total] = jnp.zeros((width, BLOCK), f32)
    out[total] = jnp.zeros((width, BLOCK), f32)

    def step(j, carry):
        for q in range(total):
            four = plain_dot(jnp.concatenate(split(held[q]), 0), operators[q])
            value = (four[:width, :BLOCK] + four[width:, :BLOCK]) + (
                four[:width, BLOCK:] + four[width:, BLOCK:]
            )
            out[q] = value * tops[q]
        for q in range(total):
            value = out[sources[q * slots]]
            for i in range(1, slots):
                value += out[sources[q * slots + i]]
            held[q] = value
        for o, send in enumerate(sends):
            for p in range(share):
                send[j, p] = held[give[o * share + p]]
        return carry

    lax.fori_loop(0, ITERS, step, 0)


def shift(x, axis, by):
    size = lax.axis_size(axis)
    return lax.ppermute(x, axis, [(i, (i - by) % size) for i in range(size)])


def whole_pieces(gradient, factor):
    piece = jnp.concatenate([gradient, factor.T], axis=1)
    others = range(1, lax.axis_size("cols"))
    return [piece] + [shift(piece, "cols", o) for o in others]


def chain_gathered(
    gradient, factor, jacobi, tiles, whole_local, whole_remote, count, order, slots
):
    width = gradient.shape[0]
    blocks = jacobi.shape[0]
    devices = lax.axis_size("rows")
    columns = lax.axis_size("cols")
    groups = devices // 2
    height = BLOCK + width
    packed = call(
        pack_kernel,
        jax.ShapeDtypeStruct((slots * height + NOTE_ROWS, BLOCK), jnp.int16),
        whole_local,
        whole_remote,
        count,
        gradient,
        jacobi,
        tiles,
        scratch=[
            pltpu.SMEM(whole_local.shape, jnp.int32),
            pltpu.SMEM(whole_remote.shape, jnp.int32),
            pltpu.SMEM(count.shape, jnp.int32),
            pltpu.VMEM(gradient.shape, f32),
            pltpu.VMEM(jacobi.shape, f32),
            pltpu.VMEM(tiles.shape, tiles.dtype),
            pltpu.SemaphoreType.DMA((6,)),
        ],
        place=pl.BlockSpec(memory_space=pl.ANY),
        grant=WHOLE_BYTES,
    )
    near = [packed] + [shift(packed, "rows", 2 * o) for o in range(1, groups)]
    gradient, factor, _ = lax.optimization_barrier((gradient, factor, packed))
    pieces = whole_pieces(gradient, factor)
    near = jnp.stack(near)
    far = lax.ppermute(near, "rows", [(i, i ^ 1) for i in range(devices)])
    powers = make_powers(pieces)
    far, pieces, powers = lax.optimization_barrier((far, pieces, powers))

    me = lax.axis_index("rows")
    position = jnp.arange(devices, dtype=jnp.int32)
    base = me ^ (position // groups)
    device = (base + 2 * (position % groups)) % devices
    told = jnp.concatenate([x[:, slots * height, :] for x in (near, far)], 0)
    locals_, remotes, lives = (
        told[:, i * slots : (i + 1) * slots].astype(jnp.int32) for i in range(3)
    )
    owner = (remotes // blocks).reshape(-1)
    holder = jnp.broadcast_to(device[:, None], locals_.shape).reshape(-1)
    alive = lives.reshape(-1) > 0
    meets = (
        (owner[:, None] == holder[None, :])
        & (owner[None, :] == holder[:, None])
        & alive[None, :]
    )
    total = devices * slots
    numbers = jnp.arange(total, dtype=jnp.int32)
    partner = jnp.sum(jnp.where(meets, numbers[None, :], 0), axis=1).reshape(devices, slots)
    same = (
        (locals_[:, :, None] == locals_[:, None, :])
        & (lives[:, None, :] > 0)
        & (lives[:, :, None] > 0)
    )
    sources = jnp.where(same, partner[:, None, :], total).reshape(-1)
    share = order.shape[0] // columns
    shape = jax.ShapeDtypeStruct
    sends = call(
        chain_kernel,
        tuple([shape((ITERS, share, width, BLOCK), f32)] * columns),
        sources,
        jnp.where(order < slots, order, total),
        near,
        far,
        scalars=2,
        scratch=[
            pltpu.VMEM((total, BLOCK, 2 * BLOCK), jnp.bfloat16),
            pltpu.VMEM((total, width, BLOCK), f32),
            pltpu.VMEM((total + 1, width, BLOCK), f32),
            pltpu.VMEM((total + 1, width, BLOCK), f32),
        ],
    )
    return list(sends), pieces, powers


def chain_exchanged(gradient, jacobi, tiles, order, local, remote, live):
    width = gradient.shape[0]
    blocks = jacobi.shape[0]
    devices = lax.axis_size("rows")
    owner = remote // blocks
    placing = (
        (local[:, None] == jnp.arange(blocks, dtype=jnp.int32)[None, :]) & live[:, None]
    ).astype(f32)
    meets = live[:, None] & (owner[:, None] == jnp.arange(devices, dtype=jnp.int32)[None, :])
    granted = jnp.sum(jnp.where(meets, local[:, None], 0), axis=0)
    vector = jnp.transpose(gradient.reshape(width, blocks, BLOCK), (1, 0, 2))
    steps = []
    for _ in range(ITERS):
        sent = jnp.einsum("nej,nji->nei", vector, jacobi, precision=highest)[granted]
        incoming = lax.all_to_all(sent, "rows", 0, 0, tiled=True)
        products = jnp.einsum(
            "kej,kji->kei", incoming[owner], tiles.astype(f32), precision=highest
        )
        vector = jnp.einsum("kei,kn->nei", products, placing, precision=highest)
        steps.append(vector)
    columns = lax.axis_size("cols")
    share = order.shape[0] // columns
    chain = jnp.pad(jnp.stack(steps), ((0, 0), (0, share * columns - blocks), (0, 0), (0, 0)))
    return [
        lax.dynamic_slice_in_dim(chain, order[o * share], share, 1) for o in range(columns)
    ]


def gather_sums(sums, s, y, weight):
    y = [weight * value for value in y]
    f = [s[0] + s[1]]
    for j in range(1, ITERS):
        f.append(0.5 * (s[j - 1] + s[j + 1]) + s[j])
    for i in range(ITERS):
        for j in range(i + 1):
            sums[i, j] = sums.get((i, j), 0.0) + y[i] * f[j]
        sums[i, ITERS] = sums.get((i, ITERS), 0.0) + y[i] * s[0]


def flat_sums(sums):
    lane = lax.broadcasted_iota(jnp.int32, (1, BLOCK), 1)
    result = jnp.zeros((1, BLOCK), f32)
    for (i, j), value in sums.items():
        value = jnp.sum(jnp.sum(value, axis=0, keepdims=True), axis=1, keepdims=True)
        here = lane == 16 * i + j
        if j < ITERS:
            here = here | (lane == 16 * j + i)
        result = jnp.where(here, value, result)
    return result


def powers_kernel(turn, *refs):
    pieces, (scaled, powers, scale) = refs[:-3], refs[-3:]
    width = pieces[0].shape[0]
    factor = jnp.concatenate([piece[:, -BLOCK:] for piece in pieces], 0)
    factor = pltpu.roll(factor, turn[0], 1)
    norm = jnp.max(jnp.sum(jnp.abs(factor), axis=1, keepdims=True), axis=0, keepdims=True)
    power = factor / norm
    for _ in range(3):
        power = dot3(power, power)
    bound = jnp.sum(jnp.sum(power * power, axis=1, keepdims=True), axis=0, keepdims=True)
    for _ in range(4):
        bound = jnp.sqrt(bound)
    ratio = 2.0 / (STRETCH * bound * norm)
    scale[...] = jnp.broadcast_to(ratio, scale.shape)
    factor = factor * ratio
    scaled[...] = factor

    row = lax.broadcasted_iota(jnp.int32, (width, BLOCK), 0)
    lane = lax.broadcasted_iota(jnp.int32, (width, BLOCK), 1)
    kept = [(row == lane).astype(f32)]
    for k in range(ITERS):
        value = dot(kept[k], factor) - kept[k]
        kept.append(2.0 * value - kept[k - 1] if k else value)
    powers[...] = jnp.concatenate(kept, 0)


def basis_kernel(where, held, powers, jacobi, *refs):
    pieces, (plain, smooth, gram, starts) = refs[:-4], refs[-4:]
    width = pieces[0].shape[0]
    for p in range(starts.shape[0]):
        columns = pl.ds(pl.multiple_of(held[p] * BLOCK, BLOCK), BLOCK)
        starts[p] = jnp.concatenate([piece[:, columns] for piece in pieces], 0)
    sums = {}
    for b in range(jacobi.shape[0]):
        columns = slice(b * BLOCK, (b + 1) * BLOCK)
        whole = jnp.concatenate([piece[:, columns] for piece in pieces], 0)
        s = dot3(powers[...], whole)
        y = dot3(s[: ITERS * width], jacobi[b])
        plain[b] = s[width:]
        smooth[b] = y
        weight = jnp.where(where[b] < NOWHERE, 0.0, 1.0)
        for r in range(0, width, 8):
            gather_sums(
                sums,
                [s[k * width + r : k * width + r + 8] for k in range(ITERS + 1)],
                [y[k * width + r : k * width + r + 8] for k in range(ITERS)],
                weight,
            )
    gram[...] = flat_sums(sums)


def make_powers(pieces):
    width = pieces[0].shape[0]
    shape = jax.ShapeDtypeStruct
    turn = (BLOCK - width * lax.axis_index("cols")) % BLOCK
    return call(
        powers_kernel,
        (
            shape((BLOCK, BLOCK), f32),
            shape(((ITERS + 1) * width, BLOCK), f32),
            shape((8, BLOCK), f32),
        ),
        turn.astype(jnp.int32).reshape(1),
        *pieces,
        scalars=1,
    )


def mix_kernel(held, used, *refs):
    devices = (len(refs) - 5) // 2
    parts = refs[:devices]
    starts, scaled, jacobi, others, gram = refs[devices : devices + 5]
    backs = refs[devices + 5 :]
    share, width = parts[0].shape[1:3]
    sums = {}
    for p in range(share):
        now = [starts[p]]
        for j in range(ITERS):
            now.append(jnp.concatenate([part[j, p] for part in parts], 0))
        past = None
        chosen = [now[0]]
        for k in range(ITERS):
            left = ITERS - k
            image = dot3(
                scaled[...], jnp.concatenate([now[i] + now[i + 1] for i in range(left)], 1)
            )
            fresh = []
            for i in range(left):
                value = image[:, i * BLOCK : (i + 1) * BLOCK] - now[i]
                fresh.append(2.0 * value - past[i] if k else value)
            past, now = now, fresh
            chosen.append(now[0])
        for o, back in enumerate(backs):
            for k in range(ITERS):
                back[k, p] = chosen[k + 1][o * width : (o + 1) * width]
        soft = dot3(jnp.concatenate(chosen[:ITERS], 0), jacobi[held[p]])
        weight = jnp.where(used[p] > 0, 1.0, 0.0)
        for r in range(0, BLOCK, 8):
            gather_sums(
                sums,
                [value[r : r + 8] for value in chosen],
                [soft[k * BLOCK + r : k * BLOCK + r + 8] for k in range(ITERS)],
                weight,
            )
    gram[...] = jnp.broadcast_to((flat_sums(sums) + others[...])[None], gram.shape)


def finish_kernel(held, where, grams, scale, gradient, plain, smooth, jacobi, *refs):
    backs, (solution, residual, extra, less) = refs[:-4], refs[-4:]
    width = gradient.shape[0]
    blocks = jacobi.shape[0]
    share = backs[0].shape[1]
    none = len(backs) * share
    flat = jnp.sum(grams[:, 0, :], axis=0, keepdims=True)
    row = lax.broadcasted_iota(jnp.int32, (8, BLOCK), 0)
    lane = lax.broadcasted_iota(jnp.int32, (8, BLOCK), 1)
    table = jnp.zeros((8, BLOCK), f32)
    for i in range(ITERS):
        moved = flat if i == 0 else pltpu.roll(flat, BLOCK - 16 * i, 1)
        table = jnp.where((row == i) & (lane <= ITERS), moved, table)
    for p in range(ITERS):
        pivot = table[p : p + 1, :] / table[p : p + 1, p : p + 1]
        table = jnp.where(row == p, pivot, table - table[:, p : p + 1] * pivot)
    steps = [table[j : j + 1, ITERS : ITERS + 1] for j in range(ITERS)]
    takes = []
    for k in range(ITERS + 1):
        value = 0.0
        if k > 0:
            value += steps[k - 1] * (1.0 if k == 1 else 0.5)
        if k < ITERS:
            value += steps[k]
        if k + 1 < ITERS:
            value += 0.5 * steps[k + 1]
        takes.append(jnp.broadcast_to(value, (width, BLOCK)))
    longer = scale[0:1, 0:1]
    gives = [jnp.broadcast_to(longer * step, (width, BLOCK)) for step in steps]

    def combine(weights, values):
        return sum(weight * value for weight, value in zip(weights, values))

    def cut(ref, b):
        return [ref[b, k * width : (k + 1) * width, :] for k in range(ITERS)]

    for n in range(none):
        values = [backs[n // share][k, n % share] for k in range(ITERS)]
        extra[n] = dot3(combine(gives[1:], values), jacobi[held[n]])
        less[n] = combine(takes[1:], values)
    for b in range(blocks):
        columns = slice(b * BLOCK, (b + 1) * BLOCK)
        n = jnp.minimum(where[b], none - 1)
        own = where[b] >= NOWHERE
        y = cut(smooth, b)
        rest = jnp.where(own, combine(gives[1:], y[1:]), extra[n])
        solution[:, columns] = gives[0] * y[0] + rest
        rest = jnp.where(own, combine(takes[1:], cut(plain, b)), less[n])
        start = gradient[:, columns]
        residual[:, columns] = start - takes[0] * start - rest


def on_device(
    gradient,
    width_factor,
    diag_blocks,
    jacobi_inverse,
    coupling_tiles,
    tile_local,
    tile_remote,
    tile_count,
    exchange=False,
):
    width, rows = gradient.shape
    blocks = diag_blocks.shape[0]
    columns = lax.axis_size("cols")
    devices = lax.axis_size("rows")
    slots = tile_local.shape[0] - 1
    live = jnp.arange(slots, dtype=jnp.int32) < tile_count[0]
    lists = (tile_local[:slots], tile_remote[:slots], live)

    gathered = devices * slots * BLOCK * (BLOCK + width) * 2
    noted = slots * (4 + width) <= BLOCK and width % NOTE_ROWS == 0 and devices * blocks < 2**15
    whole = gathered <= GATHER_BYTES and noted and devices % 2 == 0 and not exchange
    units = slots if whole else blocks
    share = -(-units // columns)
    numbers = jnp.arange(columns * share, dtype=jnp.int32)
    dealer = (lax.axis_index("cols") + columns - numbers // share) % columns
    order = dealer * share + numbers % share
    if whole:
        local = lists[0]
        earlier = jnp.arange(slots)[:, None] > jnp.arange(slots)[None, :]
        repeat = jnp.any(earlier & (local[:, None] == local[None, :]), axis=1)
        fit = order[:, None] == jnp.arange(slots, dtype=jnp.int32)[None, :]
        held = jnp.sum(jnp.where(fit, local[None, :], 0), axis=1)
        used = jnp.sum(jnp.where(fit & (live & ~repeat)[None, :], 1, 0), axis=1)
    else:
        held = jnp.minimum(order, blocks - 1)
        used = (order < blocks).astype(jnp.int32)
    mine = (held[None, :] == jnp.arange(blocks, dtype=jnp.int32)[:, None]) & (used > 0)[None, :]
    where = jnp.min(jnp.where(mine, numbers[None, :], NOWHERE), axis=1)
    if whole:
        sends, pieces, powers = chain_gathered(
            gradient,
            width_factor,
            jacobi_inverse,
            coupling_tiles,
            tile_local,
            tile_remote,
            tile_count,
            order,
            slots,
        )
    else:
        sends = chain_exchanged(
            gradient, jacobi_inverse, coupling_tiles[:slots], order, *lists
        )
        pieces = whole_pieces(gradient, width_factor)
        powers = make_powers(pieces)
    scaled, powers, scale = powers
    powers, sends = lax.optimization_barrier((powers, sends))
    parts = [sends[0]]
    for o in range(1, columns):
        parts.append(shift(sends[o], "cols", o))

    shape = jax.ShapeDtypeStruct
    plain, smooth, others, starts = call(
        basis_kernel,
        (
            shape((blocks, ITERS * width, BLOCK), f32),
            shape((blocks, ITERS * width, BLOCK), f32),
            shape((1, BLOCK), f32),
            shape((share, BLOCK, BLOCK), f32),
        ),
        where,
        held,
        powers,
        jacobi_inverse,
        *pieces,
        scalars=2,
    )
    gram, *backs = call(
        mix_kernel,
        tuple(
            [shape((columns * devices, 1, BLOCK), f32)]
            + [shape((ITERS, share, width, BLOCK), f32)] * columns
        ),
        held,
        used,
        *parts,
        starts,
        scaled,
        jacobi_inverse,
        others,
        scalars=2,
    )
    grams = lax.all_to_all(gram, ("cols", "rows"), 0, 0, tiled=True)
    for o in range(1, columns):
        backs[o] = shift(backs[o], "cols", -o)
    return call(
        finish_kernel,
        (shape((width, rows), f32), shape((width, rows), f32)),
        held,
        where,
        grams,
        scale,
        gradient,
        plain,
        smooth,
        jacobi_inverse,
        *backs,
        scalars=2,
        scratch=[pltpu.VMEM((columns * share, width, BLOCK), f32)] * 2,
    )


def solution(mesh):
    placed = (
        P("cols", "rows"),
        P(None, "cols"),
        P("rows", None, None),
        P("rows", None, None),
        P("rows", None, None),
        P("rows"),
        P("rows"),
        P("rows"),
    )

    return jax.shard_map(
        on_device,
        mesh=mesh,
        in_specs=placed,
        out_specs=(P("cols", "rows"), P("cols", "rows")),
        check_vma=False,
    )
```

```python
import jax
import jax.numpy as jnp
from jax import lax
from jax.experimental import pallas as pl
from jax.experimental.pallas import tpu as pltpu
from jax.sharding import PartitionSpec as P


BLOCK = 128
ITERS = 6
STRETCH = 1.1
GATHER_BYTES = 8 * 2**20


NOWHERE = 2**20
LEVELS = 32700.0
NOTES = 256 / 0.6931471805599453
NOTE_ROWS = 16
GRANT_BYTES = 24 * 2**20
WHOLE_BYTES = 60 * 2**20

highest = lax.Precision.HIGHEST
f32 = jnp.float32
VMEM = pl.BlockSpec(memory_space=pltpu.VMEM)
SMEM = pl.BlockSpec(memory_space=pltpu.SMEM)


def dot(a, b):
    return jnp.dot(a, b, precision=highest, preferred_element_type=f32)


def call(kernel, outs, *args, scalars=0, scratch=(), place=VMEM, grant=GRANT_BYTES):
    specs = [SMEM] * scalars + [place] * (len(args) - scalars)
    many = isinstance(outs, tuple)
    return pl.pallas_call(
        kernel,
        out_shape=outs,
        in_specs=specs,
        out_specs=tuple([VMEM] * len(outs)) if many else VMEM,
        scratch_shapes=list(scratch),
        compiler_params=pltpu.CompilerParams(vmem_limit_bytes=grant),
    )(*args)


def split(x):
    high = x.astype(jnp.bfloat16)
    return high, (x - high.astype(f32)).astype(jnp.bfloat16)


def plain_dot(a, b):
    return jnp.dot(a, b, preferred_element_type=f32)


def dot3(a, b):
    tall = a.shape[0]
    high, low = split(a)
    right, rest = split(b)
    both = plain_dot(jnp.concatenate([high, low], 0), right)
    return both[:tall] + (both[tall:] + plain_dot(high, rest))


def note(top):
    return jnp.floor(jnp.log(jnp.maximum(top, 1e-30)) * NOTES).astype(jnp.int32) + 1


def noted_range(number):
    return jnp.exp(number.astype(f32) * (1.0 / NOTES))


def code(x, number):
    unit = LEVELS / noted_range(number)
    return jnp.floor(x * unit + 0.5).astype(jnp.int32).astype(jnp.int16)


def pack_kernel(local, remote, count, gradient, jacobi, tiles, packed, *scratch):
    blocks, others, lives, whole, inverse, coupling, done = scratch
    width = whole.shape[0]
    height = BLOCK + width
    slots = packed.shape[0] // height
    contract = (((1,), (1,)), ((), ()))
    sources = [local, remote, count, jacobi, tiles, gradient]
    targets = [blocks, others, lives, inverse, coupling, whole]
    copies = [
        pltpu.make_async_copy(source, target, done.at[i])
        for i, (source, target) in enumerate(zip(sources, targets))
    ]
    for copy in copies:
        copy.start()
    for copy in copies:
        copy.wait()
    lane = lax.broadcasted_iota(jnp.int32, (width, BLOCK), 1)
    row = lax.broadcasted_iota(jnp.int32, (width, BLOCK), 0)
    notes = jnp.zeros((width, BLOCK), jnp.int32)
    for slot in range(slots):
        block = blocks[slot]
        halves = jnp.concatenate(split(inverse[block]), 0)
        both = lax.dot_general(halves, coupling[slot], contract, preferred_element_type=f32)
        operator = both[:BLOCK] + both[BLOCK:]
        top = jnp.max(jnp.max(jnp.abs(operator), axis=0, keepdims=True), axis=1, keepdims=True)
        columns = pl.ds(pl.multiple_of(block * BLOCK, BLOCK), BLOCK)
        part = whole[:, columns]
        tops = jnp.max(jnp.abs(part), axis=1, keepdims=True)
        at = slot * height
        packed[at : at + BLOCK, :] = code(operator, note(top))
        packed[at + BLOCK : at + height, :] = code(part, note(tops))
        live = jnp.where(slot < lives[0], 1, 0)
        for place, value in enumerate((block, others[slot], live, note(top))):
            here = (lane == place * slots + slot) & (row == 0)
            notes = jnp.where(here, value, notes)
        notes = jnp.where(lane == 4 * slots + slot * width + row, note(tops), notes)
    notes = jnp.sum(notes, axis=0, keepdims=True)
    packed[slots * height :, :] = jnp.broadcast_to(notes, (NOTE_ROWS, BLOCK)).astype(jnp.int16)


def chain_kernel(sources, give, near, far, *refs):
    sends, (operators, tops, held, out) = refs[:-4], refs[-4:]
    groups = near.shape[0]
    width = held.shape[1]
    height = BLOCK + width
    slots = near.shape[1] // height
    half = groups * slots
    total = 2 * half
    share = sends[0].shape[1]
    lane = lax.broadcasted_iota(jnp.int32, (width, BLOCK), 1)
    row = lax.broadcasted_iota(jnp.int32, (width, BLOCK), 0)
    for q in range(total):
        ref = near if q < half else far
        group, slot = divmod(q % half, slots)
        at = slot * height
        high, low = split(ref[group, at : at + BLOCK, :].astype(f32))
        operators[q, :, :BLOCK] = high
        operators[q, :, BLOCK:] = low
        notes = ref[group, slots * height :, :].astype(f32)
        notes = jnp.concatenate([notes] * (width // NOTE_ROWS), 0)
        scale = noted_range(
            jnp.sum(jnp.where(lane == 3 * slots + slot, notes, 0.0), axis=1, keepdims=True)
        )
        tops[q] = jnp.broadcast_to(scale * (1.0 / LEVELS), (width, BLOCK))
        here = lane == 4 * slots + slot * width + row
        scale = noted_range(jnp.sum(jnp.where(here, notes, 0.0), axis=1, keepdims=True))
        part = ref[group, at + BLOCK : at + height, :].astype(f32)
        held[q] = part * (scale * (1.0 / LEVELS))
    held[total] = jnp.zeros((width, BLOCK), f32)
    out[total] = jnp.zeros((width, BLOCK), f32)

    def step(j, carry):
        for q in range(total):
            four = plain_dot(jnp.concatenate(split(held[q]), 0), operators[q])
            value = (four[:width, :BLOCK] + four[width:, :BLOCK]) + (
                four[:width, BLOCK:] + four[width:, BLOCK:]
            )
            out[q] = value * tops[q]
        for q in range(total):
            value = out[sources[q * slots]]
            for i in range(1, slots):
                value += out[sources[q * slots + i]]
            held[q] = value
        for o, send in enumerate(sends):
            for p in range(share):
                send[j, p] = held[give[o * share + p]]
        return carry

    lax.fori_loop(0, ITERS, step, 0)


def shift(x, axis, by):
    size = lax.axis_size(axis)
    return lax.ppermute(x, axis, [(i, (i - by) % size) for i in range(size)])


def whole_pieces(x):
    others = range(1, lax.axis_size("cols"))
    return [x] + [shift(x, "cols", o) for o in others]


def chain_gathered(
    gradient, factor, jacobi, tiles, whole_local, whole_remote, count, order, slots
):
    width = gradient.shape[0]
    blocks = jacobi.shape[0]
    devices = lax.axis_size("rows")
    columns = lax.axis_size("cols")
    groups = devices // 2
    height = BLOCK + width
    packed = call(
        pack_kernel,
        jax.ShapeDtypeStruct((slots * height + NOTE_ROWS, BLOCK), jnp.int16),
        whole_local,
        whole_remote,
        count,
        gradient,
        jacobi,
        tiles,
        scratch=[
            pltpu.SMEM(whole_local.shape, jnp.int32),
            pltpu.SMEM(whole_remote.shape, jnp.int32),
            pltpu.SMEM(count.shape, jnp.int32),
            pltpu.VMEM(gradient.shape, f32),
            pltpu.VMEM(jacobi.shape, f32),
            pltpu.VMEM(tiles.shape, tiles.dtype),
            pltpu.SemaphoreType.DMA((6,)),
        ],
        place=pl.BlockSpec(memory_space=pl.ANY),
        grant=WHOLE_BYTES,
    )
    near = [packed] + [shift(packed, "rows", 2 * o) for o in range(1, groups)]
    gradient, factor, _ = lax.optimization_barrier((gradient, factor, packed))
    factors = whole_pieces(factor.T)
    pieces = whole_pieces(gradient)
    powers = make_powers(factors)
    near, powers = lax.optimization_barrier((near, powers))
    near = jnp.stack(near)
    swap = [(i, i ^ 1) for i in range(devices)]
    noted = near[:, slots * height :, :]
    told = lax.ppermute(noted, "rows", swap)
    far = lax.ppermute(near, "rows", swap)
    told = jnp.concatenate([noted[:, 0], told[:, 0]], 0)

    me = lax.axis_index("rows")
    position = jnp.arange(devices, dtype=jnp.int32)
    base = me ^ (position // groups)
    device = (base + 2 * (position % groups)) % devices
    locals_, remotes, lives = (
        told[:, i * slots : (i + 1) * slots].astype(jnp.int32) for i in range(3)
    )
    owner = (remotes // blocks).reshape(-1)
    holder = jnp.broadcast_to(device[:, None], locals_.shape).reshape(-1)
    alive = lives.reshape(-1) > 0
    meets = (
        (owner[:, None] == holder[None, :])
        & (owner[None, :] == holder[:, None])
        & alive[None, :]
    )
    total = devices * slots
    numbers = jnp.arange(total, dtype=jnp.int32)
    partner = jnp.sum(jnp.where(meets, numbers[None, :], 0), axis=1).reshape(devices, slots)
    same = (
        (locals_[:, :, None] == locals_[:, None, :])
        & (lives[:, None, :] > 0)
        & (lives[:, :, None] > 0)
    )
    sources = jnp.where(same, partner[:, None, :], total).reshape(-1)
    share = order.shape[0] // columns
    shape = jax.ShapeDtypeStruct
    sends = call(
        chain_kernel,
        tuple([shape((ITERS, share, width, BLOCK), f32)] * columns),
        sources,
        jnp.where(order < slots, order, total),
        near,
        far,
        scalars=2,
        scratch=[
            pltpu.VMEM((total, BLOCK, 2 * BLOCK), jnp.bfloat16),
            pltpu.VMEM((total, width, BLOCK), f32),
            pltpu.VMEM((total + 1, width, BLOCK), f32),
            pltpu.VMEM((total + 1, width, BLOCK), f32),
        ],
    )
    return list(sends), pieces, powers


def chain_exchanged(gradient, jacobi, tiles, order, local, remote, live):
    width = gradient.shape[0]
    blocks = jacobi.shape[0]
    devices = lax.axis_size("rows")
    owner = remote // blocks
    placing = (
        (local[:, None] == jnp.arange(blocks, dtype=jnp.int32)[None, :]) & live[:, None]
    ).astype(f32)
    meets = live[:, None] & (owner[:, None] == jnp.arange(devices, dtype=jnp.int32)[None, :])
    granted = jnp.sum(jnp.where(meets, local[:, None], 0), axis=0)
    vector = jnp.transpose(gradient.reshape(width, blocks, BLOCK), (1, 0, 2))
    steps = []
    for _ in range(ITERS):
        sent = jnp.einsum("nej,nji->nei", vector, jacobi, precision=highest)[granted]
        incoming = lax.all_to_all(sent, "rows", 0, 0, tiled=True)
        products = jnp.einsum(
            "kej,kji->kei", incoming[owner], tiles.astype(f32), precision=highest
        )
        vector = jnp.einsum("kei,kn->nei", products, placing, precision=highest)
        steps.append(vector)
    columns = lax.axis_size("cols")
    share = order.shape[0] // columns
    chain = jnp.pad(jnp.stack(steps), ((0, 0), (0, share * columns - blocks), (0, 0), (0, 0)))
    return [
        lax.dynamic_slice_in_dim(chain, order[o * share], share, 1) for o in range(columns)
    ]


def gather_sums(sums, s, y, weight):
    y = [weight * value for value in y]
    f = [s[0] + s[1]]
    for j in range(1, ITERS):
        f.append(0.5 * (s[j - 1] + s[j + 1]) + s[j])
    for i in range(ITERS):
        for j in range(i + 1):
            sums[i, j] = sums.get((i, j), 0.0) + y[i] * f[j]
        sums[i, ITERS] = sums.get((i, ITERS), 0.0) + y[i] * s[0]


def flat_sums(sums):
    lane = lax.broadcasted_iota(jnp.int32, (1, BLOCK), 1)
    result = jnp.zeros((1, BLOCK), f32)
    for (i, j), value in sums.items():
        value = jnp.sum(jnp.sum(value, axis=0, keepdims=True), axis=1, keepdims=True)
        here = lane == 16 * i + j
        if j < ITERS:
            here = here | (lane == 16 * j + i)
        result = jnp.where(here, value, result)
    return result


def powers_kernel(turn, *refs):
    pieces, (scaled, powers, scale) = refs[:-3], refs[-3:]
    width = pieces[0].shape[0]
    factor = jnp.concatenate([piece[...] for piece in pieces], 0)
    factor = pltpu.roll(factor, turn[0], 1)
    norm = jnp.max(jnp.sum(jnp.abs(factor), axis=1, keepdims=True), axis=0, keepdims=True)
    power = factor / norm
    for _ in range(3):
        power = dot3(power, power)
    bound = jnp.sum(jnp.sum(power * power, axis=1, keepdims=True), axis=0, keepdims=True)
    for _ in range(4):
        bound = jnp.sqrt(bound)
    ratio = 2.0 / (STRETCH * bound * norm)
    scale[...] = jnp.broadcast_to(ratio, scale.shape)
    factor = factor * ratio
    scaled[...] = factor

    row = lax.broadcasted_iota(jnp.int32, (width, BLOCK), 0)
    lane = lax.broadcasted_iota(jnp.int32, (width, BLOCK), 1)
    kept = [(row == lane).astype(f32)]
    for k in range(ITERS):
        value = dot(kept[k], factor) - kept[k]
        kept.append(2.0 * value - kept[k - 1] if k else value)
    powers[...] = jnp.concatenate(kept, 0)


def basis_kernel(where, held, powers, jacobi, *refs):
    pieces, (plain, smooth, gram, starts) = refs[:-4], refs[-4:]
    width = pieces[0].shape[0]
    for p in range(starts.shape[0]):
        columns = pl.ds(pl.multiple_of(held[p] * BLOCK, BLOCK), BLOCK)
        starts[p] = jnp.concatenate([piece[:, columns] for piece in pieces], 0)
    sums = {}
    for b in range(jacobi.shape[0]):
        columns = slice(b * BLOCK, (b + 1) * BLOCK)
        whole = jnp.concatenate([piece[:, columns] for piece in pieces], 0)
        s = dot3(powers[...], whole)
        y = dot3(s[: ITERS * width], jacobi[b])
        plain[b] = s[width:]
        smooth[b] = y
        weight = jnp.where(where[b] < NOWHERE, 0.0, 1.0)
        for r in range(0, width, 8):
            gather_sums(
                sums,
                [s[k * width + r : k * width + r + 8] for k in range(ITERS + 1)],
                [y[k * width + r : k * width + r + 8] for k in range(ITERS)],
                weight,
            )
    gram[...] = flat_sums(sums)


def make_powers(pieces):
    width = pieces[0].shape[0]
    shape = jax.ShapeDtypeStruct
    turn = (BLOCK - width * lax.axis_index("cols")) % BLOCK
    return call(
        powers_kernel,
        (
            shape((BLOCK, BLOCK), f32),
            shape(((ITERS + 1) * width, BLOCK), f32),
            shape((8, BLOCK), f32),
        ),
        turn.astype(jnp.int32).reshape(1),
        *pieces,
        scalars=1,
    )


def mix_kernel(held, used, *refs):
    devices = (len(refs) - 5) // 2
    parts = refs[:devices]
    starts, scaled, jacobi, others, gram = refs[devices : devices + 5]
    backs = refs[devices + 5 :]
    share, width = parts[0].shape[1:3]
    sums = {}
    for p in range(share):
        now = [starts[p]]
        for j in range(ITERS):
            now.append(jnp.concatenate([part[j, p] for part in parts], 0))
        past = None
        chosen = [now[0]]
        for k in range(ITERS):
            left = ITERS - k
            image = dot3(
                scaled[...], jnp.concatenate([now[i] + now[i + 1] for i in range(left)], 1)
            )
            fresh = []
            for i in range(left):
                value = image[:, i * BLOCK : (i + 1) * BLOCK] - now[i]
                fresh.append(2.0 * value - past[i] if k else value)
            past, now = now, fresh
            chosen.append(now[0])
        for o, back in enumerate(backs):
            for k in range(ITERS):
                back[k, p] = chosen[k + 1][o * width : (o + 1) * width]
        soft = dot3(jnp.concatenate(chosen[:ITERS], 0), jacobi[held[p]])
        weight = jnp.where(used[p] > 0, 1.0, 0.0)
        for r in range(0, BLOCK, 8):
            gather_sums(
                sums,
                [value[r : r + 8] for value in chosen],
                [soft[k * BLOCK + r : k * BLOCK + r + 8] for k in range(ITERS)],
                weight,
            )
    gram[...] = jnp.broadcast_to((flat_sums(sums) + others[...])[None], gram.shape)


def finish_kernel(held, where, grams, scale, gradient, plain, smooth, jacobi, *refs):
    backs, (solution, residual, extra, less) = refs[:-4], refs[-4:]
    width = gradient.shape[0]
    blocks = jacobi.shape[0]
    share = backs[0].shape[1]
    none = len(backs) * share
    flat = jnp.sum(grams[:, 0, :], axis=0, keepdims=True)
    row = lax.broadcasted_iota(jnp.int32, (8, BLOCK), 0)
    lane = lax.broadcasted_iota(jnp.int32, (8, BLOCK), 1)
    table = jnp.zeros((8, BLOCK), f32)
    for i in range(ITERS):
        moved = flat if i == 0 else pltpu.roll(flat, BLOCK - 16 * i, 1)
        table = jnp.where((row == i) & (lane <= ITERS), moved, table)
    for p in range(ITERS):
        pivot = table[p : p + 1, :] / table[p : p + 1, p : p + 1]
        table = jnp.where(row == p, pivot, table - table[:, p : p + 1] * pivot)
    steps = [table[j : j + 1, ITERS : ITERS + 1] for j in range(ITERS)]
    takes = []
    for k in range(ITERS + 1):
        value = 0.0
        if k > 0:
            value += steps[k - 1] * (1.0 if k == 1 else 0.5)
        if k < ITERS:
            value += steps[k]
        if k + 1 < ITERS:
            value += 0.5 * steps[k + 1]
        takes.append(jnp.broadcast_to(value, (width, BLOCK)))
    longer = scale[0:1, 0:1]
    gives = [jnp.broadcast_to(longer * step, (width, BLOCK)) for step in steps]

    def combine(weights, values):
        return sum(weight * value for weight, value in zip(weights, values))

    def cut(ref, b):
        return [ref[b, k * width : (k + 1) * width, :] for k in range(ITERS)]

    for n in range(none):
        values = [backs[n // share][k, n % share] for k in range(ITERS)]
        extra[n] = dot3(combine(gives[1:], values), jacobi[held[n]])
        less[n] = combine(takes[1:], values)
    for b in range(blocks):
        columns = slice(b * BLOCK, (b + 1) * BLOCK)
        n = jnp.minimum(where[b], none - 1)
        own = where[b] >= NOWHERE
        y = cut(smooth, b)
        rest = jnp.where(own, combine(gives[1:], y[1:]), extra[n])
        solution[:, columns] = gives[0] * y[0] + rest
        rest = jnp.where(own, combine(takes[1:], cut(plain, b)), less[n])
        start = gradient[:, columns]
        residual[:, columns] = start - takes[0] * start - rest


def on_device(
    gradient,
    width_factor,
    diag_blocks,
    jacobi_inverse,
    coupling_tiles,
    tile_local,
    tile_remote,
    tile_count,
    exchange=False,
):
    width, rows = gradient.shape
    blocks = diag_blocks.shape[0]
    columns = lax.axis_size("cols")
    devices = lax.axis_size("rows")
    slots = tile_local.shape[0] - 1
    live = jnp.arange(slots, dtype=jnp.int32) < tile_count[0]
    lists = (tile_local[:slots], tile_remote[:slots], live)

    gathered = devices * slots * BLOCK * (BLOCK + width) * 2
    noted = slots * (4 + width) <= BLOCK and width % NOTE_ROWS == 0 and devices * blocks < 2**15
    whole = gathered <= GATHER_BYTES and noted and devices % 2 == 0 and not exchange
    units = slots if whole else blocks
    share = -(-units // columns)
    numbers = jnp.arange(columns * share, dtype=jnp.int32)
    dealer = (lax.axis_index("cols") + columns - numbers // share) % columns
    order = dealer * share + numbers % share
    if whole:
        local = lists[0]
        earlier = jnp.arange(slots)[:, None] > jnp.arange(slots)[None, :]
        repeat = jnp.any(earlier & (local[:, None] == local[None, :]), axis=1)
        fit = order[:, None] == jnp.arange(slots, dtype=jnp.int32)[None, :]
        held = jnp.sum(jnp.where(fit, local[None, :], 0), axis=1)
        used = jnp.sum(jnp.where(fit & (live & ~repeat)[None, :], 1, 0), axis=1)
    else:
        held = jnp.minimum(order, blocks - 1)
        used = (order < blocks).astype(jnp.int32)
    mine = (held[None, :] == jnp.arange(blocks, dtype=jnp.int32)[:, None]) & (used > 0)[None, :]
    where = jnp.min(jnp.where(mine, numbers[None, :], NOWHERE), axis=1)
    if whole:
        sends, pieces, powers = chain_gathered(
            gradient,
            width_factor,
            jacobi_inverse,
            coupling_tiles,
            tile_local,
            tile_remote,
            tile_count,
            order,
            slots,
        )
    else:
        sends = chain_exchanged(
            gradient, jacobi_inverse, coupling_tiles[:slots], order, *lists
        )
        pieces = whole_pieces(gradient)
        powers = make_powers(whole_pieces(width_factor.T))
    scaled, powers, scale = powers
    powers, sends = lax.optimization_barrier((powers, sends))
    parts = [sends[0]]
    for o in range(1, columns):
        parts.append(shift(sends[o], "cols", o))

    shape = jax.ShapeDtypeStruct
    plain, smooth, others, starts = call(
        basis_kernel,
        (
            shape((blocks, ITERS * width, BLOCK), f32),
            shape((blocks, ITERS * width, BLOCK), f32),
            shape((1, BLOCK), f32),
            shape((share, BLOCK, BLOCK), f32),
        ),
        where,
        held,
        powers,
        jacobi_inverse,
        *pieces,
        scalars=2,
    )
    gram, *backs = call(
        mix_kernel,
        tuple(
            [shape((columns * devices, 1, BLOCK), f32)]
            + [shape((ITERS, share, width, BLOCK), f32)] * columns
        ),
        held,
        used,
        *parts,
        starts,
        scaled,
        jacobi_inverse,
        others,
        scalars=2,
    )
    grams = lax.all_to_all(gram, ("cols", "rows"), 0, 0, tiled=True)
    for o in range(1, columns):
        backs[o] = shift(backs[o], "cols", -o)
    return call(
        finish_kernel,
        (shape((width, rows), f32), shape((width, rows), f32)),
        held,
        where,
        grams,
        scale,
        gradient,
        plain,
        smooth,
        jacobi_inverse,
        *backs,
        scalars=2,
        scratch=[pltpu.VMEM((columns * share, width, BLOCK), f32)] * 2,
    )


def solution(mesh):
    placed = (
        P("cols", "rows"),
        P(None, "cols"),
        P("rows", None, None),
        P("rows", None, None),
        P("rows", None, None),
        P("rows"),
        P("rows"),
        P("rows"),
    )

    return jax.shard_map(
        on_device,
        mesh=mesh,
        in_specs=placed,
        out_specs=(P("cols", "rows"), P("cols", "rows")),
        check_vma=False,
    )
```

```python
import jax
import jax.numpy as jnp
from jax import lax
from jax.experimental import pallas as pl
from jax.experimental.pallas import tpu as pltpu
from jax.sharding import PartitionSpec as P


BLOCK = 128
ITERS = 6
STRETCH = 1.1
GATHER_BYTES = 8 * 2**20


NOWHERE = 2**20
LEVELS = 32700.0
NOTES = 256 / 0.6931471805599453
NOTE_ROWS = 16
GRANT_BYTES = 24 * 2**20
WHOLE_BYTES = 60 * 2**20

highest = lax.Precision.HIGHEST
f32 = jnp.float32
VMEM = pl.BlockSpec(memory_space=pltpu.VMEM)
SMEM = pl.BlockSpec(memory_space=pltpu.SMEM)


def dot(a, b):
    return jnp.dot(a, b, precision=highest, preferred_element_type=f32)


def call(kernel, outs, *args, scalars=0, scratch=(), place=VMEM, grant=GRANT_BYTES):
    specs = [SMEM] * scalars + [place] * (len(args) - scalars)
    many = isinstance(outs, tuple)
    return pl.pallas_call(
        kernel,
        out_shape=outs,
        in_specs=specs,
        out_specs=tuple([VMEM] * len(outs)) if many else VMEM,
        scratch_shapes=list(scratch),
        compiler_params=pltpu.CompilerParams(vmem_limit_bytes=grant),
    )(*args)


def split(x):
    high = x.astype(jnp.bfloat16)
    return high, (x - high.astype(f32)).astype(jnp.bfloat16)


def plain_dot(a, b):
    return jnp.dot(a, b, preferred_element_type=f32)


def dot3(a, b):
    tall = a.shape[0]
    high, low = split(a)
    right, rest = split(b)
    both = plain_dot(jnp.concatenate([high, low], 0), right)
    return both[:tall] + (both[tall:] + plain_dot(high, rest))


def note(top):
    return jnp.floor(jnp.log(jnp.maximum(top, 1e-30)) * NOTES).astype(jnp.int32) + 1


def noted_range(number):
    return jnp.exp(number.astype(f32) * (1.0 / NOTES))


def code(x, number):
    unit = LEVELS / noted_range(number)
    return jnp.floor(x * unit + 0.5).astype(jnp.int32).astype(jnp.int16)


def pack_kernel(local, remote, count, gradient, jacobi, tiles, packed, *scratch):
    blocks, others, lives, whole, inverse, coupling, done = scratch
    width = whole.shape[0]
    height = BLOCK + width
    slots = packed.shape[0] // height
    contract = (((1,), (1,)), ((), ()))
    sources = [local, remote, count, jacobi, tiles, gradient]
    targets = [blocks, others, lives, inverse, coupling, whole]
    copies = [
        pltpu.make_async_copy(source, target, done.at[i])
        for i, (source, target) in enumerate(zip(sources, targets))
    ]
    for copy in copies:
        copy.start()
    for copy in copies:
        copy.wait()
    lane = lax.broadcasted_iota(jnp.int32, (width, BLOCK), 1)
    row = lax.broadcasted_iota(jnp.int32, (width, BLOCK), 0)
    notes = jnp.zeros((width, BLOCK), jnp.int32)
    for slot in range(slots):
        block = blocks[slot]
        halves = jnp.concatenate(split(inverse[block]), 0)
        both = lax.dot_general(halves, coupling[slot], contract, preferred_element_type=f32)
        operator = both[:BLOCK] + both[BLOCK:]
        top = jnp.max(jnp.max(jnp.abs(operator), axis=0, keepdims=True), axis=1, keepdims=True)
        columns = pl.ds(pl.multiple_of(block * BLOCK, BLOCK), BLOCK)
        part = whole[:, columns]
        tops = jnp.max(jnp.abs(part), axis=1, keepdims=True)
        at = slot * height
        packed[at : at + BLOCK, :] = code(operator, note(top))
        packed[at + BLOCK : at + height, :] = code(part, note(tops))
        live = jnp.where(slot < lives[0], 1, 0)
        for place, value in enumerate((block, others[slot], live, note(top))):
            here = (lane == place * slots + slot) & (row == 0)
            notes = jnp.where(here, value, notes)
        notes = jnp.where(lane == 4 * slots + slot * width + row, note(tops), notes)
    notes = jnp.sum(notes, axis=0, keepdims=True)
    packed[slots * height :, :] = jnp.broadcast_to(notes, (NOTE_ROWS, BLOCK)).astype(jnp.int16)


def chain_kernel(sources, give, near, far, *refs):
    sends, (operators, tops, held, out, kept) = refs[:-5], refs[-5:]
    groups = near.shape[0]
    width = held.shape[1]
    height = BLOCK + width
    slots = near.shape[1] // height
    half = groups * slots
    total = 2 * half
    count = kept.shape[0] // len(sends)
    share = count // ITERS
    lane = lax.broadcasted_iota(jnp.int32, (width, BLOCK), 1)
    row = lax.broadcasted_iota(jnp.int32, (width, BLOCK), 0)
    for q in range(total):
        ref = near if q < half else far
        group, slot = divmod(q % half, slots)
        at = slot * height
        high, low = split(ref[group, at : at + BLOCK, :].astype(f32))
        operators[q, :, :BLOCK] = high
        operators[q, :, BLOCK:] = low
        notes = ref[group, slots * height :, :].astype(f32)
        notes = jnp.concatenate([notes] * (width // NOTE_ROWS), 0)
        scale = noted_range(
            jnp.sum(jnp.where(lane == 3 * slots + slot, notes, 0.0), axis=1, keepdims=True)
        )
        tops[q] = jnp.broadcast_to(scale * (1.0 / LEVELS), (width, BLOCK))
        here = lane == 4 * slots + slot * width + row
        scale = noted_range(jnp.sum(jnp.where(here, notes, 0.0), axis=1, keepdims=True))
        part = ref[group, at + BLOCK : at + height, :].astype(f32)
        held[q] = part * (scale * (1.0 / LEVELS))
    held[total] = jnp.zeros((width, BLOCK), f32)
    out[total] = jnp.zeros((width, BLOCK), f32)

    def step(j, carry):
        for q in range(total):
            four = plain_dot(jnp.concatenate(split(held[q]), 0), operators[q])
            value = (four[:width, :BLOCK] + four[width:, :BLOCK]) + (
                four[:width, BLOCK:] + four[width:, BLOCK:]
            )
            out[q] = value * tops[q]
        for q in range(total):
            value = out[sources[q * slots]]
            for i in range(1, slots):
                value += out[sources[q * slots + i]]
            held[q] = value
        for o in range(len(sends)):
            for p in range(share):
                kept[o * count + j * share + p] = held[give[o * share + p]]
        return carry

    lax.fori_loop(0, ITERS, step, 0)
    line = lax.broadcasted_iota(jnp.int32, (NOTE_ROWS, BLOCK), 0)
    for o, send in enumerate(sends):
        notes = jnp.zeros((NOTE_ROWS, BLOCK), jnp.int32)
        for n in range(count):
            at = n * width
            value = kept[o * count + n]
            number = note(jnp.max(jnp.abs(value), axis=1, keepdims=True))
            send[at : at + width, :] = code(value, number)
            number = jnp.where(lane == at % BLOCK + row, number, 0)
            number = jnp.sum(number, axis=0, keepdims=True)
            notes = jnp.where(line == at // BLOCK, notes + number, notes)
        send[count * width :, :] = notes.astype(jnp.int16)


def shift(x, axis, by):
    size = lax.axis_size(axis)
    return lax.ppermute(x, axis, [(i, (i - by) % size) for i in range(size)])


def whole_pieces(x):
    others = range(1, lax.axis_size("cols"))
    return [x] + [shift(x, "cols", o) for o in others]


def chain_gathered(
    gradient, factor, jacobi, tiles, whole_local, whole_remote, count, order, slots
):
    width = gradient.shape[0]
    blocks = jacobi.shape[0]
    devices = lax.axis_size("rows")
    columns = lax.axis_size("cols")
    groups = devices // 2
    height = BLOCK + width
    packed = call(
        pack_kernel,
        jax.ShapeDtypeStruct((slots * height + NOTE_ROWS, BLOCK), jnp.int16),
        whole_local,
        whole_remote,
        count,
        gradient,
        jacobi,
        tiles,
        scratch=[
            pltpu.SMEM(whole_local.shape, jnp.int32),
            pltpu.SMEM(whole_remote.shape, jnp.int32),
            pltpu.SMEM(count.shape, jnp.int32),
            pltpu.VMEM(gradient.shape, f32),
            pltpu.VMEM(jacobi.shape, f32),
            pltpu.VMEM(tiles.shape, tiles.dtype),
            pltpu.SemaphoreType.DMA((6,)),
        ],
        place=pl.BlockSpec(memory_space=pl.ANY),
        grant=WHOLE_BYTES,
    )
    near = [packed] + [shift(packed, "rows", 2 * o) for o in range(1, groups)]
    gradient, factor, _ = lax.optimization_barrier((gradient, factor, packed))
    factors = whole_pieces(factor.T)
    pieces = whole_pieces(gradient)
    powers = make_powers(factors)
    near, powers = lax.optimization_barrier((near, powers))
    near = jnp.stack(near)
    swap = [(i, i ^ 1) for i in range(devices)]
    noted = near[:, slots * height :, :]
    told = lax.ppermute(noted, "rows", swap)
    far = lax.ppermute(near, "rows", swap)
    told = jnp.concatenate([noted[:, 0], told[:, 0]], 0)

    me = lax.axis_index("rows")
    position = jnp.arange(devices, dtype=jnp.int32)
    base = me ^ (position // groups)
    device = (base + 2 * (position % groups)) % devices
    locals_, remotes, lives = (
        told[:, i * slots : (i + 1) * slots].astype(jnp.int32) for i in range(3)
    )
    owner = (remotes // blocks).reshape(-1)
    holder = jnp.broadcast_to(device[:, None], locals_.shape).reshape(-1)
    alive = lives.reshape(-1) > 0
    meets = (
        (owner[:, None] == holder[None, :])
        & (owner[None, :] == holder[:, None])
        & alive[None, :]
    )
    total = devices * slots
    numbers = jnp.arange(total, dtype=jnp.int32)
    partner = jnp.sum(jnp.where(meets, numbers[None, :], 0), axis=1).reshape(devices, slots)
    same = (
        (locals_[:, :, None] == locals_[:, None, :])
        & (lives[:, None, :] > 0)
        & (lives[:, :, None] > 0)
    )
    sources = jnp.where(same, partner[:, None, :], total).reshape(-1)
    share = order.shape[0] // columns
    shape = jax.ShapeDtypeStruct
    sends = call(
        chain_kernel,
        tuple([shape((ITERS * share * width + NOTE_ROWS, BLOCK), jnp.int16)] * columns),
        sources,
        jnp.where(order < slots, order, total),
        near,
        far,
        scalars=2,
        scratch=[
            pltpu.VMEM((total, BLOCK, 2 * BLOCK), jnp.bfloat16),
            pltpu.VMEM((total, width, BLOCK), f32),
            pltpu.VMEM((total + 1, width, BLOCK), f32),
            pltpu.VMEM((total + 1, width, BLOCK), f32),
            pltpu.VMEM((columns * ITERS * share, width, BLOCK), f32),
        ],
    )
    return list(sends), pieces, powers


def chain_exchanged(gradient, jacobi, tiles, order, local, remote, live):
    width = gradient.shape[0]
    blocks = jacobi.shape[0]
    devices = lax.axis_size("rows")
    owner = remote // blocks
    placing = (
        (local[:, None] == jnp.arange(blocks, dtype=jnp.int32)[None, :]) & live[:, None]
    ).astype(f32)
    meets = live[:, None] & (owner[:, None] == jnp.arange(devices, dtype=jnp.int32)[None, :])
    granted = jnp.sum(jnp.where(meets, local[:, None], 0), axis=0)
    vector = jnp.transpose(gradient.reshape(width, blocks, BLOCK), (1, 0, 2))
    steps = []
    for _ in range(ITERS):
        sent = jnp.einsum("nej,nji->nei", vector, jacobi, precision=highest)[granted]
        incoming = lax.all_to_all(sent, "rows", 0, 0, tiled=True)
        products = jnp.einsum(
            "kej,kji->kei", incoming[owner], tiles.astype(f32), precision=highest
        )
        vector = jnp.einsum("kei,kn->nei", products, placing, precision=highest)
        steps.append(vector)
    columns = lax.axis_size("cols")
    share = order.shape[0] // columns
    chain = jnp.pad(jnp.stack(steps), ((0, 0), (0, share * columns - blocks), (0, 0), (0, 0)))
    return [
        lax.dynamic_slice_in_dim(chain, order[o * share], share, 1) for o in range(columns)
    ]


def gather_sums(sums, s, y, weight):
    y = [weight * value for value in y]
    f = [s[0] + s[1]]
    for j in range(1, ITERS):
        f.append(0.5 * (s[j - 1] + s[j + 1]) + s[j])
    for i in range(ITERS):
        for j in range(i + 1):
            sums[i, j] = sums.get((i, j), 0.0) + y[i] * f[j]
        sums[i, ITERS] = sums.get((i, ITERS), 0.0) + y[i] * s[0]


def flat_sums(sums):
    lane = lax.broadcasted_iota(jnp.int32, (1, BLOCK), 1)
    result = jnp.zeros((1, BLOCK), f32)
    for (i, j), value in sums.items():
        value = jnp.sum(jnp.sum(value, axis=0, keepdims=True), axis=1, keepdims=True)
        here = lane == 16 * i + j
        if j < ITERS:
            here = here | (lane == 16 * j + i)
        result = jnp.where(here, value, result)
    return result


def powers_kernel(turn, *refs):
    pieces, (scaled, powers, scale) = refs[:-3], refs[-3:]
    width = pieces[0].shape[0]
    factor = jnp.concatenate([piece[...] for piece in pieces], 0)
    factor = pltpu.roll(factor, turn[0], 1)
    norm = jnp.max(jnp.sum(jnp.abs(factor), axis=1, keepdims=True), axis=0, keepdims=True)
    power = factor / norm
    for _ in range(3):
        power = dot3(power, power)
    bound = jnp.sum(jnp.sum(power * power, axis=1, keepdims=True), axis=0, keepdims=True)
    for _ in range(4):
        bound = jnp.sqrt(bound)
    ratio = 2.0 / (STRETCH * bound * norm)
    scale[...] = jnp.broadcast_to(ratio, scale.shape)
    factor = factor * ratio
    scaled[...] = factor

    row = lax.broadcasted_iota(jnp.int32, (width, BLOCK), 0)
    lane = lax.broadcasted_iota(jnp.int32, (width, BLOCK), 1)
    kept = [(row == lane).astype(f32)]
    for k in range(ITERS):
        value = dot(kept[k], factor) - kept[k]
        kept.append(2.0 * value - kept[k - 1] if k else value)
    powers[...] = jnp.concatenate(kept, 0)


def basis_kernel(where, held, powers, jacobi, *refs):
    pieces, (plain, smooth, gram, starts) = refs[:-4], refs[-4:]
    width = pieces[0].shape[0]
    for p in range(starts.shape[0]):
        columns = pl.ds(pl.multiple_of(held[p] * BLOCK, BLOCK), BLOCK)
        starts[p] = jnp.concatenate([piece[:, columns] for piece in pieces], 0)
    sums = {}
    for b in range(jacobi.shape[0]):
        columns = slice(b * BLOCK, (b + 1) * BLOCK)
        whole = jnp.concatenate([piece[:, columns] for piece in pieces], 0)
        s = dot3(powers[...], whole)
        y = dot3(s[: ITERS * width], jacobi[b])
        plain[b] = s[width:]
        smooth[b] = y
        weight = jnp.where(where[b] < NOWHERE, 0.0, 1.0)
        for r in range(0, width, 8):
            gather_sums(
                sums,
                [s[k * width + r : k * width + r + 8] for k in range(ITERS + 1)],
                [y[k * width + r : k * width + r + 8] for k in range(ITERS)],
                weight,
            )
    gram[...] = flat_sums(sums)


def make_powers(pieces):
    width = pieces[0].shape[0]
    shape = jax.ShapeDtypeStruct
    turn = (BLOCK - width * lax.axis_index("cols")) % BLOCK
    return call(
        powers_kernel,
        (
            shape((BLOCK, BLOCK), f32),
            shape(((ITERS + 1) * width, BLOCK), f32),
            shape((8, BLOCK), f32),
        ),
        turn.astype(jnp.int32).reshape(1),
        *pieces,
        scalars=1,
    )


def mix_kernel(held, used, *refs):
    devices = (len(refs) - 5) // 2
    parts = refs[:devices]
    starts, scaled, jacobi, others, gram = refs[devices : devices + 5]
    backs = refs[devices + 5 :]
    share = starts.shape[0]
    width = BLOCK // devices
    lane = lax.broadcasted_iota(jnp.int32, (width, BLOCK), 1)
    row = lax.broadcasted_iota(jnp.int32, (width, BLOCK), 0)

    def chained(part, j, p):
        if part.dtype == f32:
            return part[j, p]
        at = (j * share + p) * width
        notes = part[ITERS * share * width :, :].astype(f32)
        notes = notes[at // BLOCK : at // BLOCK + 1, :]
        number = jnp.where(lane == at % BLOCK + row, notes, 0.0)
        scale = noted_range(jnp.sum(number, axis=1, keepdims=True)) * (1.0 / LEVELS)
        return part[at : at + width, :].astype(f32) * scale

    sums = {}
    for p in range(share):
        now = [starts[p]]
        for j in range(ITERS):
            now.append(jnp.concatenate([chained(part, j, p) for part in parts], 0))
        past = None
        chosen = [now[0]]
        for k in range(ITERS):
            left = ITERS - k
            image = dot3(
                scaled[...], jnp.concatenate([now[i] + now[i + 1] for i in range(left)], 1)
            )
            fresh = []
            for i in range(left):
                value = image[:, i * BLOCK : (i + 1) * BLOCK] - now[i]
                fresh.append(2.0 * value - past[i] if k else value)
            past, now = now, fresh
            chosen.append(now[0])
        for o, back in enumerate(backs):
            for k in range(ITERS):
                back[k, p] = chosen[k + 1][o * width : (o + 1) * width]
        soft = dot3(jnp.concatenate(chosen[:ITERS], 0), jacobi[held[p]])
        weight = jnp.where(used[p] > 0, 1.0, 0.0)
        for r in range(0, BLOCK, 8):
            gather_sums(
                sums,
                [value[r : r + 8] for value in chosen],
                [soft[k * BLOCK + r : k * BLOCK + r + 8] for k in range(ITERS)],
                weight,
            )
    gram[...] = jnp.broadcast_to((flat_sums(sums) + others[...])[None], gram.shape)


def finish_kernel(held, where, grams, scale, gradient, plain, smooth, jacobi, *refs):
    backs, (solution, residual, extra, less) = refs[:-4], refs[-4:]
    width = gradient.shape[0]
    blocks = jacobi.shape[0]
    share = backs[0].shape[1]
    none = len(backs) * share
    flat = jnp.sum(grams[:, 0, :], axis=0, keepdims=True)
    row = lax.broadcasted_iota(jnp.int32, (8, BLOCK), 0)
    lane = lax.broadcasted_iota(jnp.int32, (8, BLOCK), 1)
    table = jnp.zeros((8, BLOCK), f32)
    for i in range(ITERS):
        moved = flat if i == 0 else pltpu.roll(flat, BLOCK - 16 * i, 1)
        table = jnp.where((row == i) & (lane <= ITERS), moved, table)
    for p in range(ITERS):
        pivot = table[p : p + 1, :] / table[p : p + 1, p : p + 1]
        table = jnp.where(row == p, pivot, table - table[:, p : p + 1] * pivot)
    steps = [table[j : j + 1, ITERS : ITERS + 1] for j in range(ITERS)]
    takes = []
    for k in range(ITERS + 1):
        value = 0.0
        if k > 0:
            value += steps[k - 1] * (1.0 if k == 1 else 0.5)
        if k < ITERS:
            value += steps[k]
        if k + 1 < ITERS:
            value += 0.5 * steps[k + 1]
        takes.append(jnp.broadcast_to(value, (width, BLOCK)))
    longer = scale[0:1, 0:1]
    gives = [jnp.broadcast_to(longer * step, (width, BLOCK)) for step in steps]

    def combine(weights, values):
        return sum(weight * value for weight, value in zip(weights, values))

    def cut(ref, b):
        return [ref[b, k * width : (k + 1) * width, :] for k in range(ITERS)]

    for n in range(none):
        values = [backs[n // share][k, n % share] for k in range(ITERS)]
        extra[n] = dot3(combine(gives[1:], values), jacobi[held[n]])
        less[n] = combine(takes[1:], values)
    for b in range(blocks):
        columns = slice(b * BLOCK, (b + 1) * BLOCK)
        n = jnp.minimum(where[b], none - 1)
        own = where[b] >= NOWHERE
        y = cut(smooth, b)
        rest = jnp.where(own, combine(gives[1:], y[1:]), extra[n])
        solution[:, columns] = gives[0] * y[0] + rest
        rest = jnp.where(own, combine(takes[1:], cut(plain, b)), less[n])
        start = gradient[:, columns]
        residual[:, columns] = start - takes[0] * start - rest


def on_device(
    gradient,
    width_factor,
    diag_blocks,
    jacobi_inverse,
    coupling_tiles,
    tile_local,
    tile_remote,
    tile_count,
    exchange=False,
):
    width, rows = gradient.shape
    blocks = diag_blocks.shape[0]
    columns = lax.axis_size("cols")
    devices = lax.axis_size("rows")
    slots = tile_local.shape[0] - 1
    live = jnp.arange(slots, dtype=jnp.int32) < tile_count[0]
    lists = (tile_local[:slots], tile_remote[:slots], live)

    gathered = devices * slots * BLOCK * (BLOCK + width) * 2
    noted = slots * (4 + width) <= BLOCK and width % NOTE_ROWS == 0 and devices * blocks < 2**15
    noted = noted and ITERS * -(-slots // columns) * width <= NOTE_ROWS * BLOCK
    whole = gathered <= GATHER_BYTES and noted and devices % 2 == 0 and not exchange
    units = slots if whole else blocks
    share = -(-units // columns)
    numbers = jnp.arange(columns * share, dtype=jnp.int32)
    dealer = (lax.axis_index("cols") + columns - numbers // share) % columns
    order = dealer * share + numbers % share
    if whole:
        local = lists[0]
        earlier = jnp.arange(slots)[:, None] > jnp.arange(slots)[None, :]
        repeat = jnp.any(earlier & (local[:, None] == local[None, :]), axis=1)
        fit = order[:, None] == jnp.arange(slots, dtype=jnp.int32)[None, :]
        held = jnp.sum(jnp.where(fit, local[None, :], 0), axis=1)
        used = jnp.sum(jnp.where(fit & (live & ~repeat)[None, :], 1, 0), axis=1)
    else:
        held = jnp.minimum(order, blocks - 1)
        used = (order < blocks).astype(jnp.int32)
    mine = (held[None, :] == jnp.arange(blocks, dtype=jnp.int32)[:, None]) & (used > 0)[None, :]
    where = jnp.min(jnp.where(mine, numbers[None, :], NOWHERE), axis=1)
    if whole:
        sends, pieces, powers = chain_gathered(
            gradient,
            width_factor,
            jacobi_inverse,
            coupling_tiles,
            tile_local,
            tile_remote,
            tile_count,
            order,
            slots,
        )
    else:
        sends = chain_exchanged(
            gradient, jacobi_inverse, coupling_tiles[:slots], order, *lists
        )
        pieces = whole_pieces(gradient)
        powers = make_powers(whole_pieces(width_factor.T))
    scaled, powers, scale = powers
    powers, sends = lax.optimization_barrier((powers, sends))
    parts = [sends[0]]
    for o in range(1, columns):
        parts.append(shift(sends[o], "cols", o))

    shape = jax.ShapeDtypeStruct
    plain, smooth, others, starts = call(
        basis_kernel,
        (
            shape((blocks, ITERS * width, BLOCK), f32),
            shape((blocks, ITERS * width, BLOCK), f32),
            shape((1, BLOCK), f32),
            shape((share, BLOCK, BLOCK), f32),
        ),
        where,
        held,
        powers,
        jacobi_inverse,
        *pieces,
        scalars=2,
    )
    gram, *backs = call(
        mix_kernel,
        tuple(
            [shape((columns * devices, 1, BLOCK), f32)]
            + [shape((ITERS, share, width, BLOCK), f32)] * columns
        ),
        held,
        used,
        *parts,
        starts,
        scaled,
        jacobi_inverse,
        others,
        scalars=2,
    )
    grams = lax.all_to_all(gram, ("cols", "rows"), 0, 0, tiled=True)
    for o in range(1, columns):
        backs[o] = shift(backs[o], "cols", -o)
    return call(
        finish_kernel,
        (shape((width, rows), f32), shape((width, rows), f32)),
        held,
        where,
        grams,
        scale,
        gradient,
        plain,
        smooth,
        jacobi_inverse,
        *backs,
        scalars=2,
        scratch=[pltpu.VMEM((columns * share, width, BLOCK), f32)] * 2,
    )


def solution(mesh):
    placed = (
        P("cols", "rows"),
        P(None, "cols"),
        P("rows", None, None),
        P("rows", None, None),
        P("rows", None, None),
        P("rows"),
        P("rows"),
        P("rows"),
    )

    return jax.shard_map(
        on_device,
        mesh=mesh,
        in_specs=placed,
        out_specs=(P("cols", "rows"), P("cols", "rows")),
        check_vma=False,
    )
```

```python
import jax
import jax.numpy as jnp
from jax import lax
from jax.experimental import pallas as pl
from jax.experimental.pallas import tpu as pltpu
from jax.sharding import PartitionSpec as P


BLOCK = 128
ITERS = 6
STRETCH = 1.1
GATHER_BYTES = 8 * 2**20


NOWHERE = 2**20
LEVELS = 32700.0
NOTES = 256 / 0.6931471805599453
NOTE_ROWS = 16
GRANT_BYTES = 24 * 2**20
WHOLE_BYTES = 60 * 2**20

highest = lax.Precision.HIGHEST
f32 = jnp.float32
VMEM = pl.BlockSpec(memory_space=pltpu.VMEM)
SMEM = pl.BlockSpec(memory_space=pltpu.SMEM)


def dot(a, b):
    return jnp.dot(a, b, precision=highest, preferred_element_type=f32)


def call(kernel, outs, *args, scalars=0, scratch=(), place=VMEM, grant=GRANT_BYTES):
    specs = [SMEM] * scalars + [place] * (len(args) - scalars)
    many = isinstance(outs, tuple)
    return pl.pallas_call(
        kernel,
        out_shape=outs,
        in_specs=specs,
        out_specs=tuple([VMEM] * len(outs)) if many else VMEM,
        scratch_shapes=list(scratch),
        compiler_params=pltpu.CompilerParams(vmem_limit_bytes=grant),
    )(*args)


def split(x):
    high = x.astype(jnp.bfloat16)
    return high, (x - high.astype(f32)).astype(jnp.bfloat16)


def plain_dot(a, b):
    return jnp.dot(a, b, preferred_element_type=f32)


def dot3(a, b):
    tall = a.shape[0]
    high, low = split(a)
    right, rest = split(b)
    both = plain_dot(jnp.concatenate([high, low], 0), right)
    return both[:tall] + (both[tall:] + plain_dot(high, rest))


def note(top):
    return jnp.floor(jnp.log(jnp.maximum(top, 1e-30)) * NOTES).astype(jnp.int32) + 1


def noted_range(number):
    return jnp.exp(number.astype(f32) * (1.0 / NOTES))


def code(x, number):
    unit = LEVELS / noted_range(number)
    return jnp.floor(x * unit + 0.5).astype(jnp.int32).astype(jnp.int16)


def pack_kernel(local, remote, count, gradient, jacobi, tiles, packed, *scratch):
    blocks, others, lives, whole, inverse, coupling, done = scratch
    width = whole.shape[0]
    height = BLOCK + width
    slots = packed.shape[0] // height
    contract = (((1,), (1,)), ((), ()))
    sources = [local, remote, count, jacobi, tiles, gradient]
    targets = [blocks, others, lives, inverse, coupling, whole]
    copies = [
        pltpu.make_async_copy(source, target, done.at[i])
        for i, (source, target) in enumerate(zip(sources, targets))
    ]
    for copy in copies:
        copy.start()
    for copy in copies:
        copy.wait()
    lane = lax.broadcasted_iota(jnp.int32, (width, BLOCK), 1)
    row = lax.broadcasted_iota(jnp.int32, (width, BLOCK), 0)
    notes = jnp.zeros((width, BLOCK), jnp.int32)
    for slot in range(slots):
        block = blocks[slot]
        halves = jnp.concatenate(split(inverse[block]), 0)
        both = lax.dot_general(halves, coupling[slot], contract, preferred_element_type=f32)
        operator = both[:BLOCK] + both[BLOCK:]
        top = jnp.max(jnp.max(jnp.abs(operator), axis=0, keepdims=True), axis=1, keepdims=True)
        columns = pl.ds(pl.multiple_of(block * BLOCK, BLOCK), BLOCK)
        part = whole[:, columns]
        tops = jnp.max(jnp.abs(part), axis=1, keepdims=True)
        at = slot * height
        packed[at : at + BLOCK, :] = code(operator, note(top))
        packed[at + BLOCK : at + height, :] = code(part, note(tops))
        live = jnp.where(slot < lives[0], 1, 0)
        for place, value in enumerate((block, others[slot], live, note(top))):
            here = (lane == place * slots + slot) & (row == 0)
            notes = jnp.where(here, value, notes)
        notes = jnp.where(lane == 4 * slots + slot * width + row, note(tops), notes)
    notes = jnp.sum(notes, axis=0, keepdims=True)
    packed[slots * height :, :] = jnp.broadcast_to(notes, (NOTE_ROWS, BLOCK)).astype(jnp.int16)


def chain_kernel(sources, give, near, far, *refs):
    sends, (operators, tops, held, out) = refs[:-4], refs[-4:]
    groups = near.shape[0]
    width = held.shape[1]
    height = BLOCK + width
    slots = near.shape[1] // height
    half = groups * slots
    total = 2 * half
    share = sends[0].shape[1]
    lane = lax.broadcasted_iota(jnp.int32, (width, BLOCK), 1)
    row = lax.broadcasted_iota(jnp.int32, (width, BLOCK), 0)
    for q in range(total):
        ref = near if q < half else far
        group, slot = divmod(q % half, slots)
        at = slot * height
        high, low = split(ref[group, at : at + BLOCK, :].astype(f32))
        operators[q, :, :BLOCK] = high
        operators[q, :, BLOCK:] = low
        notes = ref[group, slots * height :, :].astype(f32)
        notes = jnp.concatenate([notes] * (width // NOTE_ROWS), 0)
        scale = noted_range(
            jnp.sum(jnp.where(lane == 3 * slots + slot, notes, 0.0), axis=1, keepdims=True)
        )
        tops[q] = jnp.broadcast_to(scale * (1.0 / LEVELS), (width, BLOCK))
        here = lane == 4 * slots + slot * width + row
        scale = noted_range(jnp.sum(jnp.where(here, notes, 0.0), axis=1, keepdims=True))
        part = ref[group, at + BLOCK : at + height, :].astype(f32)
        held[q] = part * (scale * (1.0 / LEVELS))
    held[total] = jnp.zeros((width, BLOCK), f32)
    out[total] = jnp.zeros((width, BLOCK), f32)

    def step(j, carry):
        for q in range(total):
            four = plain_dot(jnp.concatenate(split(held[q]), 0), operators[q])
            value = (four[:width, :BLOCK] + four[width:, :BLOCK]) + (
                four[:width, BLOCK:] + four[width:, BLOCK:]
            )
            out[q] = value * tops[q]
        for q in range(total):
            value = out[sources[q * slots]]
            for i in range(1, slots):
                value += out[sources[q * slots + i]]
            held[q] = value
        for o, send in enumerate(sends):
            for p in range(share):
                send[j, p] = held[give[o * share + p]]
        return carry

    lax.fori_loop(0, ITERS, step, 0)


def shift(x, axis, by):
    size = lax.axis_size(axis)
    return lax.ppermute(x, axis, [(i, i ^ by) for i in range(size)])


def whole_pieces(x):
    others = range(1, lax.axis_size("cols"))
    return [x] + [shift(x, "cols", o) for o in others]


def chain_gathered(
    gradient, factor, jacobi, tiles, whole_local, whole_remote, count, order, slots
):
    width = gradient.shape[0]
    blocks = jacobi.shape[0]
    devices = lax.axis_size("rows")
    columns = lax.axis_size("cols")
    groups = devices // 2
    height = BLOCK + width
    packed = call(
        pack_kernel,
        jax.ShapeDtypeStruct((slots * height + NOTE_ROWS, BLOCK), jnp.int16),
        whole_local,
        whole_remote,
        count,
        gradient,
        jacobi,
        tiles,
        scratch=[
            pltpu.SMEM(whole_local.shape, jnp.int32),
            pltpu.SMEM(whole_remote.shape, jnp.int32),
            pltpu.SMEM(count.shape, jnp.int32),
            pltpu.VMEM(gradient.shape, f32),
            pltpu.VMEM(jacobi.shape, f32),
            pltpu.VMEM(tiles.shape, tiles.dtype),
            pltpu.SemaphoreType.DMA((6,)),
        ],
        place=pl.BlockSpec(memory_space=pl.ANY),
        grant=WHOLE_BYTES,
    )
    near = [packed] + [shift(packed, "rows", 2 * o) for o in range(1, groups)]
    gradient, factor, _ = lax.optimization_barrier((gradient, factor, packed))
    factors = whole_pieces(factor.T)
    pieces = whole_pieces(gradient)
    powers = make_powers(factors)
    near, powers = lax.optimization_barrier((near, powers))
    near = jnp.stack(near)
    swap = [(i, i ^ 1) for i in range(devices)]
    noted = near[:, slots * height :, :]
    told = lax.ppermute(noted, "rows", swap)
    far = lax.ppermute(near, "rows", swap)
    told = jnp.concatenate([noted[:, 0], told[:, 0]], 0)

    me = lax.axis_index("rows")
    position = jnp.arange(devices, dtype=jnp.int32)
    device = me ^ (position // groups) ^ (2 * (position % groups))
    locals_, remotes, lives = (
        told[:, i * slots : (i + 1) * slots].astype(jnp.int32) for i in range(3)
    )
    owner = (remotes // blocks).reshape(-1)
    holder = jnp.broadcast_to(device[:, None], locals_.shape).reshape(-1)
    alive = lives.reshape(-1) > 0
    meets = (
        (owner[:, None] == holder[None, :])
        & (owner[None, :] == holder[:, None])
        & alive[None, :]
    )
    total = devices * slots
    numbers = jnp.arange(total, dtype=jnp.int32)
    partner = jnp.sum(jnp.where(meets, numbers[None, :], 0), axis=1).reshape(devices, slots)
    same = (
        (locals_[:, :, None] == locals_[:, None, :])
        & (lives[:, None, :] > 0)
        & (lives[:, :, None] > 0)
    )
    sources = jnp.where(same, partner[:, None, :], total).reshape(-1)
    share = order.shape[0] // columns
    shape = jax.ShapeDtypeStruct
    sends = call(
        chain_kernel,
        tuple([shape((ITERS, share, width, BLOCK), f32)] * columns),
        sources,
        jnp.where(order < slots, order, total),
        near,
        far,
        scalars=2,
        scratch=[
            pltpu.VMEM((total, BLOCK, 2 * BLOCK), jnp.bfloat16),
            pltpu.VMEM((total, width, BLOCK), f32),
            pltpu.VMEM((total + 1, width, BLOCK), f32),
            pltpu.VMEM((total + 1, width, BLOCK), f32),
        ],
    )
    return list(sends), pieces, powers


def chain_exchanged(gradient, jacobi, tiles, order, local, remote, live):
    width = gradient.shape[0]
    blocks = jacobi.shape[0]
    devices = lax.axis_size("rows")
    owner = remote // blocks
    placing = (
        (local[:, None] == jnp.arange(blocks, dtype=jnp.int32)[None, :]) & live[:, None]
    ).astype(f32)
    meets = live[:, None] & (owner[:, None] == jnp.arange(devices, dtype=jnp.int32)[None, :])
    granted = jnp.sum(jnp.where(meets, local[:, None], 0), axis=0)
    vector = jnp.transpose(gradient.reshape(width, blocks, BLOCK), (1, 0, 2))
    steps = []
    for _ in range(ITERS):
        sent = jnp.einsum("nej,nji->nei", vector, jacobi, precision=highest)[granted]
        incoming = lax.all_to_all(sent, "rows", 0, 0, tiled=True)
        products = jnp.einsum(
            "kej,kji->kei", incoming[owner], tiles.astype(f32), precision=highest
        )
        vector = jnp.einsum("kei,kn->nei", products, placing, precision=highest)
        steps.append(vector)
    columns = lax.axis_size("cols")
    share = order.shape[0] // columns
    chain = jnp.pad(jnp.stack(steps), ((0, 0), (0, share * columns - blocks), (0, 0), (0, 0)))
    return [
        lax.dynamic_slice_in_dim(chain, order[o * share], share, 1) for o in range(columns)
    ]


def gather_sums(sums, s, y, weight):
    y = [weight * value for value in y]
    f = [s[0] + s[1]]
    for j in range(1, ITERS):
        f.append(0.5 * (s[j - 1] + s[j + 1]) + s[j])
    for i in range(ITERS):
        for j in range(i + 1):
            sums[i, j] = sums.get((i, j), 0.0) + y[i] * f[j]
        sums[i, ITERS] = sums.get((i, ITERS), 0.0) + y[i] * s[0]


def flat_sums(sums):
    lane = lax.broadcasted_iota(jnp.int32, (1, BLOCK), 1)
    result = jnp.zeros((1, BLOCK), f32)
    for (i, j), value in sums.items():
        value = jnp.sum(jnp.sum(value, axis=0, keepdims=True), axis=1, keepdims=True)
        here = lane == 16 * i + j
        if j < ITERS:
            here = here | (lane == 16 * j + i)
        result = jnp.where(here, value, result)
    return result


def powers_kernel(me, *refs):
    pieces, (scaled, powers, scale) = refs[:-3], refs[-3:]
    width = pieces[0].shape[0]
    factor = jnp.concatenate([piece[...] for piece in pieces], 0)
    lane = lax.broadcasted_iota(jnp.int32, factor.shape, 1)
    for bit in range((len(pieces) - 1).bit_length()):
        size = width << bit
        ahead, behind = pltpu.roll(factor, BLOCK - size, 1), pltpu.roll(factor, size, 1)
        swapped = jnp.where((lane // size) % 2 == 0, ahead, behind)
        factor = jnp.where((me[0] >> bit) % 2 == 1, swapped, factor)
    norm = jnp.max(jnp.sum(jnp.abs(factor), axis=1, keepdims=True), axis=0, keepdims=True)
    power = factor / norm
    for _ in range(3):
        power = dot3(power, power)
    bound = jnp.sum(jnp.sum(power * power, axis=1, keepdims=True), axis=0, keepdims=True)
    for _ in range(4):
        bound = jnp.sqrt(bound)
    ratio = 2.0 / (STRETCH * bound * norm)
    scale[...] = jnp.broadcast_to(ratio, scale.shape)
    factor = factor * ratio
    scaled[...] = factor

    row = lax.broadcasted_iota(jnp.int32, (width, BLOCK), 0)
    lane = lax.broadcasted_iota(jnp.int32, (width, BLOCK), 1)
    kept = [(row == lane).astype(f32)]
    for k in range(ITERS):
        value = dot(kept[k], factor) - kept[k]
        kept.append(2.0 * value - kept[k - 1] if k else value)
    powers[...] = jnp.concatenate(kept, 0)


def basis_kernel(where, held, powers, jacobi, *refs):
    pieces, (plain, smooth, gram, starts) = refs[:-4], refs[-4:]
    width = pieces[0].shape[0]
    for p in range(starts.shape[0]):
        columns = pl.ds(pl.multiple_of(held[p] * BLOCK, BLOCK), BLOCK)
        starts[p] = jnp.concatenate([piece[:, columns] for piece in pieces], 0)
    sums = {}
    for b in range(jacobi.shape[0]):
        columns = slice(b * BLOCK, (b + 1) * BLOCK)
        whole = jnp.concatenate([piece[:, columns] for piece in pieces], 0)
        s = dot3(powers[...], whole)
        y = dot3(s[: ITERS * width], jacobi[b])
        plain[b] = s[width:]
        smooth[b] = y
        weight = jnp.where(where[b] < NOWHERE, 0.0, 1.0)
        for r in range(0, width, 8):
            gather_sums(
                sums,
                [s[k * width + r : k * width + r + 8] for k in range(ITERS + 1)],
                [y[k * width + r : k * width + r + 8] for k in range(ITERS)],
                weight,
            )
    gram[...] = flat_sums(sums)


def make_powers(pieces):
    width = pieces[0].shape[0]
    shape = jax.ShapeDtypeStruct
    return call(
        powers_kernel,
        (
            shape((BLOCK, BLOCK), f32),
            shape(((ITERS + 1) * width, BLOCK), f32),
            shape((8, BLOCK), f32),
        ),
        lax.axis_index("cols").astype(jnp.int32).reshape(1),
        *pieces,
        scalars=1,
    )


def mix_kernel(held, used, *refs):
    devices = (len(refs) - 5) // 2
    parts = refs[:devices]
    starts, scaled, jacobi, others, gram = refs[devices : devices + 5]
    backs = refs[devices + 5 :]
    share, width = parts[0].shape[1:3]
    sums = {}
    for p in range(share):
        now = [starts[p]]
        for j in range(ITERS):
            now.append(jnp.concatenate([part[j, p] for part in parts], 0))
        past = None
        chosen = [now[0]]
        for k in range(ITERS):
            left = ITERS - k
            image = dot3(
                scaled[...], jnp.concatenate([now[i] + now[i + 1] for i in range(left)], 1)
            )
            fresh = []
            for i in range(left):
                value = image[:, i * BLOCK : (i + 1) * BLOCK] - now[i]
                fresh.append(2.0 * value - past[i] if k else value)
            past, now = now, fresh
            chosen.append(now[0])
        for o, back in enumerate(backs):
            for k in range(ITERS):
                back[k, p] = chosen[k + 1][o * width : (o + 1) * width]
        soft = dot3(jnp.concatenate(chosen[:ITERS], 0), jacobi[held[p]])
        weight = jnp.where(used[p] > 0, 1.0, 0.0)
        for r in range(0, BLOCK, 8):
            gather_sums(
                sums,
                [value[r : r + 8] for value in chosen],
                [soft[k * BLOCK + r : k * BLOCK + r + 8] for k in range(ITERS)],
                weight,
            )
    gram[...] = jnp.broadcast_to((flat_sums(sums) + others[...])[None], gram.shape)


def finish_kernel(held, where, grams, scale, gradient, plain, smooth, jacobi, *refs):
    backs, (solution, residual, extra, less) = refs[:-4], refs[-4:]
    width = gradient.shape[0]
    blocks = jacobi.shape[0]
    share = backs[0].shape[1]
    none = len(backs) * share
    flat = jnp.sum(grams[:, 0, :], axis=0, keepdims=True)
    row = lax.broadcasted_iota(jnp.int32, (8, BLOCK), 0)
    lane = lax.broadcasted_iota(jnp.int32, (8, BLOCK), 1)
    table = jnp.zeros((8, BLOCK), f32)
    for i in range(ITERS):
        moved = flat if i == 0 else pltpu.roll(flat, BLOCK - 16 * i, 1)
        table = jnp.where((row == i) & (lane <= ITERS), moved, table)
    for p in range(ITERS):
        pivot = table[p : p + 1, :] / table[p : p + 1, p : p + 1]
        table = jnp.where(row == p, pivot, table - table[:, p : p + 1] * pivot)
    steps = [table[j : j + 1, ITERS : ITERS + 1] for j in range(ITERS)]
    takes = []
    for k in range(ITERS + 1):
        value = 0.0
        if k > 0:
            value += steps[k - 1] * (1.0 if k == 1 else 0.5)
        if k < ITERS:
            value += steps[k]
        if k + 1 < ITERS:
            value += 0.5 * steps[k + 1]
        takes.append(jnp.broadcast_to(value, (width, BLOCK)))
    longer = scale[0:1, 0:1]
    gives = [jnp.broadcast_to(longer * step, (width, BLOCK)) for step in steps]

    def combine(weights, values):
        return sum(weight * value for weight, value in zip(weights, values))

    def cut(ref, b):
        return [ref[b, k * width : (k + 1) * width, :] for k in range(ITERS)]

    for n in range(none):
        values = [backs[n // share][k, n % share] for k in range(ITERS)]
        extra[n] = dot3(combine(gives[1:], values), jacobi[held[n]])
        less[n] = combine(takes[1:], values)
    for b in range(blocks):
        columns = slice(b * BLOCK, (b + 1) * BLOCK)
        n = jnp.minimum(where[b], none - 1)
        own = where[b] >= NOWHERE
        y = cut(smooth, b)
        rest = jnp.where(own, combine(gives[1:], y[1:]), extra[n])
        solution[:, columns] = gives[0] * y[0] + rest
        rest = jnp.where(own, combine(takes[1:], cut(plain, b)), less[n])
        start = gradient[:, columns]
        residual[:, columns] = start - takes[0] * start - rest


def on_device(
    gradient,
    width_factor,
    diag_blocks,
    jacobi_inverse,
    coupling_tiles,
    tile_local,
    tile_remote,
    tile_count,
    exchange=False,
):
    width, rows = gradient.shape
    blocks = diag_blocks.shape[0]
    columns = lax.axis_size("cols")
    devices = lax.axis_size("rows")
    slots = tile_local.shape[0] - 1
    live = jnp.arange(slots, dtype=jnp.int32) < tile_count[0]
    lists = (tile_local[:slots], tile_remote[:slots], live)

    gathered = devices * slots * BLOCK * (BLOCK + width) * 2
    noted = slots * (4 + width) <= BLOCK and width % NOTE_ROWS == 0 and devices * blocks < 2**15
    whole = gathered <= GATHER_BYTES and noted and devices & (devices - 1) == 0 and not exchange
    units = slots if whole else blocks
    share = -(-units // columns)
    numbers = jnp.arange(columns * share, dtype=jnp.int32)
    dealer = lax.axis_index("cols") ^ (numbers // share)
    order = dealer * share + numbers % share
    if whole:
        local = lists[0]
        earlier = jnp.arange(slots)[:, None] > jnp.arange(slots)[None, :]
        repeat = jnp.any(earlier & (local[:, None] == local[None, :]), axis=1)
        fit = order[:, None] == jnp.arange(slots, dtype=jnp.int32)[None, :]
        held = jnp.sum(jnp.where(fit, local[None, :], 0), axis=1)
        used = jnp.sum(jnp.where(fit & (live & ~repeat)[None, :], 1, 0), axis=1)
    else:
        held = jnp.minimum(order, blocks - 1)
        used = (order < blocks).astype(jnp.int32)
    mine = (held[None, :] == jnp.arange(blocks, dtype=jnp.int32)[:, None]) & (used > 0)[None, :]
    where = jnp.min(jnp.where(mine, numbers[None, :], NOWHERE), axis=1)
    if whole:
        sends, pieces, powers = chain_gathered(
            gradient,
            width_factor,
            jacobi_inverse,
            coupling_tiles,
            tile_local,
            tile_remote,
            tile_count,
            order,
            slots,
        )
    else:
        sends = chain_exchanged(
            gradient, jacobi_inverse, coupling_tiles[:slots], order, *lists
        )
        pieces = whole_pieces(gradient)
        powers = make_powers(whole_pieces(width_factor.T))
    scaled, powers, scale = powers
    powers, sends = lax.optimization_barrier((powers, sends))
    parts = [sends[0]]
    for o in range(1, columns):
        parts.append(shift(sends[o], "cols", o))

    shape = jax.ShapeDtypeStruct
    plain, smooth, others, starts = call(
        basis_kernel,
        (
            shape((blocks, ITERS * width, BLOCK), f32),
            shape((blocks, ITERS * width, BLOCK), f32),
            shape((1, BLOCK), f32),
            shape((share, BLOCK, BLOCK), f32),
        ),
        where,
        held,
        powers,
        jacobi_inverse,
        *pieces,
        scalars=2,
    )
    gram, *backs = call(
        mix_kernel,
        tuple(
            [shape((columns * devices, 1, BLOCK), f32)]
            + [shape((ITERS, share, width, BLOCK), f32)] * columns
        ),
        held,
        used,
        *parts,
        starts,
        scaled,
        jacobi_inverse,
        others,
        scalars=2,
    )
    grams = lax.all_to_all(gram, ("cols", "rows"), 0, 0, tiled=True)
    for o in range(1, columns):
        backs[o] = shift(backs[o], "cols", o)
    return call(
        finish_kernel,
        (shape((width, rows), f32), shape((width, rows), f32)),
        held,
        where,
        grams,
        scale,
        gradient,
        plain,
        smooth,
        jacobi_inverse,
        *backs,
        scalars=2,
        scratch=[pltpu.VMEM((columns * share, width, BLOCK), f32)] * 2,
    )


def solution(mesh):
    placed = (
        P("cols", "rows"),
        P(None, "cols"),
        P("rows", None, None),
        P("rows", None, None),
        P("rows", None, None),
        P("rows"),
        P("rows"),
        P("rows"),
    )

    return jax.shard_map(
        on_device,
        mesh=mesh,
        in_specs=placed,
        out_specs=(P("cols", "rows"), P("cols", "rows")),
        check_vma=False,
    )
```

```python
import jax
import jax.numpy as jnp
from jax import lax
from jax.experimental import pallas as pl
from jax.experimental.pallas import tpu as pltpu
from jax.sharding import PartitionSpec as P


BLOCK = 128
ITERS = 6
STRETCH = 1.1
GATHER_BYTES = 8 * 2**20


NOWHERE = 2**20
LEVELS = 32700.0
NOTES = 256 / 0.6931471805599453
NOTE_ROWS = 16
GRANT_BYTES = 24 * 2**20
WHOLE_BYTES = 60 * 2**20

highest = lax.Precision.HIGHEST
f32 = jnp.float32
VMEM = pl.BlockSpec(memory_space=pltpu.VMEM)
SMEM = pl.BlockSpec(memory_space=pltpu.SMEM)


def call(kernel, outs, *args, scalars=0, scratch=(), place=VMEM, grant=GRANT_BYTES):
    specs = [SMEM] * scalars + [place] * (len(args) - scalars)
    many = isinstance(outs, tuple)
    return pl.pallas_call(
        kernel,
        out_shape=outs,
        in_specs=specs,
        out_specs=tuple([VMEM] * len(outs)) if many else VMEM,
        scratch_shapes=list(scratch),
        compiler_params=pltpu.CompilerParams(vmem_limit_bytes=grant),
    )(*args)


def split(x):
    high = x.astype(jnp.bfloat16)
    return high, (x - high.astype(f32)).astype(jnp.bfloat16)


def plain_dot(a, b):
    return jnp.dot(a, b, preferred_element_type=f32)


def dot3(a, b):
    tall = a.shape[0]
    high, low = split(a)
    right, rest = split(b)
    both = plain_dot(jnp.concatenate([high, low], 0), right)
    return both[:tall] + (both[tall:] + plain_dot(high, rest))


def note(top):
    return jnp.floor(jnp.log(jnp.maximum(top, 1e-30)) * NOTES).astype(jnp.int32) + 1


def noted_range(number):
    return jnp.exp(number.astype(f32) * (1.0 / NOTES))


def code(x, number):
    unit = LEVELS / noted_range(number)
    return jnp.floor(x * unit + 0.5).astype(jnp.int32).astype(jnp.int16)


def pack_kernel(local, remote, count, gradient, jacobi, tiles, packed, *scratch):
    blocks, others, lives, whole, inverse, coupling, done = scratch
    width = whole.shape[0]
    height = BLOCK + width
    slots = packed.shape[0] // height
    contract = (((1,), (1,)), ((), ()))
    sources = [local, remote, count, jacobi, tiles, gradient]
    targets = [blocks, others, lives, inverse, coupling, whole]
    copies = [
        pltpu.make_async_copy(source, target, done.at[i])
        for i, (source, target) in enumerate(zip(sources, targets))
    ]
    for copy in copies:
        copy.start()
    for copy in copies:
        copy.wait()
    lane = lax.broadcasted_iota(jnp.int32, (width, BLOCK), 1)
    row = lax.broadcasted_iota(jnp.int32, (width, BLOCK), 0)
    notes = jnp.zeros((width, BLOCK), jnp.int32)
    for slot in range(slots):
        block = blocks[slot]
        halves = jnp.concatenate(split(inverse[block]), 0)
        both = lax.dot_general(halves, coupling[slot], contract, preferred_element_type=f32)
        operator = both[:BLOCK] + both[BLOCK:]
        top = jnp.max(jnp.max(jnp.abs(operator), axis=0, keepdims=True), axis=1, keepdims=True)
        columns = pl.ds(pl.multiple_of(block * BLOCK, BLOCK), BLOCK)
        part = whole[:, columns]
        tops = jnp.max(jnp.abs(part), axis=1, keepdims=True)
        at = slot * height
        packed[at : at + BLOCK, :] = code(operator, note(top))
        packed[at + BLOCK : at + height, :] = code(part, note(tops))
        live = jnp.where(slot < lives[0], 1, 0)
        for place, value in enumerate((block, others[slot], live, note(top))):
            here = (lane == place * slots + slot) & (row == 0)
            notes = jnp.where(here, value, notes)
        notes = jnp.where(lane == 4 * slots + slot * width + row, note(tops), notes)
    notes = jnp.sum(notes, axis=0, keepdims=True)
    packed[slots * height :, :] = jnp.broadcast_to(notes, (NOTE_ROWS, BLOCK)).astype(jnp.int16)


def chain_kernel(sources, give, near, far, *refs):
    sends, (operators, tops, held, out) = refs[:-4], refs[-4:]
    groups = near.shape[0]
    width = held.shape[1]
    height = BLOCK + width
    slots = near.shape[1] // height
    half = groups * slots
    total = 2 * half
    share = sends[0].shape[1]
    lane = lax.broadcasted_iota(jnp.int32, (width, BLOCK), 1)
    row = lax.broadcasted_iota(jnp.int32, (width, BLOCK), 0)
    for q in range(total):
        ref = near if q < half else far
        group, slot = divmod(q % half, slots)
        at = slot * height
        high, low = split(ref[group, at : at + BLOCK, :].astype(f32))
        operators[q, :, :BLOCK] = high
        operators[q, :, BLOCK:] = low
        notes = ref[group, slots * height :, :].astype(f32)
        notes = jnp.concatenate([notes] * (width // NOTE_ROWS), 0)
        scale = noted_range(
            jnp.sum(jnp.where(lane == 3 * slots + slot, notes, 0.0), axis=1, keepdims=True)
        )
        tops[q] = jnp.broadcast_to(scale * (1.0 / LEVELS), (width, BLOCK))
        here = lane == 4 * slots + slot * width + row
        scale = noted_range(jnp.sum(jnp.where(here, notes, 0.0), axis=1, keepdims=True))
        part = ref[group, at + BLOCK : at + height, :].astype(f32)
        held[q] = part * (scale * (1.0 / LEVELS))
    held[total] = jnp.zeros((width, BLOCK), f32)
    out[total] = jnp.zeros((width, BLOCK), f32)

    def step(j, carry):
        for q in range(total):
            four = plain_dot(jnp.concatenate(split(held[q]), 0), operators[q])
            value = (four[:width, :BLOCK] + four[width:, :BLOCK]) + (
                four[:width, BLOCK:] + four[width:, BLOCK:]
            )
            out[q] = value * tops[q]
        for q in range(total):
            value = out[sources[q * slots]]
            for i in range(1, slots):
                value += out[sources[q * slots + i]]
            held[q] = value
        for o, send in enumerate(sends):
            for p in range(share):
                send[j, p] = held[give[o * share + p]]
        return carry

    lax.fori_loop(0, ITERS, step, 0, unroll=True)


def shift(x, axis, by):
    size = lax.axis_size(axis)
    return lax.ppermute(x, axis, [(i, (i - by) % size) for i in range(size)])


def whole_pieces(x):
    others = range(1, lax.axis_size("cols"))
    return [x] + [shift(x, "cols", o) for o in others]


def chain_gathered(
    gradient, factor, jacobi, tiles, whole_local, whole_remote, count, order, slots
):
    width = gradient.shape[0]
    blocks = jacobi.shape[0]
    devices = lax.axis_size("rows")
    columns = lax.axis_size("cols")
    groups = devices // 2
    height = BLOCK + width
    packed = call(
        pack_kernel,
        jax.ShapeDtypeStruct((slots * height + NOTE_ROWS, BLOCK), jnp.int16),
        whole_local,
        whole_remote,
        count,
        gradient,
        jacobi,
        tiles,
        scratch=[
            pltpu.SMEM(whole_local.shape, jnp.int32),
            pltpu.SMEM(whole_remote.shape, jnp.int32),
            pltpu.SMEM(count.shape, jnp.int32),
            pltpu.VMEM(gradient.shape, f32),
            pltpu.VMEM(jacobi.shape, f32),
            pltpu.VMEM(tiles.shape, tiles.dtype),
            pltpu.SemaphoreType.DMA((6,)),
        ],
        place=pl.BlockSpec(memory_space=pl.ANY),
        grant=WHOLE_BYTES,
    )
    near = [packed] + [shift(packed, "rows", 2 * o) for o in range(1, groups)]
    gradient, factor, _ = lax.optimization_barrier((gradient, factor, packed))
    factors = whole_pieces(factor.T)
    pieces = whole_pieces(gradient)
    powers = make_powers(factors)
    near, powers = lax.optimization_barrier((near, powers))
    near = jnp.stack(near)
    swap = [(i, i ^ 1) for i in range(devices)]
    noted = near[:, slots * height :, :]
    told = lax.ppermute(noted, "rows", swap)
    far = lax.ppermute(near, "rows", swap)
    told = jnp.concatenate([noted[:, 0], told[:, 0]], 0)

    me = lax.axis_index("rows")
    position = jnp.arange(devices, dtype=jnp.int32)
    base = me ^ (position // groups)
    device = (base + 2 * (position % groups)) % devices
    locals_, remotes, lives = (
        told[:, i * slots : (i + 1) * slots].astype(jnp.int32) for i in range(3)
    )
    owner = (remotes // blocks).reshape(-1)
    holder = jnp.broadcast_to(device[:, None], locals_.shape).reshape(-1)
    alive = lives.reshape(-1) > 0
    meets = (
        (owner[:, None] == holder[None, :])
        & (owner[None, :] == holder[:, None])
        & alive[None, :]
    )
    total = devices * slots
    numbers = jnp.arange(total, dtype=jnp.int32)
    partner = jnp.sum(jnp.where(meets, numbers[None, :], 0), axis=1).reshape(devices, slots)
    same = (
        (locals_[:, :, None] == locals_[:, None, :])
        & (lives[:, None, :] > 0)
        & (lives[:, :, None] > 0)
    )
    sources = jnp.where(same, partner[:, None, :], total).reshape(-1)
    share = order.shape[0] // columns
    shape = jax.ShapeDtypeStruct
    sends = call(
        chain_kernel,
        tuple([shape((ITERS, share, width, BLOCK), f32)] * columns),
        sources,
        jnp.where(order < slots, order, total),
        near,
        far,
        scalars=2,
        scratch=[
            pltpu.VMEM((total, BLOCK, 2 * BLOCK), jnp.bfloat16),
            pltpu.VMEM((total, width, BLOCK), f32),
            pltpu.VMEM((total + 1, width, BLOCK), f32),
            pltpu.VMEM((total + 1, width, BLOCK), f32),
        ],
    )
    return list(sends), pieces, powers


def chain_exchanged(gradient, jacobi, tiles, order, local, remote, live):
    width = gradient.shape[0]
    blocks = jacobi.shape[0]
    devices = lax.axis_size("rows")
    owner = remote // blocks
    placing = (
        (local[:, None] == jnp.arange(blocks, dtype=jnp.int32)[None, :]) & live[:, None]
    ).astype(f32)
    meets = live[:, None] & (owner[:, None] == jnp.arange(devices, dtype=jnp.int32)[None, :])
    granted = jnp.sum(jnp.where(meets, local[:, None], 0), axis=0)
    vector = jnp.transpose(gradient.reshape(width, blocks, BLOCK), (1, 0, 2))
    steps = []
    for _ in range(ITERS):
        sent = jnp.einsum("nej,nji->nei", vector, jacobi, precision=highest)[granted]
        incoming = lax.all_to_all(sent, "rows", 0, 0, tiled=True)
        products = jnp.einsum(
            "kej,kji->kei", incoming[owner], tiles.astype(f32), precision=highest
        )
        vector = jnp.einsum("kei,kn->nei", products, placing, precision=highest)
        steps.append(vector)
    columns = lax.axis_size("cols")
    share = order.shape[0] // columns
    chain = jnp.pad(jnp.stack(steps), ((0, 0), (0, share * columns - blocks), (0, 0), (0, 0)))
    return [
        lax.dynamic_slice_in_dim(chain, order[o * share], share, 1) for o in range(columns)
    ]


def gather_sums(sums, s, y, weight):
    y = [weight * value for value in y]
    f = [s[0] + s[1]]
    for j in range(1, ITERS):
        f.append(0.5 * (s[j - 1] + s[j + 1]) + s[j])
    for i in range(ITERS):
        for j in range(i + 1):
            sums[i, j] = sums.get((i, j), 0.0) + y[i] * f[j]
        sums[i, ITERS] = sums.get((i, ITERS), 0.0) + y[i] * s[0]


def flat_sums(sums):
    lane = lax.broadcasted_iota(jnp.int32, (1, BLOCK), 1)
    result = jnp.zeros((1, BLOCK), f32)
    for (i, j), value in sums.items():
        value = jnp.sum(jnp.sum(value, axis=0, keepdims=True), axis=1, keepdims=True)
        here = lane == 16 * i + j
        if j < ITERS:
            here = here | (lane == 16 * j + i)
        result = jnp.where(here, value, result)
    return result


def powers_kernel(turn, *refs):
    pieces, (scaled, powers, scale) = refs[:-3], refs[-3:]
    width = pieces[0].shape[0]
    factor = jnp.concatenate([piece[...] for piece in pieces], 0)
    factor = pltpu.roll(factor, turn[0], 1)
    norm = jnp.max(jnp.sum(jnp.abs(factor), axis=1, keepdims=True), axis=0, keepdims=True)
    power = factor / norm
    for _ in range(3):
        power = dot3(power, power)
    bound = jnp.sum(jnp.sum(power * power, axis=1, keepdims=True), axis=0, keepdims=True)
    for _ in range(4):
        bound = jnp.sqrt(bound)
    ratio = 2.0 / (STRETCH * bound * norm)
    scale[...] = jnp.broadcast_to(ratio, scale.shape)
    factor = factor * ratio
    scaled[...] = factor

    row = lax.broadcasted_iota(jnp.int32, (width, BLOCK), 0)
    lane = lax.broadcasted_iota(jnp.int32, (width, BLOCK), 1)
    kept = [(row == lane).astype(f32)]
    for k in range(ITERS):
        value = dot3(kept[k], factor) - kept[k]
        kept.append(2.0 * value - kept[k - 1] if k else value)
    powers[...] = jnp.concatenate(kept, 0)


def basis_kernel(where, held, powers, jacobi, *refs):
    pieces, (plain, smooth, gram, starts) = refs[:-4], refs[-4:]
    width = pieces[0].shape[0]
    for p in range(starts.shape[0]):
        columns = pl.ds(pl.multiple_of(held[p] * BLOCK, BLOCK), BLOCK)
        starts[p] = jnp.concatenate([piece[:, columns] for piece in pieces], 0)
    sums = {}
    for b in range(jacobi.shape[0]):
        columns = slice(b * BLOCK, (b + 1) * BLOCK)
        whole = jnp.concatenate([piece[:, columns] for piece in pieces], 0)
        s = dot3(powers[...], whole)
        y = dot3(s[: ITERS * width], jacobi[b])
        plain[b] = s[width:]
        smooth[b] = y
        weight = jnp.where(where[b] < NOWHERE, 0.0, 1.0)
        for r in range(0, width, 8):
            gather_sums(
                sums,
                [s[k * width + r : k * width + r + 8] for k in range(ITERS + 1)],
                [y[k * width + r : k * width + r + 8] for k in range(ITERS)],
                weight,
            )
    gram[...] = flat_sums(sums)


def make_powers(pieces):
    width = pieces[0].shape[0]
    shape = jax.ShapeDtypeStruct
    turn = (BLOCK - width * lax.axis_index("cols")) % BLOCK
    return call(
        powers_kernel,
        (
            shape((BLOCK, BLOCK), f32),
            shape(((ITERS + 1) * width, BLOCK), f32),
            shape((8, BLOCK), f32),
        ),
        turn.astype(jnp.int32).reshape(1),
        *pieces,
        scalars=1,
    )


def mix_kernel(held, used, *refs):
    devices = (len(refs) - 5) // 2
    parts = refs[:devices]
    starts, scaled, jacobi, others, gram = refs[devices : devices + 5]
    backs = refs[devices + 5 :]
    share, width = parts[0].shape[1:3]
    sums = {}
    for p in range(share):
        now = [starts[p]]
        for j in range(ITERS):
            now.append(jnp.concatenate([part[j, p] for part in parts], 0))
        past = None
        chosen = [now[0]]
        for k in range(ITERS):
            left = ITERS - k
            image = dot3(
                scaled[...], jnp.concatenate([now[i] + now[i + 1] for i in range(left)], 1)
            )
            fresh = []
            for i in range(left):
                value = image[:, i * BLOCK : (i + 1) * BLOCK] - now[i]
                fresh.append(2.0 * value - past[i] if k else value)
            past, now = now, fresh
            chosen.append(now[0])
        for o, back in enumerate(backs):
            for k in range(ITERS):
                back[k, p] = chosen[k + 1][o * width : (o + 1) * width]
        soft = dot3(jnp.concatenate(chosen[:ITERS], 0), jacobi[held[p]])
        weight = jnp.where(used[p] > 0, 1.0, 0.0)
        for r in range(0, BLOCK, 8):
            gather_sums(
                sums,
                [value[r : r + 8] for value in chosen],
                [soft[k * BLOCK + r : k * BLOCK + r + 8] for k in range(ITERS)],
                weight,
            )
    gram[...] = jnp.broadcast_to((flat_sums(sums) + others[...])[None], gram.shape)


def finish_kernel(held, where, grams, scale, gradient, plain, smooth, jacobi, *refs):
    backs, (solution, residual, extra, less) = refs[:-4], refs[-4:]
    width = gradient.shape[0]
    blocks = jacobi.shape[0]
    share = backs[0].shape[1]
    none = len(backs) * share
    flat = jnp.sum(grams[:, 0, :], axis=0, keepdims=True)
    row = lax.broadcasted_iota(jnp.int32, (8, BLOCK), 0)
    lane = lax.broadcasted_iota(jnp.int32, (8, BLOCK), 1)
    table = jnp.zeros((8, BLOCK), f32)
    for i in range(ITERS):
        moved = flat if i == 0 else pltpu.roll(flat, BLOCK - 16 * i, 1)
        table = jnp.where((row == i) & (lane <= ITERS), moved, table)
    for p in range(ITERS):
        pivot = table[p : p + 1, :] / table[p : p + 1, p : p + 1]
        table = jnp.where(row == p, pivot, table - table[:, p : p + 1] * pivot)
    steps = [table[j : j + 1, ITERS : ITERS + 1] for j in range(ITERS)]
    takes = []
    for k in range(ITERS + 1):
        value = 0.0
        if k > 0:
            value += steps[k - 1] * (1.0 if k == 1 else 0.5)
        if k < ITERS:
            value += steps[k]
        if k + 1 < ITERS:
            value += 0.5 * steps[k + 1]
        takes.append(jnp.broadcast_to(value, (width, BLOCK)))
    longer = scale[0:1, 0:1]
    gives = [jnp.broadcast_to(longer * step, (width, BLOCK)) for step in steps]

    def combine(weights, values):
        return sum(weight * value for weight, value in zip(weights, values))

    def cut(ref, b):
        return [ref[b, k * width : (k + 1) * width, :] for k in range(ITERS)]

    for n in range(none):
        values = [backs[n // share][k, n % share] for k in range(ITERS)]
        extra[n] = dot3(combine(gives[1:], values), jacobi[held[n]])
        less[n] = combine(takes[1:], values)
    for b in range(blocks):
        columns = slice(b * BLOCK, (b + 1) * BLOCK)
        n = jnp.minimum(where[b], none - 1)
        own = where[b] >= NOWHERE
        y = cut(smooth, b)
        rest = jnp.where(own, combine(gives[1:], y[1:]), extra[n])
        solution[:, columns] = gives[0] * y[0] + rest
        rest = jnp.where(own, combine(takes[1:], cut(plain, b)), less[n])
        start = gradient[:, columns]
        residual[:, columns] = start - takes[0] * start - rest


def on_device(
    gradient,
    width_factor,
    diag_blocks,
    jacobi_inverse,
    coupling_tiles,
    tile_local,
    tile_remote,
    tile_count,
    exchange=False,
):
    width, rows = gradient.shape
    blocks = diag_blocks.shape[0]
    columns = lax.axis_size("cols")
    devices = lax.axis_size("rows")
    slots = tile_local.shape[0] - 1
    live = jnp.arange(slots, dtype=jnp.int32) < tile_count[0]
    lists = (tile_local[:slots], tile_remote[:slots], live)

    gathered = devices * slots * BLOCK * (BLOCK + width) * 2
    noted = slots * (4 + width) <= BLOCK and width % NOTE_ROWS == 0 and devices * blocks < 2**15
    whole = gathered <= GATHER_BYTES and noted and devices % 2 == 0 and not exchange
    units = slots if whole else blocks
    share = -(-units // columns)
    numbers = jnp.arange(columns * share, dtype=jnp.int32)
    dealer = (lax.axis_index("cols") + columns - numbers // share) % columns
    order = dealer * share + numbers % share
    if whole:
        local = lists[0]
        earlier = jnp.arange(slots)[:, None] > jnp.arange(slots)[None, :]
        repeat = jnp.any(earlier & (local[:, None] == local[None, :]), axis=1)
        fit = order[:, None] == jnp.arange(slots, dtype=jnp.int32)[None, :]
        held = jnp.sum(jnp.where(fit, local[None, :], 0), axis=1)
        used = jnp.sum(jnp.where(fit & (live & ~repeat)[None, :], 1, 0), axis=1)
    else:
        held = jnp.minimum(order, blocks - 1)
        used = (order < blocks).astype(jnp.int32)
    mine = (held[None, :] == jnp.arange(blocks, dtype=jnp.int32)[:, None]) & (used > 0)[None, :]
    where = jnp.min(jnp.where(mine, numbers[None, :], NOWHERE), axis=1)
    if whole:
        sends, pieces, powers = chain_gathered(
            gradient,
            width_factor,
            jacobi_inverse,
            coupling_tiles,
            tile_local,
            tile_remote,
            tile_count,
            order,
            slots,
        )
    else:
        sends = chain_exchanged(
            gradient, jacobi_inverse, coupling_tiles[:slots], order, *lists
        )
        pieces = whole_pieces(gradient)
        powers = make_powers(whole_pieces(width_factor.T))
    scaled, powers, scale = powers
    powers, sends = lax.optimization_barrier((powers, sends))
    parts = [sends[0]]
    for o in range(1, columns):
        parts.append(shift(sends[o], "cols", o))

    shape = jax.ShapeDtypeStruct
    plain, smooth, others, starts = call(
        basis_kernel,
        (
            shape((blocks, ITERS * width, BLOCK), f32),
            shape((blocks, ITERS * width, BLOCK), f32),
            shape((1, BLOCK), f32),
            shape((share, BLOCK, BLOCK), f32),
        ),
        where,
        held,
        powers,
        jacobi_inverse,
        *pieces,
        scalars=2,
    )
    gram, *backs = call(
        mix_kernel,
        tuple(
            [shape((columns * devices, 1, BLOCK), f32)]
            + [shape((ITERS, share, width, BLOCK), f32)] * columns
        ),
        held,
        used,
        *parts,
        starts,
        scaled,
        jacobi_inverse,
        others,
        scalars=2,
    )
    grams = lax.all_to_all(gram, ("cols", "rows"), 0, 0, tiled=True)
    for o in range(1, columns):
        backs[o] = shift(backs[o], "cols", -o)
    return call(
        finish_kernel,
        (shape((width, rows), f32), shape((width, rows), f32)),
        held,
        where,
        grams,
        scale,
        gradient,
        plain,
        smooth,
        jacobi_inverse,
        *backs,
        scalars=2,
        scratch=[pltpu.VMEM((columns * share, width, BLOCK), f32)] * 2,
    )


def solution(mesh):
    placed = (
        P("cols", "rows"),
        P(None, "cols"),
        P("rows", None, None),
        P("rows", None, None),
        P("rows", None, None),
        P("rows"),
        P("rows"),
        P("rows"),
    )

    return jax.shard_map(
        on_device,
        mesh=mesh,
        in_specs=placed,
        out_specs=(P("cols", "rows"), P("cols", "rows")),
        check_vma=False,
    )
```
